32 devices in a mesh: dp: 8 (over y, x, core), tensor: 4 (over z).
Axes of the slice: x: 2, y: 2, z: 4, core: 2. Of those that a mesh axis runs over, the one named last changes fastest.
Arguments:
- norm_input: bfloat16 [16384, 8192], P(('dp', 'tensor')), may hold values from -6 to 6
- key_grad: bfloat16 [16384, 512], P(('dp', 'tensor')), may hold values from -100 to 100
- positions: int32 [16384], P(('dp', 'tensor')), may hold values from 0 to 8191
- norm_gain: bfloat16 [8192], replicated, may hold values from 0.25 to 1.75
- key_weight: bfloat16 [512, 8192], P('dp', 'tensor'), may hold values from -0.0625 to 0.0625
- first_moment: float32 [512, 8192], P('dp', 'tensor'), may hold values from -6 to 6
- second_moment: float32 [512, 8192], P('dp', 'tensor'), may hold values from 0.1 to 4
Outputs:
- input_grad: bfloat16 [16384, 8192], P(('dp', 'tensor'))
- new_weight: bfloat16 [512, 8192], P(None, 'tensor')
- new_first: float32 [512, 8192], P('dp', 'tensor')
- new_second: float32 [512, 8192], P('dp', 'tensor')
The draws below stay inside these ranges and needn't reach their ends.
All inputs are finite; a program needn't handle non-finite values.
Results may differ from the reference program's by a relative error of at most 0.01.
Values may be sent and summed in bfloat16 or wider, within the bound.
A program may use at most 128 MiB of HBM per device.

```python
import math
import jax
import jax.numpy as jnp
from jax import lax

D = 8192
KV_HEADS = 4
HEAD = 128
TOK_DEV = 2048
KV = 512
TOKENS = 16384
N_DP = 8


def draw_key_grad(key, part):
    key_base = jax.random.fold_in(key, 11)
    key_column = jax.random.fold_in(key, 12)
    column_rise = jnp.arange(KV, dtype=jnp.float32) / KV
    column_jitter = jax.random.uniform(key_column, (KV,), jnp.float32, 0.0, 0.3)
    column_scale = 0.3 * 10.0 ** (column_rise + column_jitter)
    values = jax.random.truncated_normal(key_base, -4.0, 4.0, (TOKENS, KV), jnp.float32) * column_scale[None, :]
    return values.astype(jnp.bfloat16)


def set_ends(values, rng, smallest, top_value):
    longest = values.shape.index(max(values.shape))
    spots = []
    for shift in (0, 1):
        where = [jax.random.randint(jax.random.fold_in(rng, axis), (), 0, length) for axis, length in enumerate(values.shape)]
        where[longest] = (where[longest] + shift) % values.shape[longest]
        spots.append(tuple(where))
    return values.at[spots[0]].set(smallest).at[spots[1]].set(top_value)


def shard_levels(stream_key, extent, split, least, top_value):
    gain = 1.0
    for dim, blocks in split:
        steps = jax.random.uniform(jax.random.fold_in(jax.random.fold_in(stream_key, 6), dim), (blocks,), jnp.float32, least / len(split), top_value / len(split))
        gain = gain * jnp.repeat(jnp.exp(steps), extent[dim] // blocks).reshape((-1,) + (1,) * (len(extent) - 1 - dim))
    return gain


def centred(stream_key, extent, scale, reach, split=(), kind=jnp.bfloat16):
    drawn = scale * jax.random.normal(stream_key, extent, jnp.float32)
    if split:
        drawn = drawn * shard_levels(stream_key, extent, split, -0.22, 0.18)
    return jnp.clip(drawn, -reach, reach).astype(kind)


def setup_inputs(seed: int = 0) -> dict:
    splits = jax.random.split(jax.random.key(seed), 8)
    norm_input = centred(splits[0], (TOKENS, D), 1.0, 6.0, ((0, 32),))
    key_grad = draw_key_grad(jax.random.fold_in(splits[7], 71), 0)
    positions = set_ends(jax.random.randint(splits[2], (TOKENS,), 0, 8192), jax.random.fold_in(splits[2], 1), 0, 8191).astype(jnp.int32)
    norm_gain = jnp.clip(1.0 + 0.15 * jax.random.normal(splits[3], (D,), jnp.float32), 0.25, 1.75).astype(jnp.bfloat16)
    key_weight = centred(splits[4], (KV, D), D ** -0.5, 0.0625, ((0, 8), (1, 4)))
    first_moment = centred(splits[5], (KV, D), 1.0, 6.0, ((0, 8), (1, 4)), jnp.float32)
    second_moment = jnp.clip(jnp.exp(math.log(4.0) - 3.6888794 * jax.random.uniform(splits[6], (KV, D), jnp.float32) ** shard_levels(splits[6], (KV, D), ((0, 8), (1, 4)), -0.2, 0.2)), 0.1, 4.0)
    return {"norm_input": norm_input, "key_grad": key_grad, "positions": positions, "norm_gain": norm_gain, "key_weight": key_weight, "first_moment": first_moment, "second_moment": second_moment}


eps_norm = 1e-05
beta_one = 0.9
beta_two = 0.95
learn_rate = 0.0003
decay_rate = 0.1
eps_adam = 1e-08

def unrotate(incoming, positions):
    row_count = incoming.shape[0]
    half_width = HEAD // 2
    frequency = 500000.0 ** (-(2.0 * jnp.arange(half_width, dtype=jnp.float32)) / HEAD)
    angles = positions.astype(jnp.float32)[:, None] * frequency[None, :]
    cosine = jnp.cos(angles)[:, None, :]
    sine_table = jnp.sin(angles)[:, None, :]
    pieces = incoming.astype(jnp.float32).reshape(row_count, KV_HEADS, 2, half_width)
    first_half = pieces[:, :, 0, :]
    second_half = pieces[:, :, 1, :]
    upper_part = first_half * cosine + second_half * sine_table
    lower_part = second_half * cosine - first_half * sine_table
    return jnp.stack([upper_part, lower_part], axis=2).reshape(row_count, KV).astype(jnp.bfloat16)

def reference(norm_input, key_grad, positions, norm_gain, key_weight, first_moment, second_moment):
    gain_f32 = norm_gain.astype(jnp.float32)
    key_back = unrotate(key_grad, positions)
    inputs = norm_input.reshape(N_DP, TOK_DEV, D)
    cotangents = key_back.reshape(N_DP, TOK_DEV, KV)

    def one_group(total, group):
        inputs_g, keys_g = group
        inputs_f32 = inputs_g.astype(jnp.float32)
        scale_inv = lax.rsqrt(lax.optimization_barrier(jnp.mean(inputs_f32 * inputs_f32, axis=1, keepdims=True)) + eps_norm)
        normalized = inputs_f32 * scale_inv
        normed = (normalized * gain_f32).astype(jnp.bfloat16)
        upstream = jnp.dot(keys_g, key_weight, preferred_element_type=jnp.float32)
        weighted = upstream * gain_f32
        inner = lax.optimization_barrier(jnp.mean(weighted * normalized, axis=1, keepdims=True))
        group_grad = (scale_inv * (weighted - normalized * inner)).astype(jnp.bfloat16)
        partial_sum = lax.dot_general(keys_g, normed, (((0,), (0,)), ((), ())), preferred_element_type=jnp.float32)
        rounded = lax.optimization_barrier(partial_sum.astype(jnp.bfloat16))
        return (total + rounded.astype(jnp.float32), group_grad)
    weight_grad, grads = lax.scan(one_group, jnp.zeros((KV, D), jnp.float32), (inputs, cotangents))
    input_grad = grads.reshape(TOKENS, D)
    clip_limit = math.sqrt(KV * D)
    grad_size = jnp.sqrt(jnp.sum(weight_grad * weight_grad))
    clip_factor = jnp.minimum(1.0, clip_limit / (grad_size + 1e-06))
    clipped = weight_grad * clip_factor
    new_first = beta_one * first_moment + (1.0 - beta_one) * clipped
    new_second = beta_two * second_moment + (1.0 - beta_two) * clipped * clipped
    weight_f32 = key_weight.astype(jnp.float32)
    new_weight = (weight_f32 * (1.0 - learn_rate * decay_rate) - learn_rate * new_first / (jnp.sqrt(new_second) + eps_adam)).astype(jnp.bfloat16)
    return (input_grad, new_weight, new_first, new_second)
```

```python
import functools
import math

import jax
import jax.numpy as jnp
from jax import lax
from jax.experimental import pallas as pl
from jax.experimental.pallas import tpu as pltpu
from jax.sharding import PartitionSpec as P

KV_HEADS = 4
HEAD = 128


eps_norm = 1e-05
beta_one = 0.9
beta_two = 0.95
learn_rate = 0.0003
decay_rate = 0.1
eps_adam = 1e-08


def unrotate(incoming, positions):
    row_count = incoming.shape[0]
    half_width = HEAD // 2
    frequency = 500000.0 ** (-(2.0 * jnp.arange(half_width, dtype=jnp.float32)) / HEAD)
    angles = positions.astype(jnp.float32)[:, None] * frequency[None, :]
    cosine = jnp.cos(angles)[:, None, :]
    sine_table = jnp.sin(angles)[:, None, :]
    pieces = incoming.astype(jnp.float32).reshape(row_count, KV_HEADS, 2, half_width)
    first_half = pieces[:, :, 0, :]
    second_half = pieces[:, :, 1, :]
    upper_part = first_half * cosine + second_half * sine_table
    lower_part = second_half * cosine - first_half * sine_table
    return (
        jnp.stack([upper_part, lower_part], axis=2)
        .reshape(row_count, KV_HEADS * HEAD)
        .astype(jnp.bfloat16)
    )


MESH = pl.DeviceIdType.MESH
F32 = jnp.float32
BF16 = jnp.bfloat16


def kernel(
    ndp, nt, nqx, x_hbm, kb, kbt, gain, w, m1, m2,
    normed, nwb, nf, ns,
    x, wf, wg, rcore, r1a, r1b, r2a, r2b, zs, rz, gsum, sinv, cross, nsend, nrecv,
    lsem, xsem, a1s, a1r, a2s, a2r, a3s, a3r, b3s, b3r, cs, cr, qs, qr, q2s, q2r,
    zsd, zr, nss, nsr, ws, wr, vs, vr,
):
    nq = ndp // 2
    nqy = nq // nqx
    rows, cols = w.shape
    half = nq * rows
    tokens, width = x.shape
    tile = min(128, tokens)
    ntile = tokens // tile
    cc = min(512, cols)
    hc = cols // 2
    ha = pl.ds(0, hc)
    hb = pl.ds(hc, hc)
    dp = lax.axis_index("dp")
    t = lax.axis_index("tensor")
    c = dp % 2
    q = dp // 2
    qy = q // nqx
    qx = q % nqx
    mate = q * 2 + (1 - c)
    mine = pl.multiple_of(c * half, half)
    theirs = pl.multiple_of((1 - c) * half, half)
    sends = []

    def remote(src, dst, ssem, rsem, dev):
        copy = pltpu.make_async_remote_copy(
            src_ref=src, dst_ref=dst, send_sem=ssem, recv_sem=rsem, device_id=dev, device_id_type=MESH
        )
        copy.start()
        sends.append(copy)
        return copy

    def pos_x(k):
        return (qx + k) % nqx

    def pos_y(k):
        return (qy + k) % nqy

    def dev_x(k):
        return ((qy * nqx + pos_x(k)) * 2 + c, t)

    def dev_y(k):
        return ((pos_y(k) * nqx + qx) * 2 + c, t)

    def slot(yy, xx):
        return pl.ds(pl.multiple_of(mine + (yy * nqx + xx) * rows, rows), rows)

    def peer_t(i):
        return (t + 1 + i) % nt

    x_in = []
    for k in range(ntile):
        piece = pl.ds(k * tile, tile)
        copy = pltpu.make_async_copy(x_hbm.at[piece], x.at[piece], xsem.at[k])
        copy.start()
        x_in.append(copy)
    my_rows = slot(qy, qx)
    own = pltpu.make_async_copy(w, wf.at[t, my_rows], lsem)
    own.start()

    barrier = pltpu.get_barrier_semaphore()
    pl.semaphore_signal(barrier, inc=1, device_id=(mate, t), device_id_type=MESH)
    for k in range(1, nqx):
        pl.semaphore_signal(barrier, inc=1, device_id=dev_x(k), device_id_type=MESH)
    for k in range(1, nqy):
        pl.semaphore_signal(barrier, inc=1, device_id=dev_y(k), device_id_type=MESH)
    for i in range(nt - 1):
        pl.semaphore_signal(barrier, inc=1, device_id=(dp, peer_t(i)), device_id_type=MESH)
    pl.semaphore_wait(barrier, 1 + (nqx - 1) + (nqy - 1) + (nt - 1))

    a1 = [remote(w, wf.at[t, my_rows], a1s.at[i], a1r.at[i], (dp, peer_t(i))) for i in range(nt - 1)]
    na = nqx + nqy - 2
    first_hop = {}
    second_hop = {}

    def block(i):
        return (t + nt - i) % nt

    def gather_first(i):
        j = block(i)
        if i > 0:
            a1[i - 1].wait_recv()
        src = w if i == 0 else wf.at[j, my_rows]
        batch = []
        for k in range(1, nqx):
            n = i * na + k - 1
            batch.append(
                remote(src.at[:, ha], wf.at[j, my_rows, ha], a2s.at[n], a2r.at[n], dev_x(k))
            )
        for k in range(1, nqy):
            n = i * na + nqx - 1 + k - 1
            batch.append(
                remote(src.at[:, hb], wf.at[j, my_rows, hb], a2s.at[n], a2r.at[n], dev_y(k))
            )
        first_hop[i] = batch

    nb = (nqx - 1) * nqy + (nqy - 1) * nqx

    def gather_second(i):
        j = block(i)
        for copy in first_hop[i]:
            copy.wait_recv()
        batch = []
        n = i * nb
        for k in range(1, nqy):
            for xx in range(nqx):
                part = wf.at[j, slot(qy, xx), ha]
                batch.append(remote(part, part, b3s.at[n], b3r.at[n], dev_y(k)))
                n += 1
        for k in range(1, nqx):
            for yy in range(nqy):
                part = wf.at[j, slot(yy, qx), hb]
                batch.append(remote(part, part, b3s.at[n], b3r.at[n], dev_x(k)))
                n += 1
        second_hop[i] = batch

    gather_first(0)
    cross[...] = jnp.zeros_like(cross)

    for k in range(ntile):
        x_in[k].wait()

        @pl.loop(0, tile // 16)
        def _(g):
            r = pl.ds(pl.multiple_of(k * tile + g * 16, 16), 16)
            v = x[r, :].astype(F32)
            s = lax.rsqrt(jnp.sum(v * v, axis=1, keepdims=True) / width + eps_norm)
            sinv[r, :] = jnp.broadcast_to(s, (16, 128))
            normed[r, :] = (v * s * gain[...]).astype(BF16)

        if k == ntile // 2:
            own.wait()
            gather_second(0)
        if k == ntile - 1:
            gather_first(1)

    def product(j):
        @pl.loop(0, cols // cc)
        def _(h):
            off = pl.multiple_of(h * cc, cc)
            col = pl.ds(pl.multiple_of(j * cols + h * cc, cc), cc)
            wg[j, :, pl.ds(off, cc)] = jnp.dot(
                kbt[...], normed[:, col], preferred_element_type=F32
            ).astype(BF16)

    core_copies = []
    q_copies = []
    q2_copies = []

    def pair_sum(i):
        j = peer_t(i)
        core_copies[i].wait_recv()

        @pl.loop(0, half // 16)
        def _(g):
            r = pl.ds(pl.multiple_of(mine + g * 16, 16), 16)
            a = wg[j, r, :].astype(F32) + rcore[j, pl.ds(pl.multiple_of(g * 16, 16), 16), :].astype(F32)
            wg[j, r, :] = a.astype(BF16)

        batch = []
        n = i * nb
        for k in range(1, nqx):
            for yy in range(nqy):
                src = wg.at[j, slot(yy, pos_x(k)), ha]
                batch.append(
                    remote(src, r1a.at[i, (k - 1) * nqy + yy], qs.at[n], qr.at[n], dev_x(k))
                )
                n += 1
        for k in range(1, nqy):
            for xx in range(nqx):
                src = wg.at[j, slot(pos_y(k), xx), hb]
                batch.append(
                    remote(src, r1b.at[i, (k - 1) * nqx + xx], qs.at[n], qr.at[n], dev_y(k))
                )
                n += 1
        q_copies.append(batch)

    for i in range(nt):
        j = peer_t(i)
        product(j)
        core_copies.append(
            remote(wg.at[j, pl.ds(theirs, half)], rcore.at[j], cs.at[i], cr.at[i], (mate, t))
        )
        if i == 1:
            gather_second(1)
        if i > 0:
            pair_sum(i - 1)
    pair_sum(nt - 1)

    def middle(i):
        j = peer_t(i)
        for copy in q_copies[i]:
            copy.wait_recv()

        @pl.loop(0, rows // 16)
        def _(g):
            l = pl.ds(pl.multiple_of(g * 16, 16), 16)
            for yy in range(nqy):
                r = pl.ds(pl.multiple_of(mine + (yy * nqx + qx) * rows + g * 16, 16), 16)
                a = wg[j, r, ha].astype(F32)
                for k in range(nqx - 1):
                    a = a + r1a[i, k * nqy + yy, l, :].astype(F32)
                wg[j, r, ha] = a.astype(BF16)
            for xx in range(nqx):
                r = pl.ds(pl.multiple_of(mine + (qy * nqx + xx) * rows + g * 16, 16), 16)
                a = wg[j, r, hb].astype(F32)
                for k in range(nqy - 1):
                    a = a + r1b[i, k * nqx + xx, l, :].astype(F32)
                wg[j, r, hb] = a.astype(BF16)

        batch = []
        n = i * na
        for k in range(1, nqy):
            batch.append(
                remote(wg.at[j, slot(pos_y(k), qx), ha], r2a.at[i, k - 1], q2s.at[n], q2r.at[n], dev_y(k))
            )
            n += 1
        for k in range(1, nqx):
            batch.append(
                remote(wg.at[j, slot(qy, pos_x(k)), hb], r2b.at[i, k - 1], q2s.at[n], q2r.at[n], dev_x(k))
            )
            n += 1
        q2_copies.append(batch)

    z_copies = []

    def final(i):
        j = peer_t(i)
        for copy in q2_copies[i]:
            copy.wait_recv()

        @pl.loop(0, rows // 16)
        def _(g):
            r = pl.ds(pl.multiple_of(g * 16, 16), 16)
            m = pl.ds(pl.multiple_of(mine + q * rows + g * 16, 16), 16)
            for part, other, count in ((ha, r2a, nqy - 1), (hb, r2b, nqx - 1)):
                a = wg[j, m, part].astype(F32)
                for k in range(count):
                    a = a + other[i, k, r, :].astype(F32)
                if i < nt - 1:
                    zs[i, r, part] = a.astype(BF16)
                else:
                    gsum[r, part] = a

        if i < nt - 1:
            z_copies.append(remote(zs.at[i], rz.at[i], zsd.at[i], zr.at[i], (dp, j)))

    for i in range(nt):
        middle(i)
        if i > 1:
            gather_first(i)
    for i in range(nt):
        final(i)
        if i > 1:
            gather_second(i)

    a3 = {}

    def gather_third(i):
        for copy in second_hop[i]:
            copy.wait_recv()
        part = wf.at[block(i), pl.ds(mine, half)]
        a3[i] = remote(part, part, a3s.at[i], a3r.at[i], (mate, t))

    uc = min(256, cols)

    def upstream(i):
        j = block(i)
        a3[i].wait_recv()

        @pl.loop(0, cols // uc)
        def _(h):
            off = pl.ds(pl.multiple_of(h * uc, uc), uc)
            col = pl.ds(pl.multiple_of(j * cols + h * uc, uc), uc)
            u = jnp.dot(kb[...], wf[j, :, off], preferred_element_type=F32) * gain[:, col]
            normed[:, col] = u.astype(BF16)
            p = u * x[:, col].astype(F32)
            total = p[:, :128]
            for b in range(1, uc // 128):
                total = total + p[:, b * 128 : (b + 1) * 128]
            cross[...] += total

    for i in range(2):
        gather_third(i)
        upstream(i)
    for copy in z_copies:
        copy.wait_recv()

    nsend[0] = jnp.zeros((8, 128), F32)

    @pl.loop(0, rows // 16)
    def _(g):
        r = pl.ds(pl.multiple_of(g * 16, 16), 16)
        a = gsum[r, :]
        for i in range(nt - 1):
            a = a + rz[i, r, :].astype(F32)
        gsum[r, :] = a
        a = a * a
        a = a[:8] + a[8:]
        total = a[:, :128]
        for k in range(1, cols // 128):
            total = total + a[:, k * 128 : (k + 1) * 128]
        nsend[0] += total

    base = 0
    v = nsend[0]
    groups = (
        [(mate, t)],
        [(dp, peer_t(i)) for i in range(nt - 1)],
        [dev_x(k) for k in range(1, nqx)],
        [dev_y(k) for k in range(1, nqy)],
    )
    for step, devs in enumerate(groups):
        if step > 0:
            nsend[step] = v
        batch = [
            remote(nsend.at[step], nrecv.at[base + n], nss.at[base + n], nsr.at[base + n], dev)
            for n, dev in enumerate(devs)
        ]
        if step == 1:
            for i in range(2, nt - 1):
                gather_third(i)
                upstream(i)
        for n, copy in enumerate(batch):
            copy.wait_recv()
            v = v + nrecv[base + n]
        base += len(devs)
    total_square = jnp.sum(jnp.sum(v, axis=1, keepdims=True), axis=0, keepdims=True)
    limit = math.sqrt(kbt.shape[0] * width)
    clip = jnp.minimum(1.0, limit / (jnp.sqrt(total_square) + 1e-06))
    nat = pl.multiple_of(c * rows, rows)

    @pl.loop(0, rows // 16)
    def _(g):
        r = pl.ds(pl.multiple_of(g * 16, 16), 16)
        clipped = gsum[r, :] * clip
        first = beta_one * m1[r, :] + (1.0 - beta_one) * clipped
        second = beta_two * m2[r, :] + (1.0 - beta_two) * clipped * clipped
        nf[r, :] = first
        ns[r, :] = second
        nwb[q, pl.ds(pl.multiple_of(nat + g * 16, 16), 16), :] = (
            w[r, :].astype(F32) * (1.0 - learn_rate * decay_rate)
            - learn_rate * first / (jnp.sqrt(second) + eps_adam)
        ).astype(BF16)

    def piece_of(yy, xx, part):
        return nwb.at[yy * nqx + xx, pl.ds(nat, rows), part]

    w_first = []
    for k in range(1, nqx):
        part = piece_of(qy, qx, ha)
        w_first.append(remote(part, part, ws.at[k - 1], wr.at[k - 1], dev_x(k)))
    for k in range(1, nqy):
        n = nqx - 1 + k - 1
        part = piece_of(qy, qx, hb)
        w_first.append(remote(part, part, ws.at[n], wr.at[n], dev_y(k)))

    gather_third(nt - 1)
    upstream(nt - 1)

    for copy in w_first:
        copy.wait_recv()
    w_second = []
    for k in range(1, nqy):
        for xx in range(nqx):
            part = piece_of(qy, xx, ha)
            n = len(w_second)
            w_second.append(remote(part, part, vs.at[n], vr.at[n], dev_y(k)))
    for k in range(1, nqx):
        for yy in range(nqy):
            part = piece_of(yy, qx, hb)
            n = len(w_second)
            w_second.append(remote(part, part, vs.at[n], vr.at[n], dev_x(k)))

    for k in range(ntile):
        @pl.loop(0, tile // 16)
        def _(g):
            r = pl.ds(pl.multiple_of(k * tile + g * 16, 16), 16)
            s = sinv[r, :1]
            inner = s * (jnp.sum(cross[r, :], axis=1, keepdims=True) / width)
            normed[r, :] = (
                s * (normed[r, :].astype(F32) - x[r, :].astype(F32) * s * inner)
            ).astype(BF16)

    for copy in w_second:
        copy.wait_recv()
    part = nwb.at[:, pl.ds(nat, rows)]
    last = remote(part, part, vs.at[nb], vr.at[nb], (mate, t))
    last.wait_recv()
    for sent in sends:
        sent.wait_send()


def body(ndp, nt, norm_input, key_grad, positions, norm_gain, key_weight, first_moment, second_moment):
    rows, cols = key_weight.shape
    tokens, width = norm_input.shape
    nq = ndp // 2
    features = ndp * rows
    back = unrotate(key_grad, positions)
    back = back.reshape(tokens, nq, 2, rows).transpose(0, 2, 1, 3).reshape(tokens, features)
    tile = min(128, tokens)
    ntile = tokens // tile
    any_spec = pl.BlockSpec(memory_space=pl.ANY)
    vmem = pl.BlockSpec(memory_space=pltpu.VMEM)
    dma = pltpu.SemaphoreType.DMA
    nqx = math.isqrt(nq)
    while nq % nqx:
        nqx -= 1
    nqy = nq // nqx
    hc = cols // 2
    na = nqx + nqy - 2
    nb = (nqx - 1) * nqy + (nqy - 1) * nqx
    nn = 1 + na + nt - 1
    scratch = [
        pltpu.VMEM((tokens, width), BF16),
        pltpu.VMEM((nt, features, cols), BF16),
        pltpu.VMEM((nt, features, cols), BF16),
        pltpu.VMEM((nt, nq * rows, cols), BF16),
        pltpu.VMEM((nt, (nqx - 1) * nqy, rows, hc), BF16),
        pltpu.VMEM((nt, (nqy - 1) * nqx, rows, hc), BF16),
        pltpu.VMEM((nt, nqy - 1, rows, hc), BF16),
        pltpu.VMEM((nt, nqx - 1, rows, hc), BF16),
        pltpu.VMEM((nt - 1, rows, cols), BF16),
        pltpu.VMEM((nt - 1, rows, cols), BF16),
        pltpu.VMEM((rows, cols), F32),
        pltpu.VMEM((tokens, 128), F32),
        pltpu.VMEM((tokens, 128), F32),
        pltpu.VMEM((4, 8, 128), F32),
        pltpu.VMEM((nn, 8, 128), F32),
        dma, dma((ntile,)),
    ]
    for count in (nt - 1, nt * na, nt, nt * nb, nt, nt * nb, nt * na, nt - 1, nn, na, nb + 1):
        scratch += [dma((count,)), dma((count,))]
    input_grad, new_weight, new_first, new_second = pl.pallas_call(
        functools.partial(kernel, ndp, nt, nqx),
        out_shape=(
            pltpu.VMEM((tokens, width), BF16),
            pltpu.VMEM((nq, 2 * rows, cols), BF16),
            pltpu.VMEM((rows, cols), F32),
            pltpu.VMEM((rows, cols), F32),
        ),
        in_specs=[any_spec] + [vmem] * 6,
        out_specs=(vmem, vmem, vmem, vmem),
        scratch_shapes=scratch,
        compiler_params=pltpu.CompilerParams(
            collective_id=0, has_side_effects=True, vmem_limit_bytes=46 * 2**20
        ),
    )(
        norm_input, back, back.T, norm_gain.astype(F32)[None, :], key_weight, first_moment, second_moment,
    )
    return (input_grad, new_weight.reshape(features, cols), new_first, new_second)


def solution(mesh):
    in_specs = (
        P(("dp", "tensor"), None),
        P(("dp", "tensor"), None),
        P(("dp", "tensor")),
        P(),
        P("dp", "tensor"),
        P("dp", "tensor"),
        P("dp", "tensor"),
    )
    out_specs = (P(("dp", "tensor"), None), P(None, "tensor"), P("dp", "tensor"), P("dp", "tensor"))
    return jax.shard_map(
        functools.partial(body, mesh.shape["dp"], mesh.shape["tensor"]),
        mesh=mesh, in_specs=in_specs, out_specs=out_specs, check_vma=False,
    )
```

```python
import functools
import math

import jax
import jax.numpy as jnp
import numpy as np
from jax import lax
from jax.experimental import pallas as pl
from jax.experimental.pallas import tpu as pltpu
from jax.sharding import PartitionSpec as P

KV_HEADS = 4
HEAD = 128
ROPE_BASE = 500000.0

eps_norm = 1e-05
beta_one = 0.9
beta_two = 0.95
learn_rate = 0.0003
decay_rate = 0.1
eps_adam = 1e-08

MESH = pl.DeviceIdType.MESH
F32 = jnp.float32
BF16 = jnp.bfloat16


def kernel(
    ndp, nt, nqx, x_hbm, kg_hbm, pos_hbm, gain_hbm, freq_hbm, w_hbm, m1_hbm, m2_hbm,
    grad, nwb, nf, ns,
    x, kg, pos, gain_in, freq, m1, m2, gain, kb, kbt, sks, ssq, cross,
    wf, wg, rcore, r1a, r1b, r2a, r2b, zs, rz, gsum, nsend, nrecv,
    isem, xsem, a1s, a1r, zfs, zfr, b3s, b3r, a3s, a3r, cs, cr, qs, qr, q2s, q2r,
    zsd, zr, nss, nsr, ws, wr, vs, vr,
):
    nq = ndp // 2
    nqy = nq // nqx
    rows, cols = w_hbm.shape
    half = nq * rows
    tokens, width = x.shape
    tile = min(128, tokens)
    ntile = tokens // tile
    hc = cols // 2
    cc = min(512, hc)
    hcol = (pl.ds(0, hc), pl.ds(hc, hc))
    dp = lax.axis_index("dp")
    t = lax.axis_index("tensor")
    c = dp % 2
    q = dp // 2
    qy = q // nqx
    qx = q % nqx
    mate = q * 2 + (1 - c)
    mine = pl.multiple_of(c * half, half)
    theirs = pl.multiple_of((1 - c) * half, half)
    sends = []

    def describe(src, dst, ssem, rsem, dev):
        return pltpu.make_async_remote_copy(
            src_ref=src, dst_ref=dst, send_sem=ssem, recv_sem=rsem, device_id=dev, device_id_type=MESH
        )

    def remote(src, dst, ssem, rsem, dev):
        copy = describe(src, dst, ssem, rsem, dev)
        copy.start()
        sends.append((None, copy))
        return copy

    def pos_x(k):
        return (qx + k) % nqx

    def pos_y(k):
        return (qy + k) % nqy

    def dev_x(k):
        return ((qy * nqx + pos_x(k)) * 2 + c, t)

    def dev_y(k):
        return ((pos_y(k) * nqx + qx) * 2 + c, t)

    def slot(yy, xx):
        return pl.ds(pl.multiple_of(mine + (yy * nqx + xx) * rows, rows), rows)

    def band(yy):
        return pl.ds(pl.multiple_of(mine + yy * nqx * rows, nqx * rows), nqx * rows)

    my_rows = slot(qy, qx)
    steps = sorted(range(1, nt), key=lambda o: (-min(o, nt - o), o)) + [0]

    def dest(i):
        return (t + steps[i]) % nt

    near = jnp.minimum(t, nt - 1 - t)
    low = t < nt - 1 - t

    def block(i):
        if i == 0:
            return t
        d = (i + 1) // 2
        both = t - d if i % 2 else t + d
        return jnp.where(i <= 2 * near, both, jnp.where(low, i, nt - 1 - i))

    def local(src, dst, sem):
        copy = pltpu.make_async_copy(src, dst, sem)
        copy.start()
        return copy

    own = local(w_hbm, wf.at[t, my_rows], isem.at[0])
    kg_in = local(kg_hbm, kg, isem.at[1])
    pos_in = local(pos_hbm, pos, isem.at[2])
    freq_in = local(freq_hbm, freq, isem.at[3])
    x_in = []
    for k in range(ntile):
        piece = pl.ds(k * tile, tile)
        x_in.append(local(x_hbm.at[piece], x.at[piece], xsem.at[k]))
    gain_copy = local(gain_hbm, gain_in, isem.at[4])
    m1_in = local(m1_hbm, m1, isem.at[5])
    m2_in = local(m2_hbm, m2, isem.at[6])

    barrier = pltpu.get_barrier_semaphore()
    for k in range(1, ndp):
        pl.semaphore_signal(barrier, inc=1, device_id=((dp + k) % ndp, t), device_id_type=MESH)
    for k in range(1, nt):
        pl.semaphore_signal(barrier, inc=1, device_id=(dp, (t + k) % nt), device_id_type=MESH)
    pl.semaphore_wait(barrier, ndp - 1 + nt - 1)

    na = nqx + nqy - 2
    first = [
        remote(w_hbm.at[:, hcol[0]], wf.at[t, my_rows, hcol[0]], a1s.at[k - 1], a1r.at[k - 1], dev_x(k))
        for k in range(1, nqx)
    ]
    first += [
        remote(
            w_hbm.at[:, hcol[1]], wf.at[t, my_rows, hcol[1]],
            a1s.at[nqx + k - 2], a1r.at[nqx + k - 2], dev_y(k),
        )
        for k in range(1, nqy)
    ]

    def line_pieces(b, side, dev):
        parts = [wf.at[b, band(qy), hcol[0]]]
        parts += [wf.at[b, slot(yy, qx), hcol[1]] for yy in range(nqy)]
        return [
            describe(part, part, zfs.at[side, b, n], zfr.at[b, n], dev) for n, part in enumerate(parts)
        ]

    def pass_on(b, side):
        to, there = (t + 1, t + 1 < nt) if side == 0 else (t - 1, t >= 1)

        @pl.when(there)
        def _():
            for copy in line_pieces(b, side, (dp, to)):
                copy.start()

    line_sent = []

    def relay(d):
        for side, b, here in ((0, t - d, t - d >= 0), (1, t + d, t + d < nt)):
            @pl.when(here)
            def _(side=side, b=b):
                for copy in line_pieces(b, side, (dp, t)):
                    copy.wait_recv()
                pass_on(b, side)

            line_sent.append((side, b, here))

    nb = (nqy - 1) + (nqx - 1) * nqy
    spread_copies = {}

    def spread(i):
        b = block(i)
        batch = []
        for k in range(1, nqy):
            part = wf.at[b, band(qy), hcol[0]]
            batch.append(remote(part, part, b3s.at[i, k - 1], b3r.at[i, k - 1], dev_y(k)))
        for k in range(1, nqx):
            for yy in range(nqy):
                n = nqy - 1 + (k - 1) * nqy + yy
                part = wf.at[b, slot(yy, qx), hcol[1]]
                batch.append(remote(part, part, b3s.at[i, n], b3r.at[i, n], dev_x(k)))
        spread_copies[i] = batch

    third = {}

    def gather_third(i):
        for copy in spread_copies[i]:
            copy.wait_recv()
        part = wf.at[block(i), pl.ds(mine, half)]
        third[i] = remote(part, part, a3s.at[i], a3r.at[i], (mate, t))

    cross[...] = jnp.zeros_like(cross)
    kg_in.wait()
    pos_in.wait()
    freq_in.wait()
    hh = HEAD // 2
    for k in range(ntile):
        lanes = pl.ds(k * tile, tile)
        angle = freq[:, :tile] * pos[k : k + 1, :tile].astype(F32)
        cosine = jnp.cos(angle)
        sine = jnp.sin(angle)
        turned = kg[pl.ds(k * tile, tile), :].astype(F32).T
        for h in range(KV_HEADS):
            a = turned[h * HEAD : h * HEAD + hh]
            b = turned[h * HEAD + hh : (h + 1) * HEAD]
            for p, value in enumerate((a * cosine + b * sine, b * cosine - a * sine)):
                value = value.astype(BF16)
                for m in range(hh // rows):
                    n = (h * HEAD + p * hh) // rows + m
                    kbt[pl.ds((n % 2) * half + (n // 2) * rows, rows), lanes] = value[
                        m * rows : (m + 1) * rows
                    ]

    def sum_squares(k):
        x_in[k].wait()

        @pl.loop(0, tile // 16)
        def _(g):
            r = pl.ds(pl.multiple_of(k * tile + g * 16, 16), 16)
            total = None
            for b in range(width // 512):
                v = x[r, b * 512 : (b + 1) * 512].astype(F32)
                v = v * v
                v = (v[:, :128] + v[:, 128:256]) + (v[:, 256:384] + v[:, 384:])
                total = v if total is None else total + v
            ssq[r, :] = total

        lanes = pl.ds(k * tile, tile)
        mean = jnp.sum(ssq[lanes, :].T, axis=0, keepdims=True) / width
        sks[:, lanes] = (kbt[:, lanes].astype(F32) * lax.rsqrt(mean + eps_norm)).astype(BF16)

    for k in range(ntile):
        sum_squares(k)
        if k == ntile // 2:
            own.wait()
            for copy in first:
                copy.wait_recv()
            pass_on(t, 0)
            pass_on(t, 1)
            spread(0)

    gain_copy.wait()
    for k in range(width // 128):
        gain[:, k * 128 : (k + 1) * 128] = gain_in[k : k + 1, :].astype(F32)

    core_copies = {}

    def product(i, h):
        j = dest(i)

        @pl.loop(0, hc // cc)
        def _(n):
            off = pl.ds(pl.multiple_of(h * hc + n * cc, cc), cc)
            col = pl.ds(pl.multiple_of(j * cols + h * hc + n * cc, cc), cc)
            total = jnp.dot(sks[...], x[:, col], preferred_element_type=F32)
            wg[j, :, off] = (total * gain[:, col]).astype(BF16)

        n = i * 2 + h
        core_copies[n] = remote(
            wg.at[j, pl.ds(theirs, half), hcol[h]], rcore.at[j, :, hcol[h]], cs.at[n], cr.at[n], (mate, t)
        )

    def pair_sum(i, h):
        j = dest(i)
        core_copies[i * 2 + h].wait_recv()

        @pl.loop(0, half // 16)
        def _(g):
            r = pl.ds(pl.multiple_of(mine + g * 16, 16), 16)
            l = pl.ds(pl.multiple_of(g * 16, 16), 16)
            a = wg[j, r, hcol[h]].astype(F32) + rcore[j, l, hcol[h]].astype(F32)
            wg[j, r, hcol[h]] = a.astype(BF16)

    nx1 = (nqx - 1) * nqy
    q_copies = {}
    q2_copies = {}

    def reduce_first(i, h):
        j = dest(i)
        batch = []
        if h == 0:
            for k in range(1, nqx):
                for yy in range(nqy):
                    n = (k - 1) * nqy + yy
                    src = wg.at[j, slot(yy, pos_x(k)), hcol[0]]
                    batch.append(remote(src, r1a.at[i, n], qs.at[i, n], qr.at[i, n], dev_x(k)))
        else:
            for k in range(1, nqy):
                n = nx1 + k - 1
                src = wg.at[j, band(pos_y(k)), hcol[1]]
                batch.append(remote(src, r1b.at[i, k - 1], qs.at[i, n], qr.at[i, n], dev_y(k)))
        q_copies[i, h] = batch

    def middle(i, h):
        j = dest(i)
        for copy in q_copies[i, h]:
            copy.wait_recv()
        batch = []
        if h == 0:
            @pl.loop(0, rows // 16)
            def _(g):
                l = pl.ds(pl.multiple_of(g * 16, 16), 16)
                for yy in range(nqy):
                    r = pl.ds(pl.multiple_of(mine + (yy * nqx + qx) * rows + g * 16, 16), 16)
                    a = wg[j, r, hcol[0]].astype(F32)
                    for k in range(nqx - 1):
                        a = a + r1a[i, k * nqy + yy, l, :].astype(F32)
                    wg[j, r, hcol[0]] = a.astype(BF16)

            for k in range(1, nqy):
                n = k - 1
                src = wg.at[j, slot(pos_y(k), qx), hcol[0]]
                batch.append(remote(src, r2a.at[i, k - 1], q2s.at[i, n], q2r.at[i, n], dev_y(k)))
        else:
            @pl.loop(0, nqx * rows // 16)
            def _(g):
                l = pl.ds(pl.multiple_of(g * 16, 16), 16)
                r = pl.ds(pl.multiple_of(mine + qy * nqx * rows + g * 16, 16), 16)
                a = wg[j, r, hcol[1]].astype(F32)
                for k in range(nqy - 1):
                    a = a + r1b[i, k, l, :].astype(F32)
                wg[j, r, hcol[1]] = a.astype(BF16)

            for k in range(1, nqx):
                n = nqy - 1 + k - 1
                src = wg.at[j, slot(qy, pos_x(k)), hcol[1]]
                batch.append(remote(src, r2b.at[i, k - 1], q2s.at[i, n], q2r.at[i, n], dev_x(k)))
        q2_copies[i, h] = batch

    z_copies = []

    def final(i):
        j = dest(i)
        for h in range(2):
            for copy in q2_copies[i, h]:
                copy.wait_recv()

        @pl.loop(0, rows // 16)
        def _(g):
            r = pl.ds(pl.multiple_of(g * 16, 16), 16)
            m = pl.ds(pl.multiple_of(mine + q * rows + g * 16, 16), 16)
            for part, other, count in ((hcol[0], r2a, nqy - 1), (hcol[1], r2b, nqx - 1)):
                a = wg[j, m, part].astype(F32)
                for k in range(count):
                    a = a + other[i, k, r, :].astype(F32)
                if i < nt - 1:
                    zs[i, r, part] = a.astype(BF16)
                else:
                    gsum[r, part] = a

        if i < nt - 1:
            z_copies.append(remote(zs.at[i], rz.at[i], zsd.at[i], zr.at[i], (dp, j)))

    uc = min(256, cols)

    def upstream(i):
        b = block(i)
        third[i].wait_recv()

        @pl.loop(0, cols // uc)
        def _(h):
            off = pl.ds(pl.multiple_of(h * uc, uc), uc)
            col = pl.ds(pl.multiple_of(b * cols + h * uc, uc), uc)
            u = jnp.dot(kb[...], wf[b, :, off], preferred_element_type=F32) * gain[:, col]
            grad[:, col] = u.astype(BF16)
            p = u * x[:, col].astype(F32)
            total = p[:, :128]
            for n in range(1, uc // 128):
                total = total + p[:, n * 128 : (n + 1) * 128]
            cross[...] += total

    def turn_back():
        for k in range(ntile):
            lanes = pl.ds(k * tile, tile)
            kb[lanes, :] = kbt[:, lanes].astype(F32).T.astype(BF16)

    units = [(i, h) for i in range(nt) for h in range(2)]
    for n, unit in enumerate(units):
        product(*unit)
        if n > 0:
            pair_sum(*units[n - 1])
            if units[n - 1][0] < 2:
                reduce_first(*units[n - 1])
    pair_sum(*units[-1])
    turn_back()
    gather_third(0)
    for i in range(nt):
        for h in range(2):
            middle(i, h)
            if i + 2 < nt:
                reduce_first(i + 2, h)
        if i == 0:
            relay(1)
            upstream(0)
        if 0 < i < nt - 1:
            relay(i + 1)
        if i > 0:
            final(i - 1)
    for i in range(1, nt):
        spread(i)
    final(nt - 1)
    for copy in z_copies:
        copy.wait_recv()

    nsend[0] = jnp.zeros((8, 128), F32)

    @pl.loop(0, rows // 16)
    def _(g):
        r = pl.ds(pl.multiple_of(g * 16, 16), 16)
        a = gsum[r, :]
        for i in range(nt - 1):
            a = a + rz[i, r, :].astype(F32)
        gsum[r, :] = a
        a = a * a
        a = a[:8] + a[8:]
        total = a[:, :128]
        for k in range(1, cols // 128):
            total = total + a[:, k * 128 : (k + 1) * 128]
        nsend[0] += total

    v = nsend[0]
    base = 0
    groups = (
        [((dp + k) % ndp, t) for k in range(1, ndp)],
        [(dp, (t + k) % nt) for k in range(1, nt)],
    )
    for step, devs in enumerate(groups):
        if step > 0:
            nsend[step] = v
        batch = [
            remote(nsend.at[step], nrecv.at[base + n], nss.at[base + n], nsr.at[base + n], dev)
            for n, dev in enumerate(devs)
        ]
        if step == 0:
            gather_third(1)
        for n, copy in enumerate(batch):
            copy.wait_recv()
            v = v + nrecv[base + n]
        base += len(devs)
    total_square = jnp.sum(jnp.sum(v, axis=1, keepdims=True), axis=0, keepdims=True)
    limit = math.sqrt(kbt.shape[0] * width)
    clip = jnp.minimum(1.0, limit / (jnp.sqrt(total_square) + 1e-06))
    nat = pl.multiple_of(c * rows, rows)
    m1_in.wait()
    m2_in.wait()

    @pl.loop(0, rows // 16)
    def _(g):
        r = pl.ds(pl.multiple_of(g * 16, 16), 16)
        wr_ = pl.ds(pl.multiple_of(mine + q * rows + g * 16, 16), 16)
        clipped = gsum[r, :] * clip
        new_first = beta_one * m1[r, :] + (1.0 - beta_one) * clipped
        new_second = beta_two * m2[r, :] + (1.0 - beta_two) * clipped * clipped
        nf[r, :] = new_first
        ns[r, :] = new_second
        nwb[q, pl.ds(pl.multiple_of(nat + g * 16, 16), 16), :] = (
            wf[t, wr_, :].astype(F32) * (1.0 - learn_rate * decay_rate)
            - learn_rate * new_first / (jnp.sqrt(new_second) + eps_adam)
        ).astype(BF16)

    def piece_of(yy, xx, part):
        return nwb.at[yy * nqx + xx, pl.ds(nat, rows), part]

    w_first = []
    for k in range(1, nqx):
        part = piece_of(qy, qx, hcol[0])
        w_first.append(remote(part, part, ws.at[k - 1], wr.at[k - 1], dev_x(k)))
    for k in range(1, nqy):
        n = nqx - 1 + k - 1
        part = piece_of(qy, qx, hcol[1])
        w_first.append(remote(part, part, ws.at[n], wr.at[n], dev_y(k)))

    for i in range(1, nt - 1):
        upstream(i)
        gather_third(i + 1)

    for copy in w_first:
        copy.wait_recv()
    w_second = []
    for k in range(1, nqy):
        for xx in range(nqx):
            part = piece_of(qy, xx, hcol[0])
            n = len(w_second)
            w_second.append(remote(part, part, vs.at[n], vr.at[n], dev_y(k)))
    for k in range(1, nqx):
        for yy in range(nqy):
            part = piece_of(yy, qx, hcol[1])
            n = len(w_second)
            w_second.append(remote(part, part, vs.at[n], vr.at[n], dev_x(k)))
    upstream(nt - 1)

    sc = min(1024, width)

    @pl.loop(0, tokens // 16)
    def _(g):
        r = pl.ds(pl.multiple_of(g * 16, 16), 16)
        s = lax.rsqrt(jnp.sum(ssq[r, :], axis=1, keepdims=True) / width + eps_norm)
        inner = s * (jnp.sum(cross[r, :], axis=1, keepdims=True) / width)
        up = jnp.broadcast_to(s, (16, sc))
        down = jnp.broadcast_to(s * s * inner, (16, sc))
        for b in range(width // sc):
            col = slice(b * sc, (b + 1) * sc)
            grad[r, col] = (up * grad[r, col].astype(F32) - down * x[r, col].astype(F32)).astype(BF16)

    for copy in w_second:
        copy.wait_recv()
    part = nwb.at[:, pl.ds(nat, rows)]
    n = len(w_second)
    last = remote(part, part, vs.at[n], vr.at[n], (mate, t))
    last.wait_recv()
    for _, sent in sends:
        sent.wait_send()
    for side, b, here in [(0, t, t >= 0), (1, t, t >= 0)] + line_sent:
        there = t + 1 < nt if side == 0 else t >= 1

        @pl.when(jnp.logical_and(here, there))
        def _(side=side, b=b):
            for copy in line_pieces(b, side, (dp, t)):
                copy.wait_send()


def body(ndp, nt, norm_input, key_grad, positions, norm_gain, key_weight, first_moment, second_moment):
    rows, cols = key_weight.shape
    tokens, width = norm_input.shape
    nq = ndp // 2
    features = ndp * rows
    tile = min(128, tokens)
    ntile = tokens // tile
    hh = HEAD // 2
    frequency = ROPE_BASE ** (-(2.0 * np.arange(hh)) / HEAD)
    frequency = np.broadcast_to(frequency.astype(np.float32)[:, None], (hh, 128))
    any_spec = pl.BlockSpec(memory_space=pl.ANY)
    vmem = pl.BlockSpec(memory_space=pltpu.VMEM)
    dma = pltpu.SemaphoreType.DMA
    nqx = math.isqrt(nq)
    while nq % nqx:
        nqx -= 1
    nqy = nq // nqx
    hc = cols // 2
    na = nqx + nqy - 2
    nx1 = (nqx - 1) * nqy
    nw2 = nx1 + (nqy - 1) * nqx
    nn = ndp - 1 + nt - 1
    scratch = [
        pltpu.VMEM((tokens, width), BF16),
        pltpu.VMEM((tokens, features), BF16),
        pltpu.VMEM((ntile, tile), jnp.int32),
        pltpu.VMEM((width // 128, 128), BF16),
        pltpu.VMEM((hh, 128), F32),
        pltpu.VMEM((rows, cols), F32),
        pltpu.VMEM((rows, cols), F32),
        pltpu.VMEM((1, width), F32),
        pltpu.VMEM((tokens, features), BF16),
        pltpu.VMEM((features, tokens), BF16),
        pltpu.VMEM((features, tokens), BF16),
        pltpu.VMEM((tokens, 128), F32),
        pltpu.VMEM((tokens, 128), F32),
        pltpu.VMEM((nt, features, cols), BF16),
        pltpu.VMEM((nt, features, cols), BF16),
        pltpu.VMEM((nt, nq * rows, cols), BF16),
        pltpu.VMEM((nt, nx1, rows, hc), BF16),
        pltpu.VMEM((nt, nqy - 1, nqx * rows, hc), BF16),
        pltpu.VMEM((nt, nqy - 1, rows, hc), BF16),
        pltpu.VMEM((nt, nqx - 1, rows, hc), BF16),
        pltpu.VMEM((nt - 1, rows, cols), BF16),
        pltpu.VMEM((nt - 1, rows, cols), BF16),
        pltpu.VMEM((rows, cols), F32),
        pltpu.VMEM((2, 8, 128), F32),
        pltpu.VMEM((nn, 8, 128), F32),
        dma((7,)), dma((ntile,)),
        dma((na,)), dma((na,)),
        dma((2, nt, 1 + nqy)), dma((nt, 1 + nqy)),
        dma((nt, nqy - 1 + nx1)), dma((nt, nqy - 1 + nx1)),
        dma((nt,)), dma((nt,)),
        dma((2 * nt,)), dma((2 * nt,)),
        dma((nt, nx1 + nqy - 1)), dma((nt, nx1 + nqy - 1)),
        dma((nt, na)), dma((nt, na)),
        dma((nt - 1,)), dma((nt - 1,)),
        dma((nn,)), dma((nn,)),
        dma((na,)), dma((na,)),
        dma((nw2 + 1,)), dma((nw2 + 1,)),
    ]
    input_grad, new_weight, new_first, new_second = pl.pallas_call(
        functools.partial(kernel, ndp, nt, nqx),
        out_shape=(
            pltpu.VMEM((tokens, width), BF16),
            pltpu.VMEM((nq, 2 * rows, cols), BF16),
            pltpu.VMEM((rows, cols), F32),
            pltpu.VMEM((rows, cols), F32),
        ),
        in_specs=[any_spec] * 8,
        out_specs=(vmem, vmem, vmem, vmem),
        scratch_shapes=scratch,
        compiler_params=pltpu.CompilerParams(
            collective_id=0, has_side_effects=True, vmem_limit_bytes=48 * 2**20
        ),
    )(
        norm_input, key_grad, positions.reshape(ntile, tile), norm_gain.reshape(width // 128, 128),
        jnp.asarray(frequency), key_weight, first_moment, second_moment,
    )
    return (input_grad, new_weight.reshape(features, cols), new_first, new_second)


def solution(mesh):
    in_specs = (
        P(("dp", "tensor"), None),
        P(("dp", "tensor"), None),
        P(("dp", "tensor")),
        P(),
        P("dp", "tensor"),
        P("dp", "tensor"),
        P("dp", "tensor"),
    )
    out_specs = (P(("dp", "tensor"), None), P(None, "tensor"), P("dp", "tensor"), P("dp", "tensor"))
    return jax.shard_map(
        functools.partial(body, mesh.shape["dp"], mesh.shape["tensor"]),
        mesh=mesh, in_specs=in_specs, out_specs=out_specs, check_vma=False,
    )
```

```python
import functools
import math

import jax
import jax.numpy as jnp
import numpy as np
from jax import lax
from jax.experimental import pallas as pl
from jax.experimental.pallas import tpu as pltpu
from jax.sharding import PartitionSpec as P

KV_HEADS = 4
HEAD = 128
ROPE_BASE = 500000.0

eps_norm = 1e-05
beta_one = 0.9
beta_two = 0.95
learn_rate = 0.0003
decay_rate = 0.1
eps_adam = 1e-08

MESH = pl.DeviceIdType.MESH
F32 = jnp.float32
BF16 = jnp.bfloat16


def kernel(
    ndp, nt, nqx, x_hbm, kg_hbm, pos_hbm, gain_hbm, freq_hbm, w_hbm, m1_hbm, m2_hbm,
    grad, nwb, nf, ns,
    x, kg, pos, gain_in, freq, m1, m2, gain, kb, kbt, sks, ssq, cross,
    wf, wg, rcore, r1a, r1b, r2a, r2b, zs, rz, gsum, nsend, nrecv,
    isem, xsem, a1s, a1r, zfs, zfr, b3s, b3r, a3s, a3r, cs, cr, qs, qr, q2s, q2r,
    zsd, zr, nss, nsr, ws, wr, vs, vr, us, ur,
):
    nq = ndp // 2
    nqy = nq // nqx
    rows, cols = w_hbm.shape
    half = nq * rows
    tokens, width = x.shape
    tile = min(128, tokens)
    ntile = tokens // tile
    hc = cols // 2
    cc = min(512, hc)
    hcol = (pl.ds(0, hc), pl.ds(hc, hc))
    dp = lax.axis_index("dp")
    t = lax.axis_index("tensor")
    c = dp % 2
    q = dp // 2
    qy = q // nqx
    qx = q % nqx
    mate = q * 2 + (1 - c)
    mine = pl.multiple_of(c * half, half)
    theirs = pl.multiple_of((1 - c) * half, half)
    sends = []

    def describe(src, dst, ssem, rsem, dev):
        return pltpu.make_async_remote_copy(
            src_ref=src, dst_ref=dst, send_sem=ssem, recv_sem=rsem, device_id=dev, device_id_type=MESH
        )

    def remote(src, dst, ssem, rsem, dev):
        copy = describe(src, dst, ssem, rsem, dev)
        copy.start()
        sends.append((None, copy))
        return copy

    def pos_x(k):
        return (qx + k) % nqx

    def pos_y(k):
        return (qy + k) % nqy

    def dev_x(k):
        return ((qy * nqx + pos_x(k)) * 2 + c, t)

    def dev_y(k):
        return ((pos_y(k) * nqx + qx) * 2 + c, t)

    def slot(yy, xx):
        return pl.ds(pl.multiple_of(mine + (yy * nqx + xx) * rows, rows), rows)

    def band(yy):
        return pl.ds(pl.multiple_of(mine + yy * nqx * rows, nqx * rows), nqx * rows)

    my_rows = slot(qy, qx)
    steps = sorted(range(1, nt), key=lambda o: (-min(o, nt - o), o)) + [0]

    def dest(i):
        return (t + steps[i]) % nt

    near = jnp.minimum(t, nt - 1 - t)
    low = t < nt - 1 - t

    def block(i):
        if i == 0:
            return t
        d = (i + 1) // 2
        both = t - d if i % 2 else t + d
        return jnp.where(i <= 2 * near, both, jnp.where(low, i, nt - 1 - i))

    def local(src, dst, sem):
        copy = pltpu.make_async_copy(src, dst, sem)
        copy.start()
        return copy

    own = local(w_hbm, wf.at[t, my_rows], isem.at[0])
    kg_in = local(kg_hbm, kg, isem.at[1])
    pos_in = local(pos_hbm, pos, isem.at[2])
    freq_in = local(freq_hbm, freq, isem.at[3])
    x_in = []
    for k in range(ntile):
        piece = pl.ds(k * tile, tile)
        x_in.append(local(x_hbm.at[piece], x.at[piece], xsem.at[k]))
    gain_copy = local(gain_hbm, gain_in, isem.at[4])
    m1_in = local(m1_hbm, m1, isem.at[5])
    m2_in = local(m2_hbm, m2, isem.at[6])

    barrier = pltpu.get_barrier_semaphore()
    for k in range(1, ndp):
        pl.semaphore_signal(barrier, inc=1, device_id=((dp + k) % ndp, t), device_id_type=MESH)
    for k in range(1, nt):
        pl.semaphore_signal(barrier, inc=1, device_id=(dp, (t + k) % nt), device_id_type=MESH)
    cross[...] = jnp.zeros_like(cross)
    kg_in.wait()
    pos_in.wait()
    freq_in.wait()
    hh = HEAD // 2
    turn = jnp.broadcast_to(freq[...], (128, 128)).T[:hh, :tile]
    for k in range(ntile):
        lanes = pl.ds(k * tile, tile)
        angle = turn * pos[k : k + 1, :].astype(F32)
        cosine = jnp.cos(angle)
        sine = jnp.sin(angle)
        turned = kg[pl.ds(k * tile, tile), :].astype(F32).T
        for h in range(KV_HEADS):
            a = turned[h * HEAD : h * HEAD + hh]
            b = turned[h * HEAD + hh : (h + 1) * HEAD]
            for p, value in enumerate((a * cosine + b * sine, b * cosine - a * sine)):
                value = value.astype(BF16)
                for m in range(hh // rows):
                    n = (h * HEAD + p * hh) // rows + m
                    kbt[pl.ds((n % 2) * half + (n // 2) * rows, rows), lanes] = value[
                        m * rows : (m + 1) * rows
                    ]

    pl.semaphore_wait(barrier, ndp - 1 + nt - 1)

    na = nqx + nqy - 2
    first = [
        remote(w_hbm.at[:, hcol[0]], wf.at[t, my_rows, hcol[0]], a1s.at[k - 1], a1r.at[k - 1], dev_x(k))
        for k in range(1, nqx)
    ]
    first += [
        remote(
            w_hbm.at[:, hcol[1]], wf.at[t, my_rows, hcol[1]],
            a1s.at[nqx + k - 2], a1r.at[nqx + k - 2], dev_y(k),
        )
        for k in range(1, nqy)
    ]

    nb = nqx * (nqy - 1) + (nqx - 1) * nqy
    spread_copies = {}

    def spread(i, near=(False, True)):
        b = block(i)
        batch = spread_copies.setdefault(i, [])
        n = 0
        for h, count, other, dev in ((0, nqx, nqy, dev_y), (1, nqy, nqx, dev_x)):
            for k in range(1, other):
                for m in range(count):
                    place = slot(qy, pos_x(m)) if h == 0 else slot(pos_y(m), qx)
                    if (m == 0) in near:
                        part = wf.at[b, place, hcol[h]]
                        src = w_hbm.at[:, hcol[h]] if i == 0 and m == 0 else part
                        batch.append(remote(src, part, b3s.at[i, n], b3r.at[i, n], dev(k)))
                    n += 1

    spread(0, (True,))

    def line_pieces(b, side, p, dev):
        if p == 0:
            parts = [wf.at[b, my_rows]]
        else:
            parts = [wf.at[b, slot(qy, pos_x(k)), hcol[0]] for k in range(1, nqx)]
            parts += [wf.at[b, slot(pos_y(k), qx), hcol[1]] for k in range(1, nqy)]
        return [
            describe(part, part, zfs.at[side, b, p + n], zfr.at[b, p + n], dev)
            for n, part in enumerate(parts)
        ]

    def pass_on(b, side, p):
        to, there = (t + 1, t + 1 < nt) if side == 0 else (t - 1, t >= 1)

        @pl.when(there)
        def _():
            for copy in line_pieces(b, side, p, (dp, to)):
                copy.start()

    line_sent = [(0, t, t >= 0), (1, t, t >= 0)]

    def relay(d, p):
        for side, b, here in ((0, t - d, t - d >= 0), (1, t + d, t + d < nt)):
            @pl.when(here)
            def _(side=side, b=b):
                for copy in line_pieces(b, side, p, (dp, t)):
                    copy.wait_recv()
                pass_on(b, side, p)

            if p == 0:
                line_sent.append((side, b, here))

    for side, to, there in ((0, t + 1, t + 1 < nt), (1, t - 1, t >= 1)):
        @pl.when(there)
        def _(side=side, to=to):
            describe(w_hbm, wf.at[t, my_rows], zfs.at[side, t, 0], zfr.at[t, 0], (dp, to)).start()

    third = {}

    def gather_third(i):
        for copy in spread_copies[i]:
            copy.wait_recv()
        part = wf.at[block(i), pl.ds(mine, half)]
        third[i] = remote(part, part, a3s.at[i], a3r.at[i], (mate, t))

    def sum_squares(k):
        x_in[k].wait()

        @pl.loop(0, tile // 16)
        def _(g):
            r = pl.ds(pl.multiple_of(k * tile + g * 16, 16), 16)
            total = None
            for b in range(width // 512):
                v = x[r, b * 512 : (b + 1) * 512].astype(F32)
                v = v * v
                v = (v[:, :128] + v[:, 128:256]) + (v[:, 256:384] + v[:, 384:])
                total = v if total is None else total + v
            ssq[r, :] = total

        lanes = pl.ds(k * tile, tile)
        mean = jnp.sum(ssq[lanes, :].T, axis=0, keepdims=True) / width
        sks[:, lanes] = (kbt[:, lanes].astype(F32) * lax.rsqrt(mean + eps_norm)).astype(BF16)

    for k in range(ntile):
        sum_squares(k)

    gain_copy.wait()
    for k in range(width // 128):
        gain[:, k * 128 : (k + 1) * 128] = gain_in[k : k + 1, :].astype(F32)

    core_copies = {}

    def product(i, h):
        j = dest(i)

        @pl.loop(0, hc // cc)
        def _(n):
            off = pl.ds(pl.multiple_of(h * hc + n * cc, cc), cc)
            col = pl.ds(pl.multiple_of(j * cols + h * hc + n * cc, cc), cc)
            total = jnp.dot(sks[...], x[:, col], preferred_element_type=F32)
            wg[j, :, off] = (total * gain[:, col]).astype(BF16)

        n = i * 2 + h
        core_copies[n] = remote(
            wg.at[j, pl.ds(theirs, half), hcol[h]], rcore.at[j, :, hcol[h]], cs.at[n], cr.at[n], (mate, t)
        )

    def pair_sum(i, h):
        j = dest(i)
        core_copies[i * 2 + h].wait_recv()

        @pl.loop(0, half // 16)
        def _(g):
            r = pl.ds(pl.multiple_of(mine + g * 16, 16), 16)
            l = pl.ds(pl.multiple_of(g * 16, 16), 16)
            a = wg[j, r, hcol[h]].astype(F32) + rcore[j, l, hcol[h]].astype(F32)
            wg[j, r, hcol[h]] = a.astype(BF16)

    nx1 = (nqx - 1) * nqy
    q_copies = {}
    q2_copies = {}

    def reduce_first(i, h):
        j = dest(i)
        batch = []
        if h == 0:
            for k in range(1, nqx):
                for yy in range(nqy):
                    n = (k - 1) * nqy + yy
                    src = wg.at[j, slot(yy, pos_x(k)), hcol[0]]
                    batch.append(remote(src, r1a.at[i, n], qs.at[i, n], qr.at[i, n], dev_x(k)))
        else:
            for k in range(1, nqy):
                n = nx1 + k - 1
                src = wg.at[j, band(pos_y(k)), hcol[1]]
                batch.append(remote(src, r1b.at[i, k - 1], qs.at[i, n], qr.at[i, n], dev_y(k)))
        q_copies[i, h] = batch

    def middle(i, h):
        j = dest(i)
        for copy in q_copies[i, h]:
            copy.wait_recv()
        batch = []
        if h == 0:
            @pl.loop(0, rows // 16)
            def _(g):
                l = pl.ds(pl.multiple_of(g * 16, 16), 16)
                for yy in range(nqy):
                    r = pl.ds(pl.multiple_of(mine + (yy * nqx + qx) * rows + g * 16, 16), 16)
                    a = wg[j, r, hcol[0]].astype(F32)
                    for k in range(nqx - 1):
                        a = a + r1a[i, k * nqy + yy, l, :].astype(F32)
                    wg[j, r, hcol[0]] = a.astype(BF16)

            for k in range(1, nqy):
                n = k - 1
                src = wg.at[j, slot(pos_y(k), qx), hcol[0]]
                batch.append(remote(src, r2a.at[i, k - 1], q2s.at[i, n], q2r.at[i, n], dev_y(k)))
        else:
            @pl.loop(0, nqx * rows // 16)
            def _(g):
                l = pl.ds(pl.multiple_of(g * 16, 16), 16)
                r = pl.ds(pl.multiple_of(mine + qy * nqx * rows + g * 16, 16), 16)
                a = wg[j, r, hcol[1]].astype(F32)
                for k in range(nqy - 1):
                    a = a + r1b[i, k, l, :].astype(F32)
                wg[j, r, hcol[1]] = a.astype(BF16)

            for k in range(1, nqx):
                n = nqy - 1 + k - 1
                src = wg.at[j, slot(qy, pos_x(k)), hcol[1]]
                batch.append(remote(src, r2b.at[i, k - 1], q2s.at[i, n], q2r.at[i, n], dev_x(k)))
        q2_copies[i, h] = batch

    z_copies = []

    def final(i):
        j = dest(i)
        for h in range(2):
            for copy in q2_copies[i, h]:
                copy.wait_recv()

        @pl.loop(0, rows // 16)
        def _(g):
            r = pl.ds(pl.multiple_of(g * 16, 16), 16)
            m = pl.ds(pl.multiple_of(mine + q * rows + g * 16, 16), 16)
            for part, other, count in ((hcol[0], r2a, nqy - 1), (hcol[1], r2b, nqx - 1)):
                a = wg[j, m, part].astype(F32)
                for k in range(count):
                    a = a + other[i, k, r, :].astype(F32)
                if i < nt - 1:
                    zs[i, r, part] = a.astype(BF16)
                else:
                    gsum[r, part] = a

        if i < nt - 1:
            z_copies.append(remote(zs.at[i], rz.at[i], zsd.at[i], zr.at[i], (dp, j)))

    uc = min(256, cols)

    def upstream(i):
        b = block(i)
        third[i].wait_recv()

        @pl.loop(0, cols // uc)
        def _(h):
            off = pl.ds(pl.multiple_of(h * uc, uc), uc)
            col = pl.ds(pl.multiple_of(b * cols + h * uc, uc), uc)
            u = jnp.dot(kb[...], wf[b, :, off], preferred_element_type=F32) * gain[:, col]
            scale = ssq[...]
            u = jnp.concatenate([u[:, n * 128 : (n + 1) * 128] * scale for n in range(uc // 128)], axis=1)
            grad[:, col] = u.astype(BF16)
            p = u * x[:, col].astype(F32)
            total = p[:, :128]
            for n in range(1, uc // 128):
                total = total + p[:, n * 128 : (n + 1) * 128]
            cross[...] += total

    def turn_back():
        for k in range(ntile):
            lanes = pl.ds(k * tile, tile)
            kb[lanes, :] = kbt[:, lanes].astype(F32).T.astype(BF16)
            mean = jnp.sum(ssq[lanes, :], axis=1, keepdims=True) / width
            ssq[lanes, :] = jnp.broadcast_to(lax.rsqrt(mean + eps_norm), (tile, 128))

    units = [(i, h) for i in range(nt) for h in range(2)]
    early = min(4, len(units))
    for n, unit in enumerate(units):
        product(*unit)
        if n == 1:
            own.wait()
            for copy in first:
                copy.wait_recv()
            pass_on(t, 0, 1)
            pass_on(t, 1, 1)
        if n == len(units) - 1:
            relay(1, 1)
        if n > 0:
            pair_sum(*units[n - 1])
            if n <= early:
                reduce_first(*units[n - 1])
        if n == early:
            relay(1, 0)
    pair_sum(*units[-1])
    turn_back()

    def both_middle(i):
        middle(i, 0)
        middle(i, 1)
        if i + 2 < nt:
            reduce_first(i + 2, 0)
            reduce_first(i + 2, 1)

    both_middle(0)
    both_middle(1)
    final(0)
    for i in range(2, nt):
        both_middle(i)
        if i == nt - 1:
            spread(0, (False,))
            spread(1)
        final(i - 1)
        if i > 2:
            relay(i - 1, 0)
            if i < nt - 1:
                relay(i - 1, 1)
    final(nt - 1)
    for copy in z_copies:
        copy.wait_recv()

    nsend[0] = jnp.zeros((8, 128), F32)

    @pl.loop(0, rows // 16)
    def _(g):
        r = pl.ds(pl.multiple_of(g * 16, 16), 16)
        a = gsum[r, :]
        for i in range(nt - 1):
            a = a + rz[i, r, :].astype(F32)
        gsum[r, :] = a
        a = a * a
        a = a[:8] + a[8:]
        total = a[:, :128]
        for k in range(1, cols // 128):
            total = total + a[:, k * 128 : (k + 1) * 128]
        nsend[0] += total

    v = nsend[0]
    base = 0
    groups = (
        [((dp + k) % ndp, t) for k in range(1, ndp)],
        [(dp, (t + k) % nt) for k in range(1, nt)],
    )
    for step, devs in enumerate(groups):
        if step > 0:
            nsend[step] = v
        batch = [
            remote(nsend.at[step], nrecv.at[base + n], nss.at[base + n], nsr.at[base + n], dev)
            for n, dev in enumerate(devs)
        ]
        if step == 0:
            if nt > 2:
                relay(nt - 2, 1)
            for i in range(2, nt - 1):
                spread(i)
            gather_third(0)
        else:
            upstream(0)
            gather_third(1)
            relay(nt - 1, 0)
            relay(nt - 1, 1)
            spread(nt - 1)
        for n, copy in enumerate(batch):
            copy.wait_recv()
            v = v + nrecv[base + n]
        base += len(devs)
    total_square = jnp.sum(jnp.sum(v, axis=1, keepdims=True), axis=0, keepdims=True)
    limit = math.sqrt(kbt.shape[0] * width)
    clip = jnp.minimum(1.0, limit / (jnp.sqrt(total_square) + 1e-06))
    nat = pl.multiple_of(c * rows, rows)
    m1_in.wait()
    m2_in.wait()

    @pl.loop(0, rows // 16)
    def _(g):
        r = pl.ds(pl.multiple_of(g * 16, 16), 16)
        wr_ = pl.ds(pl.multiple_of(mine + q * rows + g * 16, 16), 16)
        clipped = gsum[r, :] * clip
        new_first = beta_one * m1[r, :] + (1.0 - beta_one) * clipped
        new_second = beta_two * m2[r, :] + (1.0 - beta_two) * clipped * clipped
        nf[r, :] = new_first
        ns[r, :] = new_second
        nwb[q, pl.ds(pl.multiple_of(nat + g * 16, 16), 16), :] = (
            wf[t, wr_, :].astype(F32) * (1.0 - learn_rate * decay_rate)
            - learn_rate * new_first / (jnp.sqrt(new_second) + eps_adam)
        ).astype(BF16)

    def piece_of(yy, xx, part):
        return nwb.at[yy * nqx + xx, pl.ds(nat, rows), part]

    w_first = []
    for k in range(1, nqx):
        part = piece_of(qy, qx, hcol[0])
        w_first.append(remote(part, part, ws.at[k - 1], wr.at[k - 1], dev_x(k)))
    for k in range(1, nqy):
        n = nqx - 1 + k - 1
        part = piece_of(qy, qx, hcol[1])
        w_first.append(remote(part, part, ws.at[n], wr.at[n], dev_y(k)))

    for i in range(1, nt - 1):
        gather_third(i + 1)
        upstream(i)

    for copy in w_first:
        copy.wait_recv()
    w_second = []
    for k in range(1, nqy):
        for xx in range(nqx):
            part = piece_of(qy, xx, hcol[0])
            n = len(w_second)
            w_second.append(remote(part, part, vs.at[n], vr.at[n], dev_y(k)))
    for k in range(1, nqx):
        for yy in range(nqy):
            part = piece_of(yy, qx, hcol[1])
            n = len(w_second)
            w_second.append(remote(part, part, vs.at[n], vr.at[n], dev_x(k)))
    nw1 = len(w_second)
    lasts = [
        remote(part, part, us.at[n], ur.at[n], (mate, t))
        for n, part in enumerate(
            [piece_of(qy, pos_x(m), hcol[0]) for m in range(nqx)]
            + [piece_of(pos_y(m), qx, hcol[1]) for m in range(nqy)]
        )
    ]
    upstream(nt - 1)

    for k in range(ntile):
        lanes = pl.ds(k * tile, tile)
        down = ssq[lanes, :1] * (jnp.sum(cross[lanes, :], axis=1, keepdims=True) / width)
        cross[lanes, :] = jnp.broadcast_to(down, (tile, 128))

    def finish(a, b):
        @pl.loop(a // 16, b // 16)
        def _(g):
            r = pl.ds(pl.multiple_of(g * 16, 16), 16)
            down = cross[r, :]
            for n in range(width // 128):
                col = slice(n * 128, (n + 1) * 128)
                grad[r, col] = (grad[r, col].astype(F32) - down * x[r, col].astype(F32)).astype(BF16)

    finish(0, tokens // 2)
    for copy in w_second:
        copy.wait_recv()
    lasts += [
        remote(part, part, vs.at[nw1 + n], vr.at[nw1 + n], (mate, t))
        for n, part in enumerate(
            [piece_of(pos_y(k), pos_x(m), hcol[0]) for k in range(1, nqy) for m in range(nqx)]
            + [piece_of(pos_y(m), pos_x(k), hcol[1]) for k in range(1, nqx) for m in range(nqy)]
        )
    ]
    finish(tokens // 2, tokens)
    for copy in lasts:
        copy.wait_recv()
    for _, sent in sends:
        sent.wait_send()
    for side, b, here in line_sent:
        there = t + 1 < nt if side == 0 else t >= 1

        @pl.when(jnp.logical_and(here, there))
        def _(side=side, b=b):
            for p in range(2):
                for copy in line_pieces(b, side, p, (dp, t)):
                    copy.wait_send()


def write_out(a, b, c, d, a_out, b_out, c_out, d_out, sem):
    copies = [
        pltpu.make_async_copy(src, dst, sem.at[n])
        for n, (src, dst) in enumerate(((a, a_out), (b, b_out), (c, c_out), (d, d_out)))
    ]
    for copy in copies:
        copy.start()
    for copy in copies:
        copy.wait()


def body(ndp, nt, norm_input, key_grad, positions, norm_gain, key_weight, first_moment, second_moment):
    rows, cols = key_weight.shape
    tokens, width = norm_input.shape
    nq = ndp // 2
    features = ndp * rows
    tile = min(128, tokens)
    ntile = tokens // tile
    hh = HEAD // 2
    frequency = ROPE_BASE ** (-(2.0 * np.arange(hh)) / HEAD)
    frequency = np.resize(frequency.astype(np.float32), (1, 128))
    any_spec = pl.BlockSpec(memory_space=pl.ANY)
    vmem = pl.BlockSpec(memory_space=pltpu.VMEM)
    dma = pltpu.SemaphoreType.DMA
    nqx = math.isqrt(nq)
    while nq % nqx:
        nqx -= 1
    nqy = nq // nqx
    hc = cols // 2
    na = nqx + nqy - 2
    nx1 = (nqx - 1) * nqy
    nw2 = nx1 + (nqy - 1) * nqx
    nn = ndp - 1 + nt - 1
    scratch = [
        pltpu.VMEM((tokens, width), BF16),
        pltpu.VMEM((tokens, features), BF16),
        pltpu.VMEM((ntile, tile), jnp.int32),
        pltpu.VMEM((width // 128, 128), BF16),
        pltpu.VMEM((1, 128), F32),
        pltpu.VMEM((rows, cols), F32),
        pltpu.VMEM((rows, cols), F32),
        pltpu.VMEM((1, width), F32),
        pltpu.VMEM((tokens, features), BF16),
        pltpu.VMEM((features, tokens), BF16),
        pltpu.VMEM((features, tokens), BF16),
        pltpu.VMEM((tokens, 128), F32),
        pltpu.VMEM((tokens, 128), F32),
        pltpu.VMEM((nt, features, cols), BF16),
        pltpu.VMEM((nt, features, cols), BF16),
        pltpu.VMEM((nt, nq * rows, cols), BF16),
        pltpu.VMEM((nt, nx1, rows, hc), BF16),
        pltpu.VMEM((nt, nqy - 1, nqx * rows, hc), BF16),
        pltpu.VMEM((nt, nqy - 1, rows, hc), BF16),
        pltpu.VMEM((nt, nqx - 1, rows, hc), BF16),
        pltpu.VMEM((nt - 1, rows, cols), BF16),
        pltpu.VMEM((nt - 1, rows, cols), BF16),
        pltpu.VMEM((rows, cols), F32),
        pltpu.VMEM((2, 8, 128), F32),
        pltpu.VMEM((nn, 8, 128), F32),
        dma((7,)), dma((ntile,)),
        dma((na,)), dma((na,)),
        dma((2, nt, 1 + na)), dma((nt, 1 + na)),
        dma((nt, nw2)), dma((nt, nw2)),
        dma((nt,)), dma((nt,)),
        dma((2 * nt,)), dma((2 * nt,)),
        dma((nt, nx1 + nqy - 1)), dma((nt, nx1 + nqy - 1)),
        dma((nt, na)), dma((nt, na)),
        dma((nt - 1,)), dma((nt - 1,)),
        dma((nn,)), dma((nn,)),
        dma((na,)), dma((na,)),
        dma((2 * nw2,)), dma((2 * nw2,)),
        dma((nqx + nqy,)), dma((nqx + nqy,)),
    ]
    results = pl.pallas_call(
        functools.partial(kernel, ndp, nt, nqx),
        out_shape=(
            pltpu.VMEM((tokens, width), BF16),
            pltpu.VMEM((nq, 2 * rows, cols), BF16),
            pltpu.VMEM((rows, cols), F32),
            pltpu.VMEM((rows, cols), F32),
        ),
        in_specs=[any_spec] * 8,
        out_specs=(vmem, vmem, vmem, vmem),
        scratch_shapes=scratch,
        compiler_params=pltpu.CompilerParams(
            collective_id=0, has_side_effects=True, vmem_limit_bytes=48 * 2**20
        ),
    )(
        norm_input, key_grad, positions.reshape(ntile, tile), norm_gain.reshape(width // 128, 128),
        jnp.asarray(frequency), key_weight, first_moment, second_moment,
    )
    results = [pltpu.with_memory_space_constraint(r, pltpu.VMEM) for r in results]
    input_grad, new_weight, new_first, new_second = pl.pallas_call(
        write_out,
        out_shape=[jax.ShapeDtypeStruct(r.shape, r.dtype) for r in results],
        in_specs=[vmem] * 4,
        out_specs=[any_spec] * 4,
        scratch_shapes=[dma((4,))],
        compiler_params=pltpu.CompilerParams(vmem_limit_bytes=2**20),
    )(*results)
    return (input_grad, new_weight.reshape(features, cols), new_first, new_second)


def solution(mesh):
    in_specs = (
        P(("dp", "tensor"), None),
        P(("dp", "tensor"), None),
        P(("dp", "tensor")),
        P(),
        P("dp", "tensor"),
        P("dp", "tensor"),
        P("dp", "tensor"),
    )
    out_specs = (P(("dp", "tensor"), None), P(None, "tensor"), P("dp", "tensor"), P("dp", "tensor"))
    return jax.shard_map(
        functools.partial(body, mesh.shape["dp"], mesh.shape["tensor"]),
        mesh=mesh, in_specs=in_specs, out_specs=out_specs, check_vma=False,
    )
```

```python
import functools
import math

import jax
import jax.numpy as jnp
import numpy as np
from jax import lax
from jax.experimental import pallas as pl
from jax.experimental.pallas import tpu as pltpu
from jax.sharding import PartitionSpec as P

KV_HEADS = 4
HEAD = 128
ROPE_BASE = 500000.0

eps_norm = 1e-05
beta_one = 0.9
beta_two = 0.95
learn_rate = 0.0003
decay_rate = 0.1
eps_adam = 1e-08

MESH = pl.DeviceIdType.MESH
F32 = jnp.float32
BF16 = jnp.bfloat16


def kernel(
    ndp, nt, nqx, x_hbm, kg_hbm, pos_hbm, gain_hbm, freq_hbm, w_hbm, m1_hbm, m2_hbm,
    grad, x, cross, nwb, nf, ns,
    kg, pos, gain_in, freq, m1, m2, gain, kb, kbt, sks, ssq,
    wf, wg, rcore, r1a, r1b, r2a, r2b, zs, rz, gsum, nsend, nrecv,
    isem, xsem, a1s, a1r, zfs, zfr, b3s, b3r, a3s, a3r, cs, cr, qs, qr, q2s, q2r,
    zsd, zr, nss, nsr, ws, wr, vs, vr, us, ur,
):
    nq = ndp // 2
    nqy = nq // nqx
    rows, cols = w_hbm.shape
    half = nq * rows
    tokens, width = x.shape
    tile = min(128, tokens)
    ntile = tokens // tile
    hc = cols // 2
    cc = min(512, hc)
    hcol = (pl.ds(0, hc), pl.ds(hc, hc))
    dp = lax.axis_index("dp")
    t = lax.axis_index("tensor")
    c = dp % 2
    q = dp // 2
    qy = q // nqx
    qx = q % nqx
    mate = q * 2 + (1 - c)
    mine = pl.multiple_of(c * half, half)
    theirs = pl.multiple_of((1 - c) * half, half)
    sent = []

    def describe(src, dst, ssem, rsem, dev):
        return pltpu.make_async_remote_copy(
            src_ref=src, dst_ref=dst, send_sem=ssem, recv_sem=rsem, device_id=dev, device_id_type=MESH
        )

    def remote(src, dst, ssem, rsem, dev):
        describe(src, dst, ssem, rsem, dev).start()

    def arrived(like, rsem):
        describe(like, like, a1s, rsem, (mate, t)).wait_recv()

    def left(like, ssem):
        describe(like, like, ssem, a1r, (mate, t)).wait_send()

    def chunks(n):
        return wg.at[0, pl.ds(0, n * rows), hcol[0]]

    def layers(n):
        return wg.at[:, pl.ds(0, n * rows), hcol[0]]

    def pos_x(k):
        return (qx + k) % nqx

    def pos_y(k):
        return (qy + k) % nqy

    def dev_x(k):
        return ((qy * nqx + pos_x(k)) * 2 + c, t)

    def dev_y(k):
        return ((pos_y(k) * nqx + qx) * 2 + c, t)

    def slot(yy, xx):
        return pl.ds(pl.multiple_of(mine + (yy * nqx + xx) * rows, rows), rows)

    def band(yy):
        return pl.ds(pl.multiple_of(mine + yy * nqx * rows, nqx * rows), nqx * rows)

    my_rows = slot(qy, qx)
    steps = sorted(range(1, nt), key=lambda o: (-min(o, nt - o), o)) + [0]

    def dest(i):
        return (t + steps[i]) % nt

    near = jnp.minimum(t, nt - 1 - t)
    low = t < nt - 1 - t

    def block(i):
        if i == 0:
            return t
        d = (i + 1) // 2
        both = t - d if i % 2 else t + d
        return jnp.where(i <= 2 * near, both, jnp.where(low, i, nt - 1 - i))

    def local(src, dst, sem):
        copy = pltpu.make_async_copy(src, dst, sem)
        copy.start()
        return copy

    own = local(w_hbm, wf.at[t, my_rows], isem.at[0])
    kg_in = local(kg_hbm, kg, isem.at[1])
    pos_in = local(pos_hbm, pos, isem.at[2])
    freq_in = local(freq_hbm, freq, isem.at[3])
    x_in = []
    for k in range(ntile):
        piece = pl.ds(k * tile, tile)
        x_in.append(local(x_hbm.at[piece], x.at[piece], xsem.at[k]))
    gain_copy = local(gain_hbm, gain_in, isem.at[4])
    m1_in = local(m1_hbm, m1, isem.at[5])
    m2_in = local(m2_hbm, m2, isem.at[6])

    barrier = pltpu.get_barrier_semaphore()
    for k in range(1, ndp):
        pl.semaphore_signal(barrier, inc=1, device_id=((dp + k) % ndp, t), device_id_type=MESH)
    for k in range(1, nt):
        pl.semaphore_signal(barrier, inc=1, device_id=(dp, (t + k) % nt), device_id_type=MESH)
    cross[...] = jnp.zeros_like(cross)
    kg_in.wait()
    pos_in.wait()
    freq_in.wait()
    hh = HEAD // 2
    turn = jnp.broadcast_to(freq[...], (128, 128)).T[:hh, :tile]
    for k in range(ntile):
        lanes = pl.ds(k * tile, tile)
        angle = turn * pos[k : k + 1, :].astype(F32)
        cosine = jnp.cos(angle)
        sine = jnp.sin(angle)
        turned = kg[pl.ds(k * tile, tile), :].astype(F32).T
        for h in range(KV_HEADS):
            a = turned[h * HEAD : h * HEAD + hh]
            b = turned[h * HEAD + hh : (h + 1) * HEAD]
            for p, value in enumerate((a * cosine + b * sine, b * cosine - a * sine)):
                value = value.astype(BF16)
                for m in range(hh // rows):
                    n = (h * HEAD + p * hh) // rows + m
                    kbt[pl.ds((n % 2) * half + (n // 2) * rows, rows), lanes] = value[
                        m * rows : (m + 1) * rows
                    ]

    pl.semaphore_wait(barrier, ndp - 1 + nt - 1)

    na = nqx + nqy - 2
    nx1 = (nqx - 1) * nqy
    ny1 = (nqy - 1) * nqx
    nw2 = nx1 + ny1
    for k in range(1, nqx):
        remote(w_hbm.at[:, hcol[0]], wf.at[t, my_rows, hcol[0]], a1s, a1r, dev_x(k))
    for k in range(1, nqy):
        remote(w_hbm.at[:, hcol[1]], wf.at[t, my_rows, hcol[1]], a1s, a1r, dev_y(k))
    sent.append((chunks(na), a1s))

    def spread(i, near=(False, True)):
        b = block(i)
        for h, count, other, dev in ((0, nqx, nqy, dev_y), (1, nqy, nqx, dev_x)):
            for k in range(1, other):
                for m in range(count):
                    place = slot(qy, pos_x(m)) if h == 0 else slot(pos_y(m), qx)
                    if (m == 0) in near:
                        part = wf.at[b, place, hcol[h]]
                        src = w_hbm.at[:, hcol[h]] if i == 0 and m == 0 else part
                        remote(src, part, b3s, b3r.at[i], dev(k))

    sent.append((layers(nw2), b3s))
    spread(0, (True,))

    def line_pieces(b, side, p, dev):
        if p == 0:
            parts = [wf.at[b, my_rows]]
        else:
            parts = [wf.at[b, slot(qy, pos_x(k)), hcol[0]] for k in range(1, nqx)]
            parts += [wf.at[b, slot(pos_y(k), qx), hcol[1]] for k in range(1, nqy)]
        return [describe(part, part, zfs.at[side, b], zfr.at[b, p], dev) for part in parts]

    def pass_on(b, side, p):
        to, there = (t + 1, t + 1 < nt) if side == 0 else (t - 1, t >= 1)

        @pl.when(there)
        def _():
            for copy in line_pieces(b, side, p, (dp, to)):
                copy.start()

    line_sent = [(0, t, t >= 0), (1, t, t >= 0)]

    def relay(d, p):
        for side, b, here in ((0, t - d, t - d >= 0), (1, t + d, t + d < nt)):
            @pl.when(here)
            def _(side=side, b=b):
                arrived(chunks(2 if p == 0 else na), zfr.at[b, p])
                pass_on(b, side, p)

            if p == 0:
                line_sent.append((side, b, here))

    for side, to, there in ((0, t + 1, t + 1 < nt), (1, t - 1, t >= 1)):
        @pl.when(there)
        def _(side=side, to=to):
            describe(w_hbm, wf.at[t, my_rows], zfs.at[side, t], zfr.at[t, 0], (dp, to)).start()

    def gather_third(i):
        arrived(chunks(nw2), b3r.at[i])
        part = wf.at[block(i), pl.ds(mine, half)]
        remote(part, part, a3s, a3r.at[i], (mate, t))

    sent.append((wg.at[:, pl.ds(0, half)], a3s))

    def sum_squares(k):
        x_in[k].wait()

        @pl.loop(0, tile // 16)
        def _(g):
            r = pl.ds(pl.multiple_of(k * tile + g * 16, 16), 16)
            total = None
            for b in range(width // 512):
                v = x[r, b * 512 : (b + 1) * 512].astype(F32)
                v = v * v
                v = (v[:, :128] + v[:, 128:256]) + (v[:, 256:384] + v[:, 384:])
                total = v if total is None else total + v
            ssq[r, :] = total

        lanes = pl.ds(k * tile, tile)
        mean = jnp.sum(ssq[lanes, :].T, axis=0, keepdims=True) / width
        sks[:, lanes] = (kbt[:, lanes].astype(F32) * lax.rsqrt(mean + eps_norm)).astype(BF16)

    for k in range(ntile):
        sum_squares(k)

    gain_copy.wait()
    for k in range(width // 128):
        gain[:, k * 128 : (k + 1) * 128] = gain_in[k : k + 1, :].astype(F32)

    sent.append((wg.at[:, pl.ds(0, half)], cs))

    def product(i, h):
        j = dest(i)

        @pl.loop(0, hc // cc)
        def _(n):
            off = pl.ds(pl.multiple_of(h * hc + n * cc, cc), cc)
            col = pl.ds(pl.multiple_of(j * cols + h * hc + n * cc, cc), cc)
            total = jnp.dot(sks[...], x[:, col], preferred_element_type=F32)
            wg[j, :, off] = (total * gain[:, col]).astype(BF16)

        n = i * 2 + h
        remote(wg.at[j, pl.ds(theirs, half), hcol[h]], rcore.at[j, :, hcol[h]], cs, cr.at[n], (mate, t))

    def pair_sum(i, h):
        j = dest(i)
        arrived(rcore.at[j, :, hcol[h]], cr.at[i * 2 + h])

        @pl.loop(0, half // 16)
        def _(g):
            r = pl.ds(pl.multiple_of(mine + g * 16, 16), 16)
            l = pl.ds(pl.multiple_of(g * 16, 16), 16)
            a = wg[j, r, hcol[h]].astype(F32) + rcore[j, l, hcol[h]].astype(F32)
            wg[j, r, hcol[h]] = a.astype(BF16)

    def reduce_first(i, h):
        j = dest(i)
        if h == 0:
            for k in range(1, nqx):
                for yy in range(nqy):
                    n = (k - 1) * nqy + yy
                    src = wg.at[j, slot(yy, pos_x(k)), hcol[0]]
                    remote(src, r1a.at[i, n], qs, qr.at[i, 0], dev_x(k))
        else:
            for k in range(1, nqy):
                src = wg.at[j, band(pos_y(k)), hcol[1]]
                remote(src, r1b.at[i, k - 1], qs, qr.at[i, 1], dev_y(k))

    sent.append((layers(nw2), qs))
    sent.append((layers(na), q2s))

    def middle(i, h):
        j = dest(i)
        arrived(chunks(ny1 if h else nx1), qr.at[i, h])
        if h == 0:
            @pl.loop(0, rows // 16)
            def _(g):
                l = pl.ds(pl.multiple_of(g * 16, 16), 16)
                for yy in range(nqy):
                    r = pl.ds(pl.multiple_of(mine + (yy * nqx + qx) * rows + g * 16, 16), 16)
                    a = wg[j, r, hcol[0]].astype(F32)
                    for k in range(nqx - 1):
                        a = a + r1a[i, k * nqy + yy, l, :].astype(F32)
                    wg[j, r, hcol[0]] = a.astype(BF16)

            for k in range(1, nqy):
                src = wg.at[j, slot(pos_y(k), qx), hcol[0]]
                remote(src, r2a.at[i, k - 1], q2s, q2r.at[i], dev_y(k))
        else:
            @pl.loop(0, nqx * rows // 16)
            def _(g):
                l = pl.ds(pl.multiple_of(g * 16, 16), 16)
                r = pl.ds(pl.multiple_of(mine + qy * nqx * rows + g * 16, 16), 16)
                a = wg[j, r, hcol[1]].astype(F32)
                for k in range(nqy - 1):
                    a = a + r1b[i, k, l, :].astype(F32)
                wg[j, r, hcol[1]] = a.astype(BF16)

            for k in range(1, nqx):
                src = wg.at[j, slot(qy, pos_x(k)), hcol[1]]
                remote(src, r2b.at[i, k - 1], q2s, q2r.at[i], dev_x(k))

    sent.append((zs, zsd))

    def final(i):
        j = dest(i)
        arrived(chunks(na), q2r.at[i])

        @pl.loop(0, rows // 16)
        def _(g):
            r = pl.ds(pl.multiple_of(g * 16, 16), 16)
            m = pl.ds(pl.multiple_of(mine + q * rows + g * 16, 16), 16)
            for part, other, count in ((hcol[0], r2a, nqy - 1), (hcol[1], r2b, nqx - 1)):
                a = wg[j, m, part].astype(F32)
                for k in range(count):
                    a = a + other[i, k, r, :].astype(F32)
                if i < nt - 1:
                    zs[i, r, part] = a.astype(BF16)
                else:
                    gsum[r, part] = a

        if i < nt - 1:
            remote(zs.at[i], rz.at[i], zsd, zr, (dp, j))

    uc = min(256, cols)

    def upstream(i):
        b = block(i)
        arrived(wf.at[b, pl.ds(mine, half)], a3r.at[i])

        @pl.loop(0, cols // uc)
        def _(h):
            off = pl.ds(pl.multiple_of(h * uc, uc), uc)
            col = pl.ds(pl.multiple_of(b * cols + h * uc, uc), uc)
            u = jnp.dot(kb[...], wf[b, :, off], preferred_element_type=F32) * gain[:, col]
            scale = ssq[...]
            u = jnp.concatenate([u[:, n * 128 : (n + 1) * 128] * scale for n in range(uc // 128)], axis=1)
            grad[:, col] = u.astype(BF16)
            p = u * x[:, col].astype(F32)
            total = p[:, :128]
            for n in range(1, uc // 128):
                total = total + p[:, n * 128 : (n + 1) * 128]
            cross[...] += total

    def turn_back():
        for k in range(ntile):
            lanes = pl.ds(k * tile, tile)
            kb[lanes, :] = kbt[:, lanes].astype(F32).T.astype(BF16)
            mean = jnp.sum(ssq[lanes, :], axis=1, keepdims=True) / width
            ssq[lanes, :] = jnp.broadcast_to(lax.rsqrt(mean + eps_norm), (tile, 128))

    units = [(i, h) for i in range(nt) for h in range(2)]
    early = min(4, len(units))
    for n, unit in enumerate(units):
        product(*unit)
        if n == len(units) - 1:
            relay(1, 1)
        if n > 0:
            pair_sum(*units[n - 1])
            if n <= early:
                reduce_first(*units[n - 1])
        if n == 2:
            own.wait()
            arrived(chunks(na), a1r)
            pass_on(t, 0, 1)
            pass_on(t, 1, 1)
        if n == early:
            relay(1, 0)
    pair_sum(*units[-1])
    turn_back()

    def both_middle(i):
        middle(i, 0)
        middle(i, 1)
        if i + 2 < nt:
            reduce_first(i + 2, 0)
            reduce_first(i + 2, 1)

    both_middle(0)
    both_middle(1)
    final(0)
    if nt > 3:
        relay(2, 0)
    for i in range(2, nt):
        both_middle(i)
        if i == nt - 1:
            spread(0, (False,))
            spread(1)
        final(i - 1)
        if i > 2:
            relay(i - 1, 1)
            if i < nt - 1:
                relay(i, 0)
    final(nt - 1)
    arrived(rz, zr)

    nsend[0] = jnp.zeros((8, 128), F32)

    @pl.loop(0, rows // 16)
    def _(g):
        r = pl.ds(pl.multiple_of(g * 16, 16), 16)
        a = gsum[r, :]
        for i in range(nt - 1):
            a = a + rz[i, r, :].astype(F32)
        gsum[r, :] = a
        a = a * a
        a = a[:8] + a[8:]
        total = a[:, :128]
        for k in range(1, cols // 128):
            total = total + a[:, k * 128 : (k + 1) * 128]
        nsend[0] += total

    v = nsend[0]
    base = 0
    groups = (
        [((dp + k) % ndp, t) for k in range(1, ndp)],
        [(dp, (t + k) % nt) for k in range(1, nt)],
    )
    for step, devs in enumerate(groups):
        if step > 0:
            nsend[step] = v
        for n, dev in enumerate(devs):
            remote(nsend.at[step], nrecv.at[base + n], nss.at[step], nsr.at[step], dev)
        batch = nrecv.at[pl.ds(base, len(devs))]
        sent.append((batch, nss.at[step]))
        if step == 0:
            for i in range(2, nt - 1):
                spread(i)
            gather_third(0)
        else:
            upstream(0)
            gather_third(1)
            relay(nt - 1, 0)
            relay(nt - 1, 1)
            spread(nt - 1, (True,))
        arrived(batch, nsr.at[step])
        for n in range(len(devs)):
            v = v + nrecv[base + n]
        base += len(devs)
    total_square = jnp.sum(jnp.sum(v, axis=1, keepdims=True), axis=0, keepdims=True)
    limit = math.sqrt(kbt.shape[0] * width)
    clip = jnp.minimum(1.0, limit / (jnp.sqrt(total_square) + 1e-06))
    nat = pl.multiple_of(c * rows, rows)
    m1_in.wait()
    m2_in.wait()

    @pl.loop(0, rows // 16)
    def _(g):
        r = pl.ds(pl.multiple_of(g * 16, 16), 16)
        wr_ = pl.ds(pl.multiple_of(mine + q * rows + g * 16, 16), 16)
        clipped = gsum[r, :] * clip
        new_first = beta_one * m1[r, :] + (1.0 - beta_one) * clipped
        new_second = beta_two * m2[r, :] + (1.0 - beta_two) * clipped * clipped
        nf[r, :] = new_first
        ns[r, :] = new_second
        nwb[q, pl.ds(pl.multiple_of(nat + g * 16, 16), 16), :] = (
            wf[t, wr_, :].astype(F32) * (1.0 - learn_rate * decay_rate)
            - learn_rate * new_first / (jnp.sqrt(new_second) + eps_adam)
        ).astype(BF16)

    def piece_of(yy, xx, part):
        return nwb.at[yy * nqx + xx, pl.ds(nat, rows), part]

    for k in range(1, nqx):
        part = piece_of(qy, qx, hcol[0])
        remote(part, part, ws, wr, dev_x(k))
    for k in range(1, nqy):
        part = piece_of(qy, qx, hcol[1])
        remote(part, part, ws, wr, dev_y(k))
    sent.append((chunks(na), ws))

    spread(nt - 1, (False,))
    for i in range(1, nt - 1):
        if i < nt - 2:
            gather_third(i + 1)
        upstream(i)

    arrived(chunks(na), wr)
    for m in range(max(nqx, nqy)):
        for k in range(1, nqy if m < nqx else 1):
            part = piece_of(qy, pos_x(m), hcol[0])
            remote(part, part, vs, vr, dev_y(k))
        for k in range(1, nqx if m < nqy else 1):
            part = piece_of(pos_y(m), qx, hcol[1])
            remote(part, part, vs, vr, dev_x(k))
    sent.append((chunks(nw2), vs))
    gather_third(nt - 1)
    early_parts = [(qy, pos_x(m), hcol[0]) for m in range(nqx)] + [(pos_y(m), qx, hcol[1]) for m in range(nqy)]
    for place in early_parts:
        part = piece_of(*place)
        remote(part, part, us, ur, (mate, t))
    upstream(nt - 1)

    for k in range(ntile):
        lanes = pl.ds(k * tile, tile)
        down = ssq[lanes, :1] * (jnp.sum(cross[lanes, :], axis=1, keepdims=True) / width)
        cross[lanes, :] = jnp.broadcast_to(down, (tile, 128))

    arrived(chunks(nw2), vr)
    late_parts = [(pos_y(k), pos_x(m), hcol[0]) for k in range(1, nqy) for m in range(nqx)]
    late_parts += [(pos_y(m), pos_x(k), hcol[1]) for k in range(1, nqx) for m in range(nqy)]
    for place in late_parts:
        part = piece_of(*place)
        remote(part, part, us, ur, (mate, t))
    whole = nwb.at[:, pl.ds(nat, rows)]
    sent.append((whole, us))
    arrived(whole, ur)
    for like, sem in sent:
        left(like, sem)
    for side, b, here in line_sent:
        there = t + 1 < nt if side == 0 else t >= 1

        @pl.when(jnp.logical_and(here, there))
        def _(side=side, b=b):
            left(chunks(2 + na), zfs.at[side, b])


def write_out(grad, x, down, nwb, nf, ns, grad_out, nw_out, nf_out, ns_out, done, sem, gsem):
    tokens, width = x.shape
    tile = min(32, tokens)
    small = [
        pltpu.make_async_copy(src, dst, sem.at[n])
        for n, (src, dst) in enumerate(((nwb, nw_out), (nf, nf_out), (ns, ns_out)))
    ]
    copies = list(small)
    for k in range(tokens // tile):
        if k == 1:
            for copy in small:
                copy.start()

        @pl.loop(0, tile // 16)
        def _(g):
            r = pl.ds(pl.multiple_of(k * tile + g * 16, 16), 16)
            factor = down[r, :]
            for n in range(width // 128):
                col = slice(n * 128, (n + 1) * 128)
                done[r, col] = (grad[r, col].astype(F32) - factor * x[r, col].astype(F32)).astype(BF16)

        piece = pl.ds(k * tile, tile)
        copy = pltpu.make_async_copy(done.at[piece], grad_out.at[piece], gsem.at[k])
        copy.start()
        copies.append(copy)
    for copy in copies:
        copy.wait()


def body(ndp, nt, norm_input, key_grad, positions, norm_gain, key_weight, first_moment, second_moment):
    rows, cols = key_weight.shape
    tokens, width = norm_input.shape
    nq = ndp // 2
    features = ndp * rows
    tile = min(128, tokens)
    ntile = tokens // tile
    hh = HEAD // 2
    frequency = ROPE_BASE ** (-(2.0 * np.arange(hh)) / HEAD)
    frequency = np.resize(frequency.astype(np.float32), (1, 128))
    any_spec = pl.BlockSpec(memory_space=pl.ANY)
    vmem = pl.BlockSpec(memory_space=pltpu.VMEM)
    dma = pltpu.SemaphoreType.DMA
    nqx = math.isqrt(nq)
    while nq % nqx:
        nqx -= 1
    nqy = nq // nqx
    hc = cols // 2
    na = nqx + nqy - 2
    nx1 = (nqx - 1) * nqy
    nw2 = nx1 + (nqy - 1) * nqx
    nn = ndp - 1 + nt - 1
    scratch = [
        pltpu.VMEM((tokens, features), BF16),
        pltpu.VMEM((ntile, tile), jnp.int32),
        pltpu.VMEM((width // 128, 128), BF16),
        pltpu.VMEM((1, 128), F32),
        pltpu.VMEM((rows, cols), F32),
        pltpu.VMEM((rows, cols), F32),
        pltpu.VMEM((1, width), F32),
        pltpu.VMEM((tokens, features), BF16),
        pltpu.VMEM((features, tokens), BF16),
        pltpu.VMEM((features, tokens), BF16),
        pltpu.VMEM((tokens, 128), F32),
        pltpu.VMEM((nt, features, cols), BF16),
        pltpu.VMEM((nt, features, cols), BF16),
        pltpu.VMEM((nt, nq * rows, cols), BF16),
        pltpu.VMEM((nt, nx1, rows, hc), BF16),
        pltpu.VMEM((nt, nqy - 1, nqx * rows, hc), BF16),
        pltpu.VMEM((nt, nqy - 1, rows, hc), BF16),
        pltpu.VMEM((nt, nqx - 1, rows, hc), BF16),
        pltpu.VMEM((nt - 1, rows, cols), BF16),
        pltpu.VMEM((nt - 1, rows, cols), BF16),
        pltpu.VMEM((rows, cols), F32),
        pltpu.VMEM((2, 8, 128), F32),
        pltpu.VMEM((nn, 8, 128), F32),
        dma((7,)), dma((ntile,)),
        dma, dma,
        dma((2, nt)), dma((nt, 2)),
        dma, dma((nt,)),
        dma, dma((nt,)),
        dma, dma((2 * nt,)),
        dma, dma((nt, 2)),
        dma, dma((nt,)),
        dma, dma,
        dma((2,)), dma((2,)),
        dma, dma,
        dma, dma,
        dma, dma,
    ]
    results = pl.pallas_call(
        functools.partial(kernel, ndp, nt, nqx),
        out_shape=(
            pltpu.VMEM((tokens, width), BF16),
            pltpu.VMEM((tokens, width), BF16),
            pltpu.VMEM((tokens, 128), F32),
            pltpu.VMEM((nq, 2 * rows, cols), BF16),
            pltpu.VMEM((rows, cols), F32),
            pltpu.VMEM((rows, cols), F32),
        ),
        in_specs=[any_spec] * 8,
        out_specs=(vmem,) * 6,
        scratch_shapes=scratch,
        compiler_params=pltpu.CompilerParams(
            collective_id=0, has_side_effects=True, vmem_limit_bytes=42 * 2**20
        ),
    )(
        norm_input, key_grad, positions.reshape(ntile, tile), norm_gain.reshape(width // 128, 128),
        jnp.asarray(frequency), key_weight, first_moment, second_moment,
    )
    results = [pltpu.with_memory_space_constraint(r, pltpu.VMEM) for r in results]
    input_grad, new_weight, new_first, new_second = pl.pallas_call(
        write_out,
        out_shape=[jax.ShapeDtypeStruct(results[n].shape, results[n].dtype) for n in (0, 3, 4, 5)],
        in_specs=[vmem] * 6,
        out_specs=[any_spec] * 4,
        scratch_shapes=[pltpu.VMEM((tokens, width), BF16), dma((3,)), dma((tokens // min(32, tokens),))],
        compiler_params=pltpu.CompilerParams(vmem_limit_bytes=10 * 2**20),
    )(*results)
    return (input_grad, new_weight.reshape(features, cols), new_first, new_second)


def solution(mesh):
    in_specs = (
        P(("dp", "tensor"), None),
        P(("dp", "tensor"), None),
        P(("dp", "tensor")),
        P(),
        P("dp", "tensor"),
        P("dp", "tensor"),
        P("dp", "tensor"),
    )
    out_specs = (P(("dp", "tensor"), None), P(None, "tensor"), P("dp", "tensor"), P("dp", "tensor"))
    return jax.shard_map(
        functools.partial(body, mesh.shape["dp"], mesh.shape["tensor"]),
        mesh=mesh, in_specs=in_specs, out_specs=out_specs, check_vma=False,
    )
```

```python
import functools
import math

import jax
import jax.numpy as jnp
import numpy as np
from jax import lax
from jax.experimental import pallas as pl
from jax.experimental.pallas import tpu as pltpu
from jax.sharding import PartitionSpec as P

KV_HEADS = 4
HEAD = 128
ROPE_BASE = 500000.0

eps_norm = 1e-05
beta_one = 0.9
beta_two = 0.95
learn_rate = 0.0003
decay_rate = 0.1
eps_adam = 1e-08

MESH = pl.DeviceIdType.MESH
F32 = jnp.float32
BF16 = jnp.bfloat16


def kernel(
    ndp, nt, nqx, x_hbm, kg_hbm, pos_hbm, gain_hbm, freq_hbm, w_hbm, m1_hbm, m2_hbm,
    grad, x, cross, nwb, nf, ns,
    kg, pos, gain_in, freq, m1, m2, gain, kb, kbt, sks, ssq,
    wf, wg, rcore, r1a, r1b, r2a, r2b, zs, rz, gsum, nsend, nrecv,
    isem, xsem, a1s, a1r, zfs, zfr, b3s, b3r, b4s, p2s, p2r, a3s, a3r, cs, cr, qs, qr, q2s, q2r,
    zsd, zr, nss, nsr, ws, wr, vs, vr, us, ur,
):
    nq = ndp // 2
    nqy = nq // nqx
    rows, cols = w_hbm.shape
    half = nq * rows
    tokens, width = x.shape
    tile = min(128, tokens)
    ntile = tokens // tile
    hc = cols // 2
    cc = min(512, hc)
    hcol = (pl.ds(0, hc), pl.ds(hc, hc))
    dp = lax.axis_index("dp")
    t = lax.axis_index("tensor")
    c = dp % 2
    q = dp // 2
    qy = q // nqx
    qx = q % nqx
    mate = q * 2 + (1 - c)
    mine = pl.multiple_of(c * half, half)
    theirs = pl.multiple_of((1 - c) * half, half)
    sent = []

    def describe(src, dst, ssem, rsem, dev):
        return pltpu.make_async_remote_copy(
            src_ref=src, dst_ref=dst, send_sem=ssem, recv_sem=rsem, device_id=dev, device_id_type=MESH
        )

    def remote(src, dst, ssem, rsem, dev):
        describe(src, dst, ssem, rsem, dev).start()

    def arrived(like, rsem):
        describe(like, like, a1s, rsem, (mate, t)).wait_recv()

    def left(like, ssem):
        describe(like, like, ssem, a1r, (mate, t)).wait_send()

    def chunks(n):
        return wg.at[0, pl.ds(0, n * rows), hcol[0]]

    def layers(n):
        return wg.at[:, pl.ds(0, n * rows), hcol[0]]

    def pos_x(k):
        return (qx + k) % nqx

    def pos_y(k):
        return (qy + k) % nqy

    def dev_x(k):
        return ((qy * nqx + pos_x(k)) * 2 + c, t)

    def dev_y(k):
        return ((pos_y(k) * nqx + qx) * 2 + c, t)

    def slot(yy, xx):
        return pl.ds(pl.multiple_of(mine + (yy * nqx + xx) * rows, rows), rows)

    def band(yy):
        return pl.ds(pl.multiple_of(mine + yy * nqx * rows, nqx * rows), nqx * rows)

    my_rows = slot(qy, qx)
    steps = sorted(range(1, nt), key=lambda o: (-min(o, nt - o), o)) + [0]

    def dest(i):
        return (t + steps[i]) % nt

    near = jnp.minimum(t, nt - 1 - t)
    low = t < nt - 1 - t

    def block(i):
        if i == 0:
            return t
        d = (i + 1) // 2
        both = t + (d if i % 2 else -d) * jnp.where(low, -1, 1)
        return jnp.where(i <= 2 * near, both, jnp.where(low, i, nt - 1 - i))

    def local(src, dst, sem):
        copy = pltpu.make_async_copy(src, dst, sem)
        copy.start()
        return copy

    own = local(w_hbm, wf.at[t, my_rows], isem.at[0])
    kg_in = local(kg_hbm, kg, isem.at[1])
    pos_in = local(pos_hbm, pos, isem.at[2])
    freq_in = local(freq_hbm, freq, isem.at[3])
    x_in = []
    for k in range(ntile):
        piece = pl.ds(k * tile, tile)
        x_in.append(local(x_hbm.at[piece], x.at[piece], xsem.at[k]))
    gain_copy = local(gain_hbm, gain_in, isem.at[4])
    m1_in = local(m1_hbm, m1, isem.at[5])
    m2_in = local(m2_hbm, m2, isem.at[6])

    barrier = pltpu.get_barrier_semaphore()
    for k in range(1, ndp):
        pl.semaphore_signal(barrier, inc=1, device_id=((dp + k) % ndp, t), device_id_type=MESH)
    for k in range(1, nt):
        pl.semaphore_signal(barrier, inc=1, device_id=(dp, (t + k) % nt), device_id_type=MESH)
    cross[...] = jnp.zeros_like(cross)
    kg_in.wait()
    pos_in.wait()
    freq_in.wait()
    hh = HEAD // 2
    turn = jnp.broadcast_to(freq[...], (128, 128)).T[:hh, :tile]
    for k in range(ntile):
        lanes = pl.ds(k * tile, tile)
        angle = turn * pos[k : k + 1, :].astype(F32)
        cosine = jnp.cos(angle)
        sine = jnp.sin(angle)
        turned = kg[pl.ds(k * tile, tile), :].astype(F32).T
        for h in range(KV_HEADS):
            a = turned[h * HEAD : h * HEAD + hh]
            b = turned[h * HEAD + hh : (h + 1) * HEAD]
            for p, value in enumerate((a * cosine + b * sine, b * cosine - a * sine)):
                value = value.astype(BF16)
                for m in range(hh // rows):
                    n = (h * HEAD + p * hh) // rows + m
                    kbt[pl.ds((n % 2) * half + (n // 2) * rows, rows), lanes] = value[
                        m * rows : (m + 1) * rows
                    ]

    pl.semaphore_wait(barrier, ndp - 1 + nt - 1)

    na = nqx + nqy - 2
    nx1 = (nqx - 1) * nqy
    ny1 = (nqy - 1) * nqx
    nw2 = nx1 + ny1
    for k in range(1, nqx):
        remote(w_hbm.at[:, hcol[0]], wf.at[t, my_rows, hcol[0]], a1s, a1r, dev_x(k))
    for k in range(1, nqy):
        remote(w_hbm.at[:, hcol[1]], wf.at[t, my_rows, hcol[1]], a1s, a1r, dev_y(k))
    sent.append((chunks(na), a1s))

    def spread(i, near=(False, True)):
        b = block(i)
        for h, count, other, dev in ((0, nqx, nqy, dev_y), (1, nqy, nqx, dev_x)):
            for k in range(1, other):
                for m in range(count):
                    place = slot(qy, pos_x(m)) if h == 0 else slot(pos_y(m), qx)
                    if (m == 0) in near:
                        part = wf.at[b, place, hcol[h]]
                        src = w_hbm.at[:, hcol[h]] if i == 0 and m == 0 else part
                        remote(src, part, b4s if i == nt - 1 else b3s, b3r.at[i], dev(k))

    sent.append((wg.at[pl.ds(0, nt - 1), pl.ds(0, nw2 * rows), hcol[0]], b3s))
    sent.append((chunks(nw2 - na), b4s))
    spread(0, (True,))

    def line_pieces(b, side, p, dev):
        if p == 0:
            parts = [wf.at[b, my_rows]]
        else:
            parts = [wf.at[b, slot(qy, pos_x(k)), hcol[0]] for k in range(1, nqx)]
            parts += [wf.at[b, slot(pos_y(k), qx), hcol[1]] for k in range(1, nqy)]
        return [describe(part, part, zfs.at[side, b], zfr.at[b, p], dev) for part in parts]

    def pass_on(b, side, p):
        to, there = (t + 1, t + 1 < nt) if side == 0 else (t - 1, t >= 1)

        @pl.when(there)
        def _():
            for copy in line_pieces(b, side, p, (dp, to)):
                copy.start()

    line_sent = [(0, t, t >= 0), (1, t, t >= 0)]

    def relay(d, p):
        for side, b, here in ((0, t - d, t - d >= 0), (1, t + d, t + d < nt)):
            @pl.when(here)
            def _(side=side, b=b):
                arrived(chunks(2 if p == 0 else na), zfr.at[b, p])
                pass_on(b, side, p)

            if p == 0:
                line_sent.append((side, b, here))

    for side, to, there in ((0, t + 1, t + 1 < nt), (1, t - 1, t >= 1)):
        @pl.when(there)
        def _(side=side, to=to):
            describe(w_hbm, wf.at[t, my_rows], zfs.at[side, t], zfr.at[t, 0], (dp, to)).start()

    def other_parts(b):
        parts = [wf.at[b, slot(pos_y(k), qx), hcol[0]] for k in range(1, nqy)]
        return parts + [wf.at[b, slot(qy, pos_x(k)), hcol[1]] for k in range(1, nqx)]

    half_line = nt // 2
    middle_low = t == half_line - 1
    middle_high = t == half_line

    def cross_over():
        for here, b, far in (
            (middle_low, 0, [half_line + n for n in range(half_line)]),
            (middle_high, nt - 1, [half_line - 1 - n for n in range(half_line)]),
        ):
            @pl.when(here)
            def _(b=b, far=far):
                for n, to in enumerate(far):
                    for part in other_parts(b):
                        remote(part, part, p2s.at[n], p2r, (dp, to))

    def crossed_over():
        @pl.when(jnp.logical_or(middle_low, middle_high))
        def _():
            for n in range(half_line):
                left(chunks(na), p2s.at[n])

    def gather_third(i):
        if i == nt - 1:
            arrived(chunks(na), p2r)
            arrived(chunks(nw2 - na), b3r.at[i])
        else:
            arrived(chunks(nw2), b3r.at[i])
        if i == nt - 3 and i > 1:
            cross_over()
        part = wf.at[block(i), pl.ds(mine, half)]
        remote(part, part, a3s, a3r.at[i], (mate, t))

    sent.append((wg.at[:, pl.ds(0, half)], a3s))

    def sum_squares(k):
        x_in[k].wait()

        @pl.loop(0, tile // 16)
        def _(g):
            r = pl.ds(pl.multiple_of(k * tile + g * 16, 16), 16)
            total = None
            for b in range(width // 512):
                v = x[r, b * 512 : (b + 1) * 512].astype(F32)
                v = v * v
                v = (v[:, :128] + v[:, 128:256]) + (v[:, 256:384] + v[:, 384:])
                total = v if total is None else total + v
            ssq[r, :] = total

        lanes = pl.ds(k * tile, tile)
        mean = jnp.sum(ssq[lanes, :].T, axis=0, keepdims=True) / width
        sks[:, lanes] = (kbt[:, lanes].astype(F32) * lax.rsqrt(mean + eps_norm)).astype(BF16)

    for k in range(ntile):
        sum_squares(k)

    gain_copy.wait()
    for k in range(width // 128):
        gain[:, k * 128 : (k + 1) * 128] = gain_in[k : k + 1, :].astype(F32)

    sent.append((wg.at[:, pl.ds(0, half)], cs))

    def product(i, h):
        j = dest(i)

        @pl.loop(0, hc // cc)
        def _(n):
            off = pl.ds(pl.multiple_of(h * hc + n * cc, cc), cc)
            col = pl.ds(pl.multiple_of(j * cols + h * hc + n * cc, cc), cc)
            total = jnp.dot(sks[...], x[:, col], preferred_element_type=F32)
            wg[j, :, off] = (total * gain[:, col]).astype(BF16)

        n = i * 2 + h
        remote(wg.at[j, pl.ds(theirs, half), hcol[h]], rcore.at[j, :, hcol[h]], cs, cr.at[n], (mate, t))

    def pair_sum(i, h):
        j = dest(i)
        arrived(rcore.at[j, :, hcol[h]], cr.at[i * 2 + h])

        @pl.loop(0, half // 16)
        def _(g):
            r = pl.ds(pl.multiple_of(mine + g * 16, 16), 16)
            l = pl.ds(pl.multiple_of(g * 16, 16), 16)
            a = wg[j, r, hcol[h]].astype(F32) + rcore[j, l, hcol[h]].astype(F32)
            wg[j, r, hcol[h]] = a.astype(BF16)

    def reduce_first(i, h):
        j = dest(i)
        if h == 0:
            for k in range(1, nqx):
                for yy in range(nqy):
                    n = (k - 1) * nqy + yy
                    src = wg.at[j, slot(yy, pos_x(k)), hcol[0]]
                    remote(src, r1a.at[i, n], qs, qr.at[i, 0], dev_x(k))
        else:
            for k in range(1, nqy):
                src = wg.at[j, band(pos_y(k)), hcol[1]]
                remote(src, r1b.at[i, k - 1], qs, qr.at[i, 1], dev_y(k))

    sent.append((layers(nw2), qs))
    sent.append((layers(na), q2s))

    def middle(i, h):
        j = dest(i)
        arrived(chunks(ny1 if h else nx1), qr.at[i, h])
        if h == 0:
            @pl.loop(0, rows // 16)
            def _(g):
                l = pl.ds(pl.multiple_of(g * 16, 16), 16)
                for yy in range(nqy):
                    r = pl.ds(pl.multiple_of(mine + (yy * nqx + qx) * rows + g * 16, 16), 16)
                    a = wg[j, r, hcol[0]].astype(F32)
                    for k in range(nqx - 1):
                        a = a + r1a[i, k * nqy + yy, l, :].astype(F32)
                    wg[j, r, hcol[0]] = a.astype(BF16)

            for k in range(1, nqy):
                src = wg.at[j, slot(pos_y(k), qx), hcol[0]]
                remote(src, r2a.at[i, k - 1], q2s, q2r.at[i], dev_y(k))
        else:
            @pl.loop(0, nqx * rows // 16)
            def _(g):
                l = pl.ds(pl.multiple_of(g * 16, 16), 16)
                r = pl.ds(pl.multiple_of(mine + qy * nqx * rows + g * 16, 16), 16)
                a = wg[j, r, hcol[1]].astype(F32)
                for k in range(nqy - 1):
                    a = a + r1b[i, k, l, :].astype(F32)
                wg[j, r, hcol[1]] = a.astype(BF16)

            for k in range(1, nqx):
                src = wg.at[j, slot(qy, pos_x(k)), hcol[1]]
                remote(src, r2b.at[i, k - 1], q2s, q2r.at[i], dev_x(k))

    sent.append((zs, zsd))

    def final(i):
        j = dest(i)
        arrived(chunks(na), q2r.at[i])

        @pl.loop(0, rows // 16)
        def _(g):
            r = pl.ds(pl.multiple_of(g * 16, 16), 16)
            m = pl.ds(pl.multiple_of(mine + q * rows + g * 16, 16), 16)
            for part, other, count in ((hcol[0], r2a, nqy - 1), (hcol[1], r2b, nqx - 1)):
                a = wg[j, m, part].astype(F32)
                for k in range(count):
                    a = a + other[i, k, r, :].astype(F32)
                if i < nt - 1:
                    zs[i, r, part] = a.astype(BF16)
                else:
                    gsum[r, part] = a

        if i < nt - 1:
            remote(zs.at[i], rz.at[i], zsd, zr, (dp, j))

    uc = min(256, cols)

    def upstream(i):
        b = block(i)
        arrived(wf.at[b, pl.ds(mine, half)], a3r.at[i])

        @pl.loop(0, cols // uc)
        def _(h):
            off = pl.ds(pl.multiple_of(h * uc, uc), uc)
            col = pl.ds(pl.multiple_of(b * cols + h * uc, uc), uc)
            u = jnp.dot(kb[...], wf[b, :, off], preferred_element_type=F32) * gain[:, col]
            scale = ssq[...]
            u = jnp.concatenate([u[:, n * 128 : (n + 1) * 128] * scale for n in range(uc // 128)], axis=1)
            grad[:, col] = u.astype(BF16)
            p = u * x[:, col].astype(F32)
            total = p[:, :128]
            for n in range(1, uc // 128):
                total = total + p[:, n * 128 : (n + 1) * 128]
            cross[...] += total

    def turn_back():
        for k in range(ntile):
            lanes = pl.ds(k * tile, tile)
            kb[lanes, :] = kbt[:, lanes].astype(F32).T.astype(BF16)
            mean = jnp.sum(ssq[lanes, :], axis=1, keepdims=True) / width
            ssq[lanes, :] = jnp.broadcast_to(lax.rsqrt(mean + eps_norm), (tile, 128))

    units = [(i, h) for i in range(nt) for h in range(2)]
    early = min(4, len(units))
    for n, unit in enumerate(units):
        product(*unit)
        if n == len(units) - 1:
            relay(1, 1)
        if n > 0:
            pair_sum(*units[n - 1])
            if n <= early:
                reduce_first(*units[n - 1])
        if n == 2:
            own.wait()
            arrived(chunks(na), a1r)
            pass_on(t, 0, 1)
            pass_on(t, 1, 1)
        if n == early:
            relay(1, 0)
    pair_sum(*units[-1])
    turn_back()

    def both_middle(i):
        middle(i, 0)
        middle(i, 1)
        if i + 2 < nt:
            reduce_first(i + 2, 0)
            reduce_first(i + 2, 1)

    both_middle(0)
    both_middle(1)
    final(0)
    if nt > 3:
        relay(2, 0)
    for i in range(2, nt):
        both_middle(i)
        if i == nt - 1:
            spread(1)
            spread(0, (False,))
        final(i - 1)
        if 2 < i < nt - 1:
            relay(i - 1, 1)
            relay(i, 0)
    final(nt - 1)
    arrived(rz, zr)

    nsend[...] = jnp.zeros_like(nsend)

    @pl.loop(0, rows // 16)
    def _(g):
        r = pl.ds(pl.multiple_of(g * 16, 16), 16)
        a = gsum[r, :]
        for i in range(nt - 1):
            a = a + rz[i, r, :].astype(F32)
        gsum[r, :] = a
        a = a * a
        total = a[:, :128]
        for k in range(1, cols // 128):
            total = total + a[:, k * 128 : (k + 1) * 128]
        nsend[...] += jnp.sum(total, axis=0, keepdims=True)

    n = 0
    for b in reversed(range(nt)):
        for a in range(ndp):
            if a or b:
                remote(nsend, nrecv.at[n], nss, nsr, ((dp + a) % ndp, (t + b) % nt))
                n += 1
    sent.append((nrecv, nss))
    if nt > 3:
        relay(nt - 2, 1)
    gather_third(1)
    if nt - 3 == 1:
        cross_over()
    for i in range(2, nt - 1):
        spread(i)
    gather_third(0)
    upstream(1)
    arrived(nrecv, nsr)
    v = nsend[...] + jnp.sum(nrecv[...], axis=0)
    total_square = jnp.sum(v, axis=1, keepdims=True)
    limit = math.sqrt(kbt.shape[0] * width)
    clip = jnp.minimum(1.0, limit / (jnp.sqrt(total_square) + 1e-06))
    nat = pl.multiple_of(c * rows, rows)
    m1_in.wait()
    m2_in.wait()

    @pl.loop(0, rows // 16)
    def _(g):
        r = pl.ds(pl.multiple_of(g * 16, 16), 16)
        wr_ = pl.ds(pl.multiple_of(mine + q * rows + g * 16, 16), 16)
        clipped = gsum[r, :] * clip
        new_first = beta_one * m1[r, :] + (1.0 - beta_one) * clipped
        new_second = beta_two * m2[r, :] + (1.0 - beta_two) * clipped * clipped
        nf[r, :] = new_first
        ns[r, :] = new_second
        nwb[q, pl.ds(pl.multiple_of(nat + g * 16, 16), 16), :] = (
            wf[t, wr_, :].astype(F32) * (1.0 - learn_rate * decay_rate)
            - learn_rate * new_first / (jnp.sqrt(new_second) + eps_adam)
        ).astype(BF16)

    def piece_of(yy, xx, part):
        return nwb.at[yy * nqx + xx, pl.ds(nat, rows), part]

    for k in range(1, nqx):
        part = piece_of(qy, qx, hcol[0])
        remote(part, part, ws, wr, dev_x(k))
    for k in range(1, nqy):
        part = piece_of(qy, qx, hcol[1])
        remote(part, part, ws, wr, dev_y(k))
    sent.append((chunks(na), ws))

    upstream(0)
    relay(nt - 1, 0)
    relay(nt - 1, 1)
    spread(nt - 1, (False,))
    for i in range(2, nt - 1):
        gather_third(i)
        if i < nt - 2:
            upstream(i)

    arrived(chunks(na), wr)
    for m in range(max(nqx, nqy)):
        for k in range(1, nqy if m < nqx else 1):
            part = piece_of(qy, pos_x(m), hcol[0])
            remote(part, part, vs, vr.at[min(m, 1)], dev_y(k))
        for k in range(1, nqx if m < nqy else 1):
            part = piece_of(pos_y(m), qx, hcol[1])
            remote(part, part, vs, vr.at[min(m, 1)], dev_x(k))
    sent.append((chunks(nw2), vs))
    early_parts = [(qy, pos_x(m), hcol[0]) for m in range(nqx)] + [(pos_y(m), qx, hcol[1]) for m in range(nqy)]
    for place in early_parts:
        part = piece_of(*place)
        remote(part, part, us, ur, (mate, t))
    upstream(nt - 2)
    gather_third(nt - 1)
    upstream(nt - 1)

    for k in range(ntile):
        lanes = pl.ds(k * tile, tile)
        down = ssq[lanes, :1] * (jnp.sum(cross[lanes, :], axis=1, keepdims=True) / width)
        cross[lanes, :] = jnp.broadcast_to(down, (tile, 128))

    for late, count in ((0, na), (1, nw2 - na)):
        arrived(chunks(count), vr.at[late])
        late_parts = [
            (pos_y(k), pos_x(m), hcol[0]) for k in range(1, nqy) for m in range(nqx) if min(m, 1) == late
        ]
        late_parts += [
            (pos_y(m), pos_x(k), hcol[1]) for k in range(1, nqx) for m in range(nqy) if min(m, 1) == late
        ]
        for place in late_parts:
            part = piece_of(*place)
            remote(part, part, us, ur, (mate, t))
    whole = nwb.at[:, pl.ds(nat, rows)]
    sent.append((whole, us))
    arrived(whole, ur)
    for like, sem in sent:
        left(like, sem)
    crossed_over()
    for side, b, here in line_sent:
        there = t + 1 < nt if side == 0 else t >= 1

        @pl.when(jnp.logical_and(here, there))
        def _(side=side, b=b):
            left(chunks(2 + na), zfs.at[side, b])


def write_out(grad, x, down, nwb, nf, ns, grad_out, nw_out, nf_out, ns_out, done, sem, gsem):
    tokens, width = x.shape
    tile = min(32, tokens)
    small = [
        pltpu.make_async_copy(src, dst, sem.at[n])
        for n, (src, dst) in enumerate(((nwb, nw_out), (nf, nf_out), (ns, ns_out)))
    ]
    copies = list(small)
    for k in range(tokens // tile):
        if k == 1:
            for copy in small:
                copy.start()

        @pl.loop(0, tile // 16)
        def _(g):
            r = pl.ds(pl.multiple_of(k * tile + g * 16, 16), 16)
            factor = down[r, :]
            for n in range(width // 128):
                col = slice(n * 128, (n + 1) * 128)
                done[r, col] = (grad[r, col].astype(F32) - factor * x[r, col].astype(F32)).astype(BF16)

        piece = pl.ds(k * tile, tile)
        copy = pltpu.make_async_copy(done.at[piece], grad_out.at[piece], gsem.at[k])
        copy.start()
        copies.append(copy)
    for copy in copies:
        copy.wait()


def body(ndp, nt, norm_input, key_grad, positions, norm_gain, key_weight, first_moment, second_moment):
    rows, cols = key_weight.shape
    tokens, width = norm_input.shape
    nq = ndp // 2
    features = ndp * rows
    tile = min(128, tokens)
    ntile = tokens // tile
    hh = HEAD // 2
    frequency = ROPE_BASE ** (-(2.0 * np.arange(hh)) / HEAD)
    frequency = np.resize(frequency.astype(np.float32), (1, 128))
    any_spec = pl.BlockSpec(memory_space=pl.ANY)
    vmem = pl.BlockSpec(memory_space=pltpu.VMEM)
    dma = pltpu.SemaphoreType.DMA
    nqx = math.isqrt(nq)
    while nq % nqx:
        nqx -= 1
    nqy = nq // nqx
    hc = cols // 2
    na = nqx + nqy - 2
    nx1 = (nqx - 1) * nqy
    nw2 = nx1 + (nqy - 1) * nqx
    nn = ndp * nt - 1
    scratch = [
        pltpu.VMEM((tokens, features), BF16),
        pltpu.VMEM((ntile, tile), jnp.int32),
        pltpu.VMEM((width // 128, 128), BF16),
        pltpu.VMEM((1, 128), F32),
        pltpu.VMEM((rows, cols), F32),
        pltpu.VMEM((rows, cols), F32),
        pltpu.VMEM((1, width), F32),
        pltpu.VMEM((tokens, features), BF16),
        pltpu.VMEM((features, tokens), BF16),
        pltpu.VMEM((features, tokens), BF16),
        pltpu.VMEM((tokens, 128), F32),
        pltpu.VMEM((nt, features, cols), BF16),
        pltpu.VMEM((nt, features, cols), BF16),
        pltpu.VMEM((nt, nq * rows, cols), BF16),
        pltpu.VMEM((nt, nx1, rows, hc), BF16),
        pltpu.VMEM((nt, nqy - 1, nqx * rows, hc), BF16),
        pltpu.VMEM((nt, nqy - 1, rows, hc), BF16),
        pltpu.VMEM((nt, nqx - 1, rows, hc), BF16),
        pltpu.VMEM((nt - 1, rows, cols), BF16),
        pltpu.VMEM((nt - 1, rows, cols), BF16),
        pltpu.VMEM((rows, cols), F32),
        pltpu.VMEM((1, 128), F32),
        pltpu.VMEM((nn, 1, 128), F32),
        dma((7,)), dma((ntile,)),
        dma, dma,
        dma((2, nt)), dma((nt, 2)),
        dma, dma((nt,)), dma,
        dma((nt // 2,)), dma,
        dma, dma((nt,)),
        dma, dma((2 * nt,)),
        dma, dma((nt, 2)),
        dma, dma((nt,)),
        dma, dma,
        dma, dma,
        dma, dma,
        dma, dma((2,)),
        dma, dma,
    ]
    results = pl.pallas_call(
        functools.partial(kernel, ndp, nt, nqx),
        out_shape=(
            pltpu.VMEM((tokens, width), BF16),
            pltpu.VMEM((tokens, width), BF16),
            pltpu.VMEM((tokens, 128), F32),
            pltpu.VMEM((nq, 2 * rows, cols), BF16),
            pltpu.VMEM((rows, cols), F32),
            pltpu.VMEM((rows, cols), F32),
        ),
        in_specs=[any_spec] * 8,
        out_specs=(vmem,) * 6,
        scratch_shapes=scratch,
        compiler_params=pltpu.CompilerParams(
            collective_id=0, has_side_effects=True, vmem_limit_bytes=42 * 2**20
        ),
    )(
        norm_input, key_grad, positions.reshape(ntile, tile), norm_gain.reshape(width // 128, 128),
        jnp.asarray(frequency), key_weight, first_moment, second_moment,
    )
    results = [pltpu.with_memory_space_constraint(r, pltpu.VMEM) for r in results]
    input_grad, new_weight, new_first, new_second = pl.pallas_call(
        write_out,
        out_shape=[jax.ShapeDtypeStruct(results[n].shape, results[n].dtype) for n in (0, 3, 4, 5)],
        in_specs=[vmem] * 6,
        out_specs=[any_spec] * 4,
        scratch_shapes=[pltpu.VMEM((tokens, width), BF16), dma((3,)), dma((tokens // min(32, tokens),))],
        compiler_params=pltpu.CompilerParams(vmem_limit_bytes=10 * 2**20),
    )(*results)
    return (input_grad, new_weight.reshape(features, cols), new_first, new_second)


def solution(mesh):
    in_specs = (
        P(("dp", "tensor"), None),
        P(("dp", "tensor"), None),
        P(("dp", "tensor")),
        P(),
        P("dp", "tensor"),
        P("dp", "tensor"),
        P("dp", "tensor"),
    )
    out_specs = (P(("dp", "tensor"), None), P(None, "tensor"), P("dp", "tensor"), P("dp", "tensor"))
    return jax.shard_map(
        functools.partial(body, mesh.shape["dp"], mesh.shape["tensor"]),
        mesh=mesh, in_specs=in_specs, out_specs=out_specs, check_vma=False,
    )
```

```python
import functools
import math

import jax
import jax.numpy as jnp
import numpy as np
from jax import lax
from jax.experimental import pallas as pl
from jax.experimental.pallas import tpu as pltpu
from jax.sharding import PartitionSpec as P

KV_HEADS = 4
HEAD = 128
ROPE_BASE = 500000.0

eps_norm = 1e-05
beta_one = 0.9
beta_two = 0.95
learn_rate = 0.0003
decay_rate = 0.1
eps_adam = 1e-08

MESH = pl.DeviceIdType.MESH
F32 = jnp.float32
BF16 = jnp.bfloat16


def kernel(
    ndp, nt, nqx, x_hbm, kg_hbm, pos_hbm, gain_hbm, freq_hbm, w_hbm, m1_hbm, m2_hbm,
    grad, x, cross, nwb, nf, ns,
    kg, pos, gain_in, freq, m1, m2, gain, kb, kbt, sks, ssq,
    wf, wg, rcore, r1a, r1b, r2a, r2b, zs, rz, gsum, nsend, nrecv,
    isem, xsem, a1s, a1r, zfs, zfr, b3s, b3r, b4s, p2s, p2r, a3s, a3r, cs, cr, qs, qr, q2s, q2r,
    zsd, zr, nss, nsr, ws, wr, vs, vr, us, ur,
):
    nq = ndp // 2
    nqy = nq // nqx
    rows, cols = w_hbm.shape
    half = nq * rows
    tokens, width = x.shape
    tile = min(128, tokens)
    ntile = tokens // tile
    hc = cols // 2
    cc = min(512, hc)
    hcol = (pl.ds(0, hc), pl.ds(hc, hc))
    dp = lax.axis_index("dp")
    t = lax.axis_index("tensor")
    c = dp % 2
    q = dp // 2
    qy = q // nqx
    qx = q % nqx
    mate = q * 2 + (1 - c)
    mine = pl.multiple_of(c * half, half)
    theirs = pl.multiple_of((1 - c) * half, half)
    sent = []

    def describe(src, dst, ssem, rsem, dev):
        return pltpu.make_async_remote_copy(
            src_ref=src, dst_ref=dst, send_sem=ssem, recv_sem=rsem, device_id=dev, device_id_type=MESH
        )

    def remote(src, dst, ssem, rsem, dev):
        describe(src, dst, ssem, rsem, dev).start()

    def arrived(like, rsem):
        describe(like, like, a1s, rsem, (mate, t)).wait_recv()

    def left(like, ssem):
        describe(like, like, ssem, a1r, (mate, t)).wait_send()

    def chunks(n):
        return wg.at[0, pl.ds(0, n * rows), hcol[0]]

    def layers(n):
        return wg.at[:, pl.ds(0, n * rows), hcol[0]]

    def pos_x(k):
        return (qx + k) % nqx

    def pos_y(k):
        return (qy + k) % nqy

    def dev_x(k):
        return ((qy * nqx + pos_x(k)) * 2 + c, t)

    def dev_y(k):
        return ((pos_y(k) * nqx + qx) * 2 + c, t)

    def slot(yy, xx):
        return pl.ds(pl.multiple_of(mine + (yy * nqx + xx) * rows, rows), rows)

    def band(yy):
        return pl.ds(pl.multiple_of(mine + yy * nqx * rows, nqx * rows), nqx * rows)

    my_rows = slot(qy, qx)
    steps = sorted(range(1, nt), key=lambda o: (-min(o, nt - o), o)) + [0]

    def dest(i):
        return (t + steps[i]) % nt

    near = jnp.minimum(t, nt - 1 - t)
    low = t < nt - 1 - t

    def block(i):
        if i == 0:
            return t
        d = (i + 1) // 2
        both = t + (d if i % 2 else -d) * jnp.where(low, -1, 1)
        return jnp.where(i <= 2 * near, both, jnp.where(low, i, nt - 1 - i))

    def local(src, dst, sem):
        copy = pltpu.make_async_copy(src, dst, sem)
        copy.start()
        return copy

    own = local(w_hbm, wf.at[t, my_rows], isem.at[0])
    kg_in = local(kg_hbm, kg, isem.at[1])
    pos_in = local(pos_hbm, pos, isem.at[2])
    freq_in = local(freq_hbm, freq, isem.at[3])
    x_in = []
    for k in range(ntile):
        piece = pl.ds(k * tile, tile)
        x_in.append(local(x_hbm.at[piece], x.at[piece], xsem.at[k]))
    gain_copy = local(gain_hbm, gain_in, isem.at[4])
    m1_in = local(m1_hbm, m1, isem.at[5])
    m2_in = local(m2_hbm, m2, isem.at[6])

    barrier = pltpu.get_barrier_semaphore()

    def greet(dev):
        pl.semaphore_signal(barrier, inc=1, device_id=dev, device_id_type=MESH)

    greet((mate, t))
    for k in range(1, nqx):
        greet(dev_x(k))
    for k in range(1, nqy):
        greet(dev_y(k))
    met = 1 + (nqx - 1) + (nqy - 1)
    if nt > 4:
        for k in range(1, nt):
            greet((dp, (t + k) % nt))
        pl.semaphore_wait(barrier, met + nt - 1)
    else:
        pl.when(t >= 1)(lambda: greet((dp, t - 1)))
        pl.when(t + 1 < nt)(lambda: greet((dp, t + 1)))
        pl.semaphore_wait(barrier, met + jnp.where(t >= 1, 1, 0) + jnp.where(t + 1 < nt, 1, 0))


    na = nqx + nqy - 2
    nx1 = (nqx - 1) * nqy
    ny1 = (nqy - 1) * nqx
    nw2 = nx1 + ny1
    own.wait()
    for k in range(1, nqx):
        remote(wf.at[t, my_rows, hcol[0]], wf.at[t, my_rows, hcol[0]], a1s, a1r, dev_x(k))
    for k in range(1, nqy):
        remote(wf.at[t, my_rows, hcol[1]], wf.at[t, my_rows, hcol[1]], a1s, a1r, dev_y(k))
    sent.append((chunks(na), a1s))

    def spread(i, near=(False, True)):
        b = block(i)
        for h, count, other, dev in ((0, nqx, nqy, dev_y), (1, nqy, nqx, dev_x)):
            for k in range(1, other):
                for m in range(count):
                    place = slot(qy, pos_x(m)) if h == 0 else slot(pos_y(m), qx)
                    if (m == 0) in near:
                        part = wf.at[b, place, hcol[h]]
                        remote(part, part, b4s if i == nt - 1 else b3s, b3r.at[i], dev(k))

    sent.append((wg.at[pl.ds(0, nt - 1), pl.ds(0, nw2 * rows), hcol[0]], b3s))
    sent.append((chunks(nw2 - na), b4s))
    spread(0, (True,))

    def line_pieces(b, side, p, dev):
        if p == 0:
            parts = [wf.at[b, my_rows]]
        else:
            parts = [wf.at[b, slot(qy, pos_x(k)), hcol[0]] for k in range(1, nqx)]
            parts += [wf.at[b, slot(pos_y(k), qx), hcol[1]] for k in range(1, nqy)]
        return [describe(part, part, zfs.at[side, b], zfr.at[b, p], dev) for part in parts]

    def pass_on(b, side, p):
        to, there = (t + 1, t + 1 < nt) if side == 0 else (t - 1, t >= 1)

        @pl.when(there)
        def _():
            for copy in line_pieces(b, side, p, (dp, to)):
                copy.start()

    line_sent = [(0, t, t >= 0), (1, t, t >= 0)]

    def relay(d, p):
        for side, b, here in ((0, t - d, t - d >= 0), (1, t + d, t + d < nt)):
            @pl.when(here)
            def _(side=side, b=b):
                arrived(chunks(2 if p == 0 else na), zfr.at[b, p])
                pass_on(b, side, p)

            if p == 0:
                line_sent.append((side, b, here))

    for side, to, there in ((0, t + 1, t + 1 < nt), (1, t - 1, t >= 1)):
        @pl.when(there)
        def _(side=side, to=to):
            describe(wf.at[t, my_rows], wf.at[t, my_rows], zfs.at[side, t], zfr.at[t, 0], (dp, to)).start()

    def other_parts(b):
        parts = [wf.at[b, slot(pos_y(k), qx), hcol[0]] for k in range(1, nqy)]
        return parts + [wf.at[b, slot(qy, pos_x(k)), hcol[1]] for k in range(1, nqx)]

    half_line = nt // 2
    middle_low = t == half_line - 1
    middle_high = t == half_line

    def cross_over():
        for here, b, far in (
            (middle_low, 0, [half_line + n for n in range(half_line)]),
            (middle_high, nt - 1, [half_line - 1 - n for n in range(half_line)]),
        ):
            @pl.when(here)
            def _(b=b, far=far):
                for n, to in enumerate(far):
                    for part in other_parts(b):
                        remote(part, part, p2s.at[n], p2r, (dp, to))

    def crossed_over():
        @pl.when(jnp.logical_or(middle_low, middle_high))
        def _():
            for n in range(half_line):
                left(chunks(na), p2s.at[n])

    def gather_third(i):
        if i == nt - 1:
            arrived(chunks(na), p2r)
            arrived(chunks(nw2 - na), b3r.at[i])
        else:
            arrived(chunks(nw2), b3r.at[i])
        if i == nt - 3 and i > 1:
            cross_over()
        part = wf.at[block(i), pl.ds(mine, half)]
        remote(part, part, a3s, a3r.at[i], (mate, t))

    sent.append((wg.at[:, pl.ds(0, half)], a3s))

    cross[...] = jnp.zeros_like(cross)
    kg_in.wait()
    pos_in.wait()
    freq_in.wait()
    hh = HEAD // 2
    turn = jnp.broadcast_to(freq[...], (128, 128)).T[:hh, :tile]
    for k in range(ntile):
        lanes = pl.ds(k * tile, tile)
        angle = turn * pos[k : k + 1, :].astype(F32)
        cosine = jnp.cos(angle)
        sine = jnp.sin(angle)
        turned = kg[pl.ds(k * tile, tile), :].astype(F32).T
        for h in range(KV_HEADS):
            a = turned[h * HEAD : h * HEAD + hh]
            b = turned[h * HEAD + hh : (h + 1) * HEAD]
            for p, value in enumerate((a * cosine + b * sine, b * cosine - a * sine)):
                value = value.astype(BF16)
                for m in range(hh // rows):
                    n = (h * HEAD + p * hh) // rows + m
                    kbt[pl.ds((n % 2) * half + (n // 2) * rows, rows), lanes] = value[
                        m * rows : (m + 1) * rows
                    ]

    def sum_squares(k):
        x_in[k].wait()

        @pl.loop(0, tile // 16)
        def _(g):
            r = pl.ds(pl.multiple_of(k * tile + g * 16, 16), 16)
            total = None
            for b in range(width // 512):
                v = x[r, b * 512 : (b + 1) * 512].astype(F32)
                v = v * v
                v = (v[:, :128] + v[:, 128:256]) + (v[:, 256:384] + v[:, 384:])
                total = v if total is None else total + v
            ssq[r, :] = total

        lanes = pl.ds(k * tile, tile)
        mean = jnp.sum(ssq[lanes, :].T, axis=0, keepdims=True) / width
        sks[:, lanes] = (kbt[:, lanes].astype(F32) * lax.rsqrt(mean + eps_norm)).astype(BF16)

    for k in range(ntile):
        sum_squares(k)

    gain_copy.wait()
    for k in range(width // 128):
        gain[:, k * 128 : (k + 1) * 128] = gain_in[k : k + 1, :].astype(F32)

    sent.append((wg.at[:, pl.ds(0, half)], cs))

    def product(i, h):
        j = dest(i)

        @pl.loop(0, hc // cc)
        def _(n):
            off = pl.ds(pl.multiple_of(h * hc + n * cc, cc), cc)
            col = pl.ds(pl.multiple_of(j * cols + h * hc + n * cc, cc), cc)
            total = jnp.dot(sks[...], x[:, col], preferred_element_type=F32)
            wg[j, :, off] = (total * gain[:, col]).astype(BF16)

        n = i * 2 + h
        remote(wg.at[j, pl.ds(theirs, half), hcol[h]], rcore.at[j, :, hcol[h]], cs, cr.at[n], (mate, t))

    def pair_sum(i, h):
        j = dest(i)
        arrived(rcore.at[j, :, hcol[h]], cr.at[i * 2 + h])

        @pl.loop(0, half // 16)
        def _(g):
            r = pl.ds(pl.multiple_of(mine + g * 16, 16), 16)
            l = pl.ds(pl.multiple_of(g * 16, 16), 16)
            a = wg[j, r, hcol[h]].astype(F32) + rcore[j, l, hcol[h]].astype(F32)
            wg[j, r, hcol[h]] = a.astype(BF16)

    def reduce_first(i, h):
        j = dest(i)
        if h == 0:
            for k in range(1, nqx):
                for yy in range(nqy):
                    n = (k - 1) * nqy + yy
                    src = wg.at[j, slot(yy, pos_x(k)), hcol[0]]
                    remote(src, r1a.at[i, n], qs, qr.at[i, 0], dev_x(k))
        else:
            for k in range(1, nqy):
                src = wg.at[j, band(pos_y(k)), hcol[1]]
                remote(src, r1b.at[i, k - 1], qs, qr.at[i, 1], dev_y(k))

    sent.append((layers(nw2), qs))
    sent.append((layers(na), q2s))

    def middle(i, h):
        j = dest(i)
        arrived(chunks(ny1 if h else nx1), qr.at[i, h])
        if h == 0:
            @pl.loop(0, rows // 16)
            def _(g):
                l = pl.ds(pl.multiple_of(g * 16, 16), 16)
                for yy in range(nqy):
                    r = pl.ds(pl.multiple_of(mine + (yy * nqx + qx) * rows + g * 16, 16), 16)
                    a = wg[j, r, hcol[0]].astype(F32)
                    for k in range(nqx - 1):
                        a = a + r1a[i, k * nqy + yy, l, :].astype(F32)
                    wg[j, r, hcol[0]] = a.astype(BF16)

            for k in range(1, nqy):
                src = wg.at[j, slot(pos_y(k), qx), hcol[0]]
                remote(src, r2a.at[i, k - 1], q2s, q2r.at[i], dev_y(k))
        else:
            @pl.loop(0, nqx * rows // 16)
            def _(g):
                l = pl.ds(pl.multiple_of(g * 16, 16), 16)
                r = pl.ds(pl.multiple_of(mine + qy * nqx * rows + g * 16, 16), 16)
                a = wg[j, r, hcol[1]].astype(F32)
                for k in range(nqy - 1):
                    a = a + r1b[i, k, l, :].astype(F32)
                wg[j, r, hcol[1]] = a.astype(BF16)

            for k in range(1, nqx):
                src = wg.at[j, slot(qy, pos_x(k)), hcol[1]]
                remote(src, r2b.at[i, k - 1], q2s, q2r.at[i], dev_x(k))

    sent.append((zs, zsd))

    def final(i):
        j = dest(i)
        arrived(chunks(na), q2r.at[i])

        @pl.loop(0, rows // 16)
        def _(g):
            r = pl.ds(pl.multiple_of(g * 16, 16), 16)
            m = pl.ds(pl.multiple_of(mine + q * rows + g * 16, 16), 16)
            for part, other, count in ((hcol[0], r2a, nqy - 1), (hcol[1], r2b, nqx - 1)):
                a = wg[j, m, part].astype(F32)
                for k in range(count):
                    a = a + other[i, k, r, :].astype(F32)
                if i < nt - 1:
                    zs[i, r, part] = a.astype(BF16)
                else:
                    gsum[r, part] = a

        if i < nt - 1:
            remote(zs.at[i], rz.at[i], zsd, zr, (dp, j))

    uc = min(256, cols)

    def upstream(i):
        b = block(i)
        arrived(wf.at[b, pl.ds(mine, half)], a3r.at[i])

        @pl.loop(0, cols // uc)
        def _(h):
            off = pl.ds(pl.multiple_of(h * uc, uc), uc)
            col = pl.ds(pl.multiple_of(b * cols + h * uc, uc), uc)
            u = jnp.dot(kb[...], wf[b, :, off], preferred_element_type=F32) * gain[:, col]
            scale = ssq[...]
            u = jnp.concatenate([u[:, n * 128 : (n + 1) * 128] * scale for n in range(uc // 128)], axis=1)
            grad[:, col] = u.astype(BF16)
            p = u * x[:, col].astype(F32)
            total = p[:, :128]
            for n in range(1, uc // 128):
                total = total + p[:, n * 128 : (n + 1) * 128]
            cross[...] += total

    def turn_back():
        for k in range(ntile):
            lanes = pl.ds(k * tile, tile)
            kb[lanes, :] = kbt[:, lanes].astype(F32).T.astype(BF16)
            mean = jnp.sum(ssq[lanes, :], axis=1, keepdims=True) / width
            ssq[lanes, :] = jnp.broadcast_to(lax.rsqrt(mean + eps_norm), (tile, 128))

    units = [(i, h) for i in range(nt) for h in range(2)]
    early = min(4, len(units))
    for n, unit in enumerate(units):
        product(*unit)
        if n == len(units) - 1:
            relay(1, 1)
        for m in {1: (0, 1), 0: (), 2: ()}.get(n, (n - 1,)):
            pair_sum(*units[m])
            if m < early:
                reduce_first(*units[m])
        if n == 1:
            arrived(chunks(na), a1r)
            pass_on(t, 0, 1)
            pass_on(t, 1, 1)
        if n == early:
            relay(1, 0)
    pair_sum(*units[-1])
    turn_back()

    def both_middle(i):
        middle(i, 0)
        middle(i, 1)
        if i + 2 < nt:
            reduce_first(i + 2, 0)
            reduce_first(i + 2, 1)

    both_middle(0)
    both_middle(1)
    final(0)
    if nt > 3:
        relay(2, 0)
    for i in range(2, nt):
        both_middle(i)
        if i == nt - 1:
            spread(1)
            spread(0, (False,))
        final(i - 1)
        if 2 < i < nt - 1:
            relay(i - 1, 1)
            relay(i, 0)
    final(nt - 1)
    arrived(rz, zr)

    nsend[...] = jnp.zeros_like(nsend)

    @pl.loop(0, rows // 16)
    def _(g):
        r = pl.ds(pl.multiple_of(g * 16, 16), 16)
        a = gsum[r, :]
        for i in range(nt - 1):
            a = a + rz[i, r, :].astype(F32)
        gsum[r, :] = a
        a = a * a
        total = a[:, :128]
        for k in range(1, cols // 128):
            total = total + a[:, k * 128 : (k + 1) * 128]
        nsend[...] += jnp.sum(total, axis=0, keepdims=True)

    n = 0
    for b in reversed(range(nt)):
        for a in range(ndp):
            if a or b:
                remote(nsend, nrecv.at[n], nss, nsr, ((dp + a) % ndp, (t + b) % nt))
                n += 1
    sent.append((nrecv, nss))
    if nt > 3:
        relay(nt - 2, 1)
    gather_third(1)
    if nt - 3 == 1:
        cross_over()
    for i in range(2, nt - 1):
        spread(i)
    gather_third(0)
    upstream(1)
    arrived(nrecv, nsr)
    v = nsend[...] + jnp.sum(nrecv[...], axis=0)
    total_square = jnp.sum(v, axis=1, keepdims=True)
    limit = math.sqrt(kbt.shape[0] * width)
    clip = jnp.minimum(1.0, limit / (jnp.sqrt(total_square) + 1e-06))
    nat = pl.multiple_of(c * rows, rows)
    m1_in.wait()
    m2_in.wait()

    @pl.loop(0, rows // 16)
    def _(g):
        r = pl.ds(pl.multiple_of(g * 16, 16), 16)
        wr_ = pl.ds(pl.multiple_of(mine + q * rows + g * 16, 16), 16)
        clipped = gsum[r, :] * clip
        new_first = beta_one * m1[r, :] + (1.0 - beta_one) * clipped
        new_second = beta_two * m2[r, :] + (1.0 - beta_two) * clipped * clipped
        nf[r, :] = new_first
        ns[r, :] = new_second
        nwb[q, pl.ds(pl.multiple_of(nat + g * 16, 16), 16), :] = (
            wf[t, wr_, :].astype(F32) * (1.0 - learn_rate * decay_rate)
            - learn_rate * new_first / (jnp.sqrt(new_second) + eps_adam)
        ).astype(BF16)

    def piece_of(yy, xx, part):
        return nwb.at[yy * nqx + xx, pl.ds(nat, rows), part]

    for k in range(1, nqx):
        part = piece_of(qy, qx, hcol[0])
        remote(part, part, ws, wr, dev_x(k))
    for k in range(1, nqy):
        part = piece_of(qy, qx, hcol[1])
        remote(part, part, ws, wr, dev_y(k))
    sent.append((chunks(na), ws))

    upstream(0)
    relay(nt - 1, 0)
    relay(nt - 1, 1)
    spread(nt - 1, (False,))
    for i in range(2, nt - 1):
        gather_third(i)
        if i < nt - 2:
            upstream(i)

    arrived(chunks(na), wr)
    for m in range(max(nqx, nqy)):
        for k in range(1, nqy if m < nqx else 1):
            part = piece_of(qy, pos_x(m), hcol[0])
            remote(part, part, vs, vr.at[min(m, 1)], dev_y(k))
        for k in range(1, nqx if m < nqy else 1):
            part = piece_of(pos_y(m), qx, hcol[1])
            remote(part, part, vs, vr.at[min(m, 1)], dev_x(k))
    sent.append((chunks(nw2), vs))
    early_parts = [(qy, pos_x(m), hcol[0]) for m in range(nqx)] + [(pos_y(m), qx, hcol[1]) for m in range(nqy)]
    for place in early_parts:
        part = piece_of(*place)
        remote(part, part, us, ur, (mate, t))
    upstream(nt - 2)
    gather_third(nt - 1)
    upstream(nt - 1)

    for k in range(ntile):
        lanes = pl.ds(k * tile, tile)
        down = ssq[lanes, :1] * (jnp.sum(cross[lanes, :], axis=1, keepdims=True) / width)
        cross[lanes, :] = jnp.broadcast_to(down, (tile, 128))

    for late, count in ((0, na), (1, nw2 - na)):
        arrived(chunks(count), vr.at[late])
        late_parts = [
            (pos_y(k), pos_x(m), hcol[0]) for k in range(1, nqy) for m in range(nqx) if min(m, 1) == late
        ]
        late_parts += [
            (pos_y(m), pos_x(k), hcol[1]) for k in range(1, nqx) for m in range(nqy) if min(m, 1) == late
        ]
        for place in late_parts:
            part = piece_of(*place)
            remote(part, part, us, ur, (mate, t))
    whole = nwb.at[:, pl.ds(nat, rows)]
    sent.append((whole, us))
    arrived(whole, ur)
    for like, sem in sent:
        left(like, sem)
    crossed_over()
    for side, b, here in line_sent:
        there = t + 1 < nt if side == 0 else t >= 1

        @pl.when(jnp.logical_and(here, there))
        def _(side=side, b=b):
            left(chunks(2 + na), zfs.at[side, b])


def write_out(grad, x, down, nwb, nf, ns, grad_out, nw_out, nf_out, ns_out, done, sem, gsem):
    tokens, width = x.shape
    tile = min(32, tokens)
    small = [
        pltpu.make_async_copy(src, dst, sem.at[n])
        for n, (src, dst) in enumerate(((nwb, nw_out), (nf, nf_out), (ns, ns_out)))
    ]
    for copy in small:
        copy.start()
    copies = list(small)
    for k in range(tokens // tile):
        @pl.loop(0, tile // 16)
        def _(g):
            r = pl.ds(pl.multiple_of(k * tile + g * 16, 16), 16)
            factor = down[r, :]
            for n in range(width // 128):
                col = slice(n * 128, (n + 1) * 128)
                done[r, col] = (grad[r, col].astype(F32) - factor * x[r, col].astype(F32)).astype(BF16)

        piece = pl.ds(k * tile, tile)
        copy = pltpu.make_async_copy(done.at[piece], grad_out.at[piece], gsem.at[k])
        copy.start()
        copies.append(copy)
    for copy in copies:
        copy.wait()


def body(ndp, nt, norm_input, key_grad, positions, norm_gain, key_weight, first_moment, second_moment):
    rows, cols = key_weight.shape
    tokens, width = norm_input.shape
    nq = ndp // 2
    features = ndp * rows
    tile = min(128, tokens)
    ntile = tokens // tile
    hh = HEAD // 2
    frequency = ROPE_BASE ** (-(2.0 * np.arange(hh)) / HEAD)
    frequency = np.resize(frequency.astype(np.float32), (1, 128))
    any_spec = pl.BlockSpec(memory_space=pl.ANY)
    vmem = pl.BlockSpec(memory_space=pltpu.VMEM)
    dma = pltpu.SemaphoreType.DMA
    nqx = math.isqrt(nq)
    while nq % nqx:
        nqx -= 1
    nqy = nq // nqx
    hc = cols // 2
    na = nqx + nqy - 2
    nx1 = (nqx - 1) * nqy
    nw2 = nx1 + (nqy - 1) * nqx
    nn = ndp * nt - 1
    scratch = [
        pltpu.VMEM((tokens, features), BF16),
        pltpu.VMEM((ntile, tile), jnp.int32),
        pltpu.VMEM((width // 128, 128), BF16),
        pltpu.VMEM((1, 128), F32),
        pltpu.VMEM((rows, cols), F32),
        pltpu.VMEM((rows, cols), F32),
        pltpu.VMEM((1, width), F32),
        pltpu.VMEM((tokens, features), BF16),
        pltpu.VMEM((features, tokens), BF16),
        pltpu.VMEM((features, tokens), BF16),
        pltpu.VMEM((tokens, 128), F32),
        pltpu.VMEM((nt, features, cols), BF16),
        pltpu.VMEM((nt, features, cols), BF16),
        pltpu.VMEM((nt, nq * rows, cols), BF16),
        pltpu.VMEM((nt, nx1, rows, hc), BF16),
        pltpu.VMEM((nt, nqy - 1, nqx * rows, hc), BF16),
        pltpu.VMEM((nt, nqy - 1, rows, hc), BF16),
        pltpu.VMEM((nt, nqx - 1, rows, hc), BF16),
        pltpu.VMEM((nt - 1, rows, cols), BF16),
        pltpu.VMEM((nt - 1, rows, cols), BF16),
        pltpu.VMEM((rows, cols), F32),
        pltpu.VMEM((1, 128), F32),
        pltpu.VMEM((nn, 1, 128), F32),
        dma((7,)), dma((ntile,)),
        dma, dma,
        dma((2, nt)), dma((nt, 2)),
        dma, dma((nt,)), dma,
        dma((nt // 2,)), dma,
        dma, dma((nt,)),
        dma, dma((2 * nt,)),
        dma, dma((nt, 2)),
        dma, dma((nt,)),
        dma, dma,
        dma, dma,
        dma, dma,
        dma, dma((2,)),
        dma, dma,
    ]
    results = pl.pallas_call(
        functools.partial(kernel, ndp, nt, nqx),
        out_shape=(
            pltpu.VMEM((tokens, width), BF16),
            pltpu.VMEM((tokens, width), BF16),
            pltpu.VMEM((tokens, 128), F32),
            pltpu.VMEM((nq, 2 * rows, cols), BF16),
            pltpu.VMEM((rows, cols), F32),
            pltpu.VMEM((rows, cols), F32),
        ),
        in_specs=[any_spec] * 8,
        out_specs=(vmem,) * 6,
        scratch_shapes=scratch,
        compiler_params=pltpu.CompilerParams(
            collective_id=0, has_side_effects=True, vmem_limit_bytes=42 * 2**20
        ),
    )(
        norm_input, key_grad, positions.reshape(ntile, tile), norm_gain.reshape(width // 128, 128),
        jnp.asarray(frequency), key_weight, first_moment, second_moment,
    )
    results = [pltpu.with_memory_space_constraint(r, pltpu.VMEM) for r in results]
    input_grad, new_weight, new_first, new_second = pl.pallas_call(
        write_out,
        out_shape=[jax.ShapeDtypeStruct(results[n].shape, results[n].dtype) for n in (0, 3, 4, 5)],
        in_specs=[vmem] * 6,
        out_specs=[any_spec] * 4,
        scratch_shapes=[pltpu.VMEM((tokens, width), BF16), dma((3,)), dma((tokens // min(32, tokens),))],
        compiler_params=pltpu.CompilerParams(vmem_limit_bytes=10 * 2**20),
    )(*results)
    return (input_grad, new_weight.reshape(features, cols), new_first, new_second)


def solution(mesh):
    in_specs = (
        P(("dp", "tensor"), None),
        P(("dp", "tensor"), None),
        P(("dp", "tensor")),
        P(),
        P("dp", "tensor"),
        P("dp", "tensor"),
        P("dp", "tensor"),
    )
    out_specs = (P(("dp", "tensor"), None), P(None, "tensor"), P("dp", "tensor"), P("dp", "tensor"))
    return jax.shard_map(
        functools.partial(body, mesh.shape["dp"], mesh.shape["tensor"]),
        mesh=mesh, in_specs=in_specs, out_specs=out_specs, check_vma=False,
    )
```

```python
import functools
import math

import jax
import jax.numpy as jnp
import numpy as np
from jax import lax
from jax.experimental import pallas as pl
from jax.experimental.pallas import tpu as pltpu
from jax.sharding import PartitionSpec as P

KV_HEADS = 4
HEAD = 128
ROPE_BASE = 500000.0

eps_norm = 1e-05
beta_one = 0.9
beta_two = 0.95
learn_rate = 0.0003
decay_rate = 0.1
eps_adam = 1e-08

MESH = pl.DeviceIdType.MESH
F32 = jnp.float32
BF16 = jnp.bfloat16


def kernel(
    ndp, nt, nqx, x_hbm, kg_hbm, pos_hbm, gain_hbm, freq_hbm, w_hbm, m1_hbm, m2_hbm,
    grad, x, cross, nwb, nf, ns,
    kg, pos, gain_in, freq, m1, m2, gain, kb, kbt, sks, ssq,
    wf, wg, rcore, r1a, r1b, r2a, r2b, zs, rz, gsum, nsend, nrecv,
    isem, xsem, a1s, a1r, zfs, zfr, b3s, b3r, b4s, p2s, p2r, a3s, a3r, cs, cr, qs, qr, q2s, q2r,
    zsd, zr, nss, nsr, ws, wr, vs, vr, us, ur,
):
    nq = ndp // 2
    nqy = nq // nqx
    rows, cols = w_hbm.shape
    half = nq * rows
    tokens, width = x.shape
    tile = min(128, tokens)
    ntile = tokens // tile
    hc = cols // 2
    cc = min(512, hc)
    hcol = (pl.ds(0, hc), pl.ds(hc, hc))
    dp = lax.axis_index("dp")
    t = lax.axis_index("tensor")
    c = dp % 2
    q = dp // 2
    qy = q // nqx
    qx = q % nqx
    mate = q * 2 + (1 - c)
    mine = pl.multiple_of(c * half, half)
    theirs = pl.multiple_of((1 - c) * half, half)
    sent = []

    def describe(src, dst, ssem, rsem, dev):
        return pltpu.make_async_remote_copy(
            src_ref=src, dst_ref=dst, send_sem=ssem, recv_sem=rsem, device_id=dev, device_id_type=MESH
        )

    def remote(src, dst, ssem, rsem, dev):
        describe(src, dst, ssem, rsem, dev).start()

    def arrived(like, rsem):
        describe(like, like, a1s, rsem, (mate, t)).wait_recv()

    def left(like, ssem):
        describe(like, like, ssem, a1r, (mate, t)).wait_send()

    def chunks(n):
        return wg.at[0, pl.ds(0, n * rows), hcol[0]]

    def layers(n):
        return wg.at[:, pl.ds(0, n * rows), hcol[0]]

    def pos_x(k):
        return (qx + k) % nqx

    def pos_y(k):
        return (qy + k) % nqy

    def dev_x(k):
        return ((qy * nqx + pos_x(k)) * 2 + c, t)

    def dev_y(k):
        return ((pos_y(k) * nqx + qx) * 2 + c, t)

    def slot(yy, xx):
        return pl.ds(pl.multiple_of(mine + (yy * nqx + xx) * rows, rows), rows)

    def band(yy):
        return pl.ds(pl.multiple_of(mine + yy * nqx * rows, nqx * rows), nqx * rows)

    my_rows = slot(qy, qx)
    steps = sorted(range(1, nt), key=lambda o: (-min(o, nt - o), o)) + [0]

    def dest(i):
        return (t + steps[i]) % nt

    near = jnp.minimum(t, nt - 1 - t)
    low = t < nt - 1 - t

    def block(i):
        if i == 0:
            return t
        d = (i + 1) // 2
        both = t + (d if i % 2 else -d) * jnp.where(low, -1, 1)
        return jnp.where(i <= 2 * near, both, jnp.where(low, i, nt - 1 - i))

    def local(src, dst, sem):
        copy = pltpu.make_async_copy(src, dst, sem)
        copy.start()
        return copy

    own = local(w_hbm, wf.at[t, my_rows], isem.at[0])
    kg_in = local(kg_hbm, kg, isem.at[1])
    pos_in = local(pos_hbm, pos, isem.at[2])
    freq_in = local(freq_hbm, freq, isem.at[3])
    x_in = []
    for k in range(ntile):
        piece = pl.ds(k * tile, tile)
        x_in.append(local(x_hbm.at[piece], x.at[piece], xsem.at[k]))
    gain_copy = local(gain_hbm, gain_in, isem.at[4])
    m1_in = local(m1_hbm, m1, isem.at[5])
    m2_in = local(m2_hbm, m2, isem.at[6])

    barrier = pltpu.get_barrier_semaphore()

    def greet(dev):
        pl.semaphore_signal(barrier, inc=1, device_id=dev, device_id_type=MESH)

    greet((mate, t))
    for k in range(1, nqx):
        greet(dev_x(k))
    for k in range(1, nqy):
        greet(dev_y(k))
    met = 1 + (nqx - 1) + (nqy - 1)
    if nt > 4:
        for k in range(1, nt):
            greet((dp, (t + k) % nt))
        pl.semaphore_wait(barrier, met + nt - 1)
    else:
        pl.when(t >= 1)(lambda: greet((dp, t - 1)))
        pl.when(t + 1 < nt)(lambda: greet((dp, t + 1)))
        pl.semaphore_wait(barrier, met + jnp.where(t >= 1, 1, 0) + jnp.where(t + 1 < nt, 1, 0))


    na = nqx + nqy - 2
    nx1 = (nqx - 1) * nqy
    ny1 = (nqy - 1) * nqx
    nw2 = nx1 + ny1
    own.wait()
    for k in range(1, nqx):
        remote(wf.at[t, my_rows, hcol[0]], wf.at[t, my_rows, hcol[0]], a1s, a1r, dev_x(k))
    for k in range(1, nqy):
        remote(wf.at[t, my_rows, hcol[1]], wf.at[t, my_rows, hcol[1]], a1s, a1r, dev_y(k))
    sent.append((chunks(na), a1s))

    def spread(i, near=(False, True)):
        b = block(i)
        for h, count, other, dev in ((0, nqx, nqy, dev_y), (1, nqy, nqx, dev_x)):
            for k in range(1, other):
                for m in range(count):
                    place = slot(qy, pos_x(m)) if h == 0 else slot(pos_y(m), qx)
                    if (m == 0) in near:
                        part = wf.at[b, place, hcol[h]]
                        remote(part, part, b4s if i == nt - 1 else b3s, b3r.at[i], dev(k))

    sent.append((wg.at[pl.ds(0, nt - 1), pl.ds(0, nw2 * rows), hcol[0]], b3s))
    sent.append((chunks(nw2 - na), b4s))
    spread(0, (True,))

    def line_pieces(b, side, p, dev):
        if p == 0:
            parts = [wf.at[b, my_rows]]
        else:
            parts = [wf.at[b, slot(qy, pos_x(k)), hcol[0]] for k in range(1, nqx)]
            parts += [wf.at[b, slot(pos_y(k), qx), hcol[1]] for k in range(1, nqy)]
        return [describe(part, part, zfs.at[side, b], zfr.at[b, p], dev) for part in parts]

    def pass_on(b, side, p):
        to, there = (t + 1, t + 1 < nt) if side == 0 else (t - 1, t >= 1)

        @pl.when(there)
        def _():
            for copy in line_pieces(b, side, p, (dp, to)):
                copy.start()

    line_sent = [(0, t, t >= 0), (1, t, t >= 0)]

    def relay(d, p):
        for side, b, here in ((0, t - d, t - d >= 0), (1, t + d, t + d < nt)):
            @pl.when(here)
            def _(side=side, b=b):
                arrived(chunks(2 if p == 0 else na), zfr.at[b, p])
                pass_on(b, side, p)

            if p == 0:
                line_sent.append((side, b, here))

    for side, to, there in ((0, t + 1, t + 1 < nt), (1, t - 1, t >= 1)):
        @pl.when(there)
        def _(side=side, to=to):
            describe(wf.at[t, my_rows], wf.at[t, my_rows], zfs.at[side, t], zfr.at[t, 0], (dp, to)).start()

    def other_parts(b):
        parts = [wf.at[b, slot(pos_y(k), qx), hcol[0]] for k in range(1, nqy)]
        return parts + [wf.at[b, slot(qy, pos_x(k)), hcol[1]] for k in range(1, nqx)]

    half_line = nt // 2
    middle_low = t == half_line - 1
    middle_high = t == half_line

    def cross_over():
        for here, b, far in (
            (middle_low, 0, [half_line + n for n in range(half_line)]),
            (middle_high, nt - 1, [half_line - 1 - n for n in range(half_line)]),
        ):
            @pl.when(here)
            def _(b=b, far=far):
                for n, to in enumerate(far):
                    for part in other_parts(b):
                        remote(part, part, p2s.at[n], p2r, (dp, to))

    def crossed_over():
        @pl.when(jnp.logical_or(middle_low, middle_high))
        def _():
            for n in range(half_line):
                left(chunks(na), p2s.at[n])

    def gather_third(i):
        if i == nt - 1:
            arrived(chunks(na), p2r)
            arrived(chunks(nw2 - na), b3r.at[i])
        else:
            arrived(chunks(nw2), b3r.at[i])
        if i == nt - 3 and i > 1:
            cross_over()
        part = wf.at[block(i), pl.ds(mine, half)]
        remote(part, part, a3s, a3r.at[i], (mate, t))

    sent.append((wg.at[:, pl.ds(0, half)], a3s))

    cross[...] = jnp.zeros_like(cross)
    kg_in.wait()
    pos_in.wait()
    freq_in.wait()
    hh = HEAD // 2
    turn = jnp.broadcast_to(freq[...], (128, 128)).T[:hh, :tile]
    for k in range(ntile):
        lanes = pl.ds(k * tile, tile)
        angle = turn * pos[k : k + 1, :].astype(F32)
        cosine = jnp.cos(angle)
        sine = jnp.sin(angle)
        turned = kg[pl.ds(k * tile, tile), :].astype(F32).T
        for h in range(KV_HEADS):
            a = turned[h * HEAD : h * HEAD + hh]
            b = turned[h * HEAD + hh : (h + 1) * HEAD]
            for p, value in enumerate((a * cosine + b * sine, b * cosine - a * sine)):
                value = value.astype(BF16)
                for m in range(hh // rows):
                    n = (h * HEAD + p * hh) // rows + m
                    kbt[pl.ds((n % 2) * half + (n // 2) * rows, rows), lanes] = value[
                        m * rows : (m + 1) * rows
                    ]

    def sum_squares(k):
        x_in[k].wait()

        @pl.loop(0, tile // 16)
        def _(g):
            r = pl.ds(pl.multiple_of(k * tile + g * 16, 16), 16)
            total = None
            for b in range(width // 512):
                v = x[r, b * 512 : (b + 1) * 512].astype(F32)
                v = v * v
                v = (v[:, :128] + v[:, 128:256]) + (v[:, 256:384] + v[:, 384:])
                total = v if total is None else total + v
            ssq[r, :] = total

        lanes = pl.ds(k * tile, tile)
        mean = jnp.sum(ssq[lanes, :].T, axis=0, keepdims=True) / width
        sks[:, lanes] = (kbt[:, lanes].astype(F32) * lax.rsqrt(mean + eps_norm)).astype(BF16)

    for k in range(ntile):
        sum_squares(k)

    gain_copy.wait()
    for k in range(width // 128):
        gain[:, k * 128 : (k + 1) * 128] = gain_in[k : k + 1, :].astype(F32)

    sent.append((wg.at[:, pl.ds(0, half)], cs))

    def product(i, h, n, first=0, size=hc):
        j = dest(i)
        step = min(cc, size)

        @pl.loop(0, size // step)
        def _(m):
            off = pl.ds(pl.multiple_of(h * hc + first + m * step, step), step)
            col = pl.ds(pl.multiple_of(j * cols + h * hc + first + m * step, step), step)
            total = jnp.dot(sks[...], x[:, col], preferred_element_type=F32)
            wg[j, :, off] = (total * gain[:, col]).astype(BF16)

        part = pl.ds(h * hc + first, size)
        remote(wg.at[j, pl.ds(theirs, half), part], rcore.at[j, :, part], cs, cr.at[n], (mate, t))

    def pair_sum(i, h, n, first=0, size=hc):
        j = dest(i)
        part = pl.ds(h * hc + first, size)
        arrived(rcore.at[j, :, part], cr.at[n])

        @pl.loop(0, half // 16)
        def _(g):
            r = pl.ds(pl.multiple_of(mine + g * 16, 16), 16)
            l = pl.ds(pl.multiple_of(g * 16, 16), 16)
            a = wg[j, r, part].astype(F32) + rcore[j, l, part].astype(F32)
            wg[j, r, part] = a.astype(BF16)

    def reduce_first(i, h, first=0, size=hc):
        j = dest(i)
        if h == 0:
            for k in range(1, nqx):
                for yy in range(nqy):
                    n = (k - 1) * nqy + yy
                    src = wg.at[j, slot(yy, pos_x(k)), pl.ds(first, size)]
                    remote(src, r1a.at[i, n, :, pl.ds(first, size)], qs, qr.at[i, 0], dev_x(k))
        else:
            for k in range(1, nqy):
                src = wg.at[j, band(pos_y(k)), pl.ds(hc + first, size)]
                remote(src, r1b.at[i, k - 1, :, pl.ds(first, size)], qs, qr.at[i, 1], dev_y(k))

    sent.append((layers(nw2), qs))
    sent.append((layers(na), q2s))

    def middle(i, h):
        j = dest(i)
        arrived(chunks(ny1 if h else nx1), qr.at[i, h])
        if h == 0:
            @pl.loop(0, rows // 16)
            def _(g):
                l = pl.ds(pl.multiple_of(g * 16, 16), 16)
                for yy in range(nqy):
                    r = pl.ds(pl.multiple_of(mine + (yy * nqx + qx) * rows + g * 16, 16), 16)
                    a = wg[j, r, hcol[0]].astype(F32)
                    for k in range(nqx - 1):
                        a = a + r1a[i, k * nqy + yy, l, :].astype(F32)
                    wg[j, r, hcol[0]] = a.astype(BF16)

            for k in range(1, nqy):
                src = wg.at[j, slot(pos_y(k), qx), hcol[0]]
                remote(src, r2a.at[i, k - 1], q2s, q2r.at[i], dev_y(k))
        else:
            @pl.loop(0, nqx * rows // 16)
            def _(g):
                l = pl.ds(pl.multiple_of(g * 16, 16), 16)
                r = pl.ds(pl.multiple_of(mine + qy * nqx * rows + g * 16, 16), 16)
                a = wg[j, r, hcol[1]].astype(F32)
                for k in range(nqy - 1):
                    a = a + r1b[i, k, l, :].astype(F32)
                wg[j, r, hcol[1]] = a.astype(BF16)

            for k in range(1, nqx):
                src = wg.at[j, slot(qy, pos_x(k)), hcol[1]]
                remote(src, r2b.at[i, k - 1], q2s, q2r.at[i], dev_x(k))

    sent.append((zs, zsd))

    def final(i):
        j = dest(i)
        arrived(chunks(na), q2r.at[i])

        @pl.loop(0, rows // 16)
        def _(g):
            r = pl.ds(pl.multiple_of(g * 16, 16), 16)
            m = pl.ds(pl.multiple_of(mine + q * rows + g * 16, 16), 16)
            for part, other, count in ((hcol[0], r2a, nqy - 1), (hcol[1], r2b, nqx - 1)):
                a = wg[j, m, part].astype(F32)
                for k in range(count):
                    a = a + other[i, k, r, :].astype(F32)
                if i < nt - 1:
                    zs[i, r, part] = a.astype(BF16)
                else:
                    gsum[r, part] = a

        if i < nt - 1:
            remote(zs.at[i], rz.at[i], zsd, zr, (dp, j))

    uc = min(256, cols)

    def upstream(i):
        b = block(i)
        arrived(wf.at[b, pl.ds(mine, half)], a3r.at[i])

        @pl.loop(0, cols // uc)
        def _(h):
            off = pl.ds(pl.multiple_of(h * uc, uc), uc)
            col = pl.ds(pl.multiple_of(b * cols + h * uc, uc), uc)
            u = jnp.dot(kb[...], wf[b, :, off], preferred_element_type=F32) * gain[:, col]
            scale = ssq[...]
            u = jnp.concatenate([u[:, n * 128 : (n + 1) * 128] * scale for n in range(uc // 128)], axis=1)
            grad[:, col] = u.astype(BF16)
            p = u * x[:, col].astype(F32)
            total = p[:, :128]
            for n in range(1, uc // 128):
                total = total + p[:, n * 128 : (n + 1) * 128]
            cross[...] += total

    def turn_back():
        for k in range(ntile):
            lanes = pl.ds(k * tile, tile)
            kb[lanes, :] = kbt[:, lanes].astype(F32).T.astype(BF16)
            mean = jnp.sum(ssq[lanes, :], axis=1, keepdims=True) / width
            ssq[lanes, :] = jnp.broadcast_to(lax.rsqrt(mean + eps_norm), (tile, 128))

    hq = hc // 2
    units = [(0, 0, 0, 0, hq), (0, 1, 1, 0, hq), (0, 0, 2 * nt, hq, hq), (0, 1, 2 * nt + 1, hq, hq)]
    units += [(i, h, i * 2 + h) for i in range(1, nt) for h in range(2)]
    early = min(6, len(units))
    for n, unit in enumerate(units):
        product(*unit)
        if n == len(units) - 1:
            relay(1, 1)
        for m in {0: (), 1: (), 2: (), 3: (0, 1, 2, 3), 4: ()}.get(n, (n - 1,)):
            pair_sum(*units[m])
            if m < early:
                reduce_first(*units[m][:2], *units[m][3:])
        if n == 3:
            arrived(chunks(na), a1r)
            pass_on(t, 0, 1)
            pass_on(t, 1, 1)
        if n == early:
            relay(1, 0)
    pair_sum(*units[-1])
    turn_back()

    def both_middle(i):
        middle(i, 0)
        middle(i, 1)
        if i + 2 < nt:
            reduce_first(i + 2, 0)
            reduce_first(i + 2, 1)

    both_middle(0)
    both_middle(1)
    final(0)
    if nt > 3:
        relay(2, 0)
    for i in range(2, nt):
        both_middle(i)
        if i == nt - 1:
            spread(1)
            spread(0, (False,))
        final(i - 1)
        if 2 < i < nt - 1:
            relay(i - 1, 1)
            relay(i, 0)
    final(nt - 1)
    arrived(rz, zr)

    nsend[...] = jnp.zeros_like(nsend)

    @pl.loop(0, rows // 16)
    def _(g):
        r = pl.ds(pl.multiple_of(g * 16, 16), 16)
        a = gsum[r, :]
        for i in range(nt - 1):
            a = a + rz[i, r, :].astype(F32)
        gsum[r, :] = a
        a = a * a
        total = a[:, :128]
        for k in range(1, cols // 128):
            total = total + a[:, k * 128 : (k + 1) * 128]
        nsend[...] += jnp.sum(total, axis=0, keepdims=True)

    n = 0
    for b in reversed(range(nt)):
        for a in range(ndp):
            if a or b:
                remote(nsend, nrecv.at[n], nss, nsr, ((dp + a) % ndp, (t + b) % nt))
                n += 1
    sent.append((nrecv, nss))
    if nt > 3:
        relay(nt - 2, 1)
    gather_third(1)
    if nt - 3 == 1:
        cross_over()
    for i in range(2, nt - 1):
        spread(i)
    gather_third(0)
    upstream(1)
    arrived(nrecv, nsr)
    v = nsend[...] + jnp.sum(nrecv[...], axis=0)
    total_square = jnp.sum(v, axis=1, keepdims=True)
    limit = math.sqrt(kbt.shape[0] * width)
    clip = jnp.minimum(1.0, limit / (jnp.sqrt(total_square) + 1e-06))
    nat = pl.multiple_of(c * rows, rows)
    m1_in.wait()
    m2_in.wait()

    @pl.loop(0, rows // 16)
    def _(g):
        r = pl.ds(pl.multiple_of(g * 16, 16), 16)
        wr_ = pl.ds(pl.multiple_of(mine + q * rows + g * 16, 16), 16)
        clipped = gsum[r, :] * clip
        new_first = beta_one * m1[r, :] + (1.0 - beta_one) * clipped
        new_second = beta_two * m2[r, :] + (1.0 - beta_two) * clipped * clipped
        nf[r, :] = new_first
        ns[r, :] = new_second
        nwb[q, pl.ds(pl.multiple_of(nat + g * 16, 16), 16), :] = (
            wf[t, wr_, :].astype(F32) * (1.0 - learn_rate * decay_rate)
            - learn_rate * new_first / (jnp.sqrt(new_second) + eps_adam)
        ).astype(BF16)

    def piece_of(yy, xx, part):
        return nwb.at[yy * nqx + xx, pl.ds(nat, rows), part]

    for k in range(1, nqx):
        part = piece_of(qy, qx, hcol[0])
        remote(part, part, ws, wr, dev_x(k))
    for k in range(1, nqy):
        part = piece_of(qy, qx, hcol[1])
        remote(part, part, ws, wr, dev_y(k))
    sent.append((chunks(na), ws))

    upstream(0)
    relay(nt - 1, 0)
    relay(nt - 1, 1)
    spread(nt - 1, (False,))
    for i in range(2, nt - 1):
        gather_third(i)
        if i < nt - 2:
            upstream(i)

    arrived(chunks(na), wr)
    for m in range(max(nqx, nqy)):
        for k in range(1, nqy if m < nqx else 1):
            part = piece_of(qy, pos_x(m), hcol[0])
            remote(part, part, vs, vr.at[min(m, 1)], dev_y(k))
        for k in range(1, nqx if m < nqy else 1):
            part = piece_of(pos_y(m), qx, hcol[1])
            remote(part, part, vs, vr.at[min(m, 1)], dev_x(k))
    sent.append((chunks(nw2), vs))
    early_parts = [(qy, pos_x(m), hcol[0]) for m in range(nqx)] + [(pos_y(m), qx, hcol[1]) for m in range(nqy)]
    for place in early_parts:
        part = piece_of(*place)
        remote(part, part, us, ur, (mate, t))
    upstream(nt - 2)
    gather_third(nt - 1)
    upstream(nt - 1)

    for k in range(ntile):
        lanes = pl.ds(k * tile, tile)
        down = ssq[lanes, :1] * (jnp.sum(cross[lanes, :], axis=1, keepdims=True) / width)
        cross[lanes, :] = jnp.broadcast_to(down, (tile, 128))

    for late, count in ((0, na), (1, nw2 - na)):
        arrived(chunks(count), vr.at[late])
        late_parts = [
            (pos_y(k), pos_x(m), hcol[0]) for k in range(1, nqy) for m in range(nqx) if min(m, 1) == late
        ]
        late_parts += [
            (pos_y(m), pos_x(k), hcol[1]) for k in range(1, nqx) for m in range(nqy) if min(m, 1) == late
        ]
        for place in late_parts:
            part = piece_of(*place)
            remote(part, part, us, ur, (mate, t))
    whole = nwb.at[:, pl.ds(nat, rows)]
    sent.append((whole, us))
    arrived(whole, ur)
    for like, sem in sent:
        left(like, sem)
    crossed_over()
    for side, b, here in line_sent:
        there = t + 1 < nt if side == 0 else t >= 1

        @pl.when(jnp.logical_and(here, there))
        def _(side=side, b=b):
            left(chunks(2 + na), zfs.at[side, b])


def write_out(grad, x, down, nwb, nf, ns, grad_out, nw_out, nf_out, ns_out, done, sem, gsem):
    tokens, width = x.shape
    tile = min(32, tokens)
    small = [
        pltpu.make_async_copy(src, dst, sem.at[n])
        for n, (src, dst) in enumerate(((nwb, nw_out), (nf, nf_out), (ns, ns_out)))
    ]
    for copy in small:
        copy.start()
    copies = list(small)
    for k in range(tokens // tile):
        @pl.loop(0, tile // 16)
        def _(g):
            r = pl.ds(pl.multiple_of(k * tile + g * 16, 16), 16)
            factor = down[r, :]
            for n in range(width // 128):
                col = slice(n * 128, (n + 1) * 128)
                done[r, col] = (grad[r, col].astype(F32) - factor * x[r, col].astype(F32)).astype(BF16)

        piece = pl.ds(k * tile, tile)
        copy = pltpu.make_async_copy(done.at[piece], grad_out.at[piece], gsem.at[k])
        copy.start()
        copies.append(copy)
    for copy in copies:
        copy.wait()


def body(ndp, nt, norm_input, key_grad, positions, norm_gain, key_weight, first_moment, second_moment):
    rows, cols = key_weight.shape
    tokens, width = norm_input.shape
    nq = ndp // 2
    features = ndp * rows
    tile = min(128, tokens)
    ntile = tokens // tile
    hh = HEAD // 2
    frequency = ROPE_BASE ** (-(2.0 * np.arange(hh)) / HEAD)
    frequency = np.resize(frequency.astype(np.float32), (1, 128))
    any_spec = pl.BlockSpec(memory_space=pl.ANY)
    vmem = pl.BlockSpec(memory_space=pltpu.VMEM)
    dma = pltpu.SemaphoreType.DMA
    nqx = math.isqrt(nq)
    while nq % nqx:
        nqx -= 1
    nqy = nq // nqx
    hc = cols // 2
    na = nqx + nqy - 2
    nx1 = (nqx - 1) * nqy
    nw2 = nx1 + (nqy - 1) * nqx
    nn = ndp * nt - 1
    scratch = [
        pltpu.VMEM((tokens, features), BF16),
        pltpu.VMEM((ntile, tile), jnp.int32),
        pltpu.VMEM((width // 128, 128), BF16),
        pltpu.VMEM((1, 128), F32),
        pltpu.VMEM((rows, cols), F32),
        pltpu.VMEM((rows, cols), F32),
        pltpu.VMEM((1, width), F32),
        pltpu.VMEM((tokens, features), BF16),
        pltpu.VMEM((features, tokens), BF16),
        pltpu.VMEM((features, tokens), BF16),
        pltpu.VMEM((tokens, 128), F32),
        pltpu.VMEM((nt, features, cols), BF16),
        pltpu.VMEM((nt, features, cols), BF16),
        pltpu.VMEM((nt, nq * rows, cols), BF16),
        pltpu.VMEM((nt, nx1, rows, hc), BF16),
        pltpu.VMEM((nt, nqy - 1, nqx * rows, hc), BF16),
        pltpu.VMEM((nt, nqy - 1, rows, hc), BF16),
        pltpu.VMEM((nt, nqx - 1, rows, hc), BF16),
        pltpu.VMEM((nt - 1, rows, cols), BF16),
        pltpu.VMEM((nt - 1, rows, cols), BF16),
        pltpu.VMEM((rows, cols), F32),
        pltpu.VMEM((1, 128), F32),
        pltpu.VMEM((nn, 1, 128), F32),
        dma((7,)), dma((ntile,)),
        dma, dma,
        dma((2, nt)), dma((nt, 2)),
        dma, dma((nt,)), dma,
        dma((nt // 2,)), dma,
        dma, dma((nt,)),
        dma, dma((2 * nt + 2,)),
        dma, dma((nt, 2)),
        dma, dma((nt,)),
        dma, dma,
        dma, dma,
        dma, dma,
        dma, dma((2,)),
        dma, dma,
    ]
    results = pl.pallas_call(
        functools.partial(kernel, ndp, nt, nqx),
        out_shape=(
            pltpu.VMEM((tokens, width), BF16),
            pltpu.VMEM((tokens, width), BF16),
            pltpu.VMEM((tokens, 128), F32),
            pltpu.VMEM((nq, 2 * rows, cols), BF16),
            pltpu.VMEM((rows, cols), F32),
            pltpu.VMEM((rows, cols), F32),
        ),
        in_specs=[any_spec] * 8,
        out_specs=(vmem,) * 6,
        scratch_shapes=scratch,
        compiler_params=pltpu.CompilerParams(
            collective_id=0, has_side_effects=True, vmem_limit_bytes=42 * 2**20
        ),
    )(
        norm_input, key_grad, positions.reshape(ntile, tile), norm_gain.reshape(width // 128, 128),
        jnp.asarray(frequency), key_weight, first_moment, second_moment,
    )
    results = [pltpu.with_memory_space_constraint(r, pltpu.VMEM) for r in results]
    input_grad, new_weight, new_first, new_second = pl.pallas_call(
        write_out,
        out_shape=[jax.ShapeDtypeStruct(results[n].shape, results[n].dtype) for n in (0, 3, 4, 5)],
        in_specs=[vmem] * 6,
        out_specs=[any_spec] * 4,
        scratch_shapes=[pltpu.VMEM((tokens, width), BF16), dma((3,)), dma((tokens // min(32, tokens),))],
        compiler_params=pltpu.CompilerParams(vmem_limit_bytes=10 * 2**20),
    )(*results)
    return (input_grad, new_weight.reshape(features, cols), new_first, new_second)


def solution(mesh):
    in_specs = (
        P(("dp", "tensor"), None),
        P(("dp", "tensor"), None),
        P(("dp", "tensor")),
        P(),
        P("dp", "tensor"),
        P("dp", "tensor"),
        P("dp", "tensor"),
    )
    out_specs = (P(("dp", "tensor"), None), P(None, "tensor"), P("dp", "tensor"), P("dp", "tensor"))
    return jax.shard_map(
        functools.partial(body, mesh.shape["dp"], mesh.shape["tensor"]),
        mesh=mesh, in_specs=in_specs, out_specs=out_specs, check_vma=False,
    )
```

```python
import functools
import math

import jax
import jax.numpy as jnp
import numpy as np
from jax import lax
from jax.experimental import pallas as pl
from jax.experimental.pallas import tpu as pltpu
from jax.sharding import PartitionSpec as P

KV_HEADS = 4
HEAD = 128
ROPE_BASE = 500000.0

eps_norm = 1e-05
beta_one = 0.9
beta_two = 0.95
learn_rate = 0.0003
decay_rate = 0.1
eps_adam = 1e-08

MESH = pl.DeviceIdType.MESH
F32 = jnp.float32
BF16 = jnp.bfloat16


def kernel(
    ndp, nt, nqx, x_hbm, kg_hbm, pos_hbm, gain_hbm, freq_hbm, w_hbm, m1_hbm, m2_hbm,
    grad, x, cross, nwb, nf, ns,
    kg, pos, gain_in, freq, m1, m2, gain, kb, kbt, sks, ssq,
    wf, wg, rcore, r1a, r1b, r2a, r2b, zs, rz, gsum, nsend, nrecv,
    isem, xsem, a1s, a1r, zfs, zfr, b3s, b3r, b4s, p2s, p2r, a3s, a3r, cs, cr, qs, qr, q2s, q2r,
    zsd, zr, nss, nsr, ws, wr, vs, vr, us, ur,
):
    nq = ndp // 2
    nqy = nq // nqx
    rows, cols = w_hbm.shape
    half = nq * rows
    tokens, width = x.shape
    tile = min(128, tokens)
    ntile = tokens // tile
    hc = cols // 2
    cc = min(512, hc)
    hcol = (pl.ds(0, hc), pl.ds(hc, hc))
    dp = lax.axis_index("dp")
    t = lax.axis_index("tensor")
    c = dp % 2
    q = dp // 2
    qy = q // nqx
    qx = q % nqx
    mate = q * 2 + (1 - c)
    mine = pl.multiple_of(c * half, half)
    theirs = pl.multiple_of((1 - c) * half, half)
    sent = []

    def describe(src, dst, ssem, rsem, dev):
        return pltpu.make_async_remote_copy(
            src_ref=src, dst_ref=dst, send_sem=ssem, recv_sem=rsem, device_id=dev, device_id_type=MESH
        )

    def remote(src, dst, ssem, rsem, dev):
        describe(src, dst, ssem, rsem, dev).start()

    def arrived(like, rsem):
        describe(like, like, a1s, rsem, (mate, t)).wait_recv()

    def left(like, ssem):
        describe(like, like, ssem, a1r, (mate, t)).wait_send()

    def chunks(n):
        return wg.at[0, pl.ds(0, n * rows), hcol[0]]

    def layers(n):
        return wg.at[:, pl.ds(0, n * rows), hcol[0]]

    def pos_x(k):
        return (qx + k) % nqx

    def pos_y(k):
        return (qy + k) % nqy

    def dev_x(k):
        return ((qy * nqx + pos_x(k)) * 2 + c, t)

    def dev_y(k):
        return ((pos_y(k) * nqx + qx) * 2 + c, t)

    def slot(yy, xx):
        return pl.ds(pl.multiple_of(mine + (yy * nqx + xx) * rows, rows), rows)

    def band(yy):
        return pl.ds(pl.multiple_of(mine + yy * nqx * rows, nqx * rows), nqx * rows)

    my_rows = slot(qy, qx)
    steps = sorted(range(1, nt), key=lambda o: (-min(o, nt - o), o)) + [0]

    def dest(i):
        return (t + steps[i]) % nt

    near = jnp.minimum(t, nt - 1 - t)
    low = t < nt - 1 - t

    def block(i):
        if i == 0:
            return t
        d = (i + 1) // 2
        both = t + (d if i % 2 else -d) * jnp.where(low, -1, 1)
        return jnp.where(i <= 2 * near, both, jnp.where(low, i, nt - 1 - i))

    def local(src, dst, sem):
        copy = pltpu.make_async_copy(src, dst, sem)
        copy.start()
        return copy

    own = local(w_hbm, wf.at[t, my_rows], isem.at[0])
    kg_in = local(kg_hbm, kg, isem.at[1])
    pos_in = local(pos_hbm, pos, isem.at[2])
    freq_in = local(freq_hbm, freq, isem.at[3])
    x_in = []
    for k in range(ntile):
        piece = pl.ds(k * tile, tile)
        x_in.append(local(x_hbm.at[piece], x.at[piece], xsem.at[k]))
    gain_copy = local(gain_hbm, gain_in, isem.at[4])
    m1_in = local(m1_hbm, m1, isem.at[5])
    m2_in = local(m2_hbm, m2, isem.at[6])

    barrier = pltpu.get_barrier_semaphore()

    def greet(dev):
        pl.semaphore_signal(barrier, inc=1, device_id=dev, device_id_type=MESH)

    greet((mate, t))
    for k in range(1, nqx):
        greet(dev_x(k))
    for k in range(1, nqy):
        greet(dev_y(k))
    met = 1 + (nqx - 1) + (nqy - 1)
    if nt > 4:
        for k in range(1, nt):
            greet((dp, (t + k) % nt))
        pl.semaphore_wait(barrier, met + nt - 1)
    else:
        pl.when(t >= 1)(lambda: greet((dp, t - 1)))
        pl.when(t + 1 < nt)(lambda: greet((dp, t + 1)))
        pl.semaphore_wait(barrier, met + jnp.where(t >= 1, 1, 0) + jnp.where(t + 1 < nt, 1, 0))


    na = nqx + nqy - 2
    nx1 = (nqx - 1) * nqy
    ny1 = (nqy - 1) * nqx
    nw2 = nx1 + ny1
    own.wait()
    for k in range(1, nqx):
        remote(wf.at[t, my_rows, hcol[0]], wf.at[t, my_rows, hcol[0]], a1s, a1r, dev_x(k))
    for k in range(1, nqy):
        remote(wf.at[t, my_rows, hcol[1]], wf.at[t, my_rows, hcol[1]], a1s, a1r, dev_y(k))
    sent.append((chunks(na), a1s))

    def spread(i, near=(False, True)):
        b = block(i)
        for h, count, other, dev in ((0, nqx, nqy, dev_y), (1, nqy, nqx, dev_x)):
            for k in range(1, other):
                for m in range(count):
                    place = slot(qy, pos_x(m)) if h == 0 else slot(pos_y(m), qx)
                    if (m == 0) in near:
                        part = wf.at[b, place, hcol[h]]
                        remote(part, part, b4s if i == nt - 1 else b3s, b3r.at[i], dev(k))

    sent.append((wg.at[pl.ds(0, nt - 1), pl.ds(0, nw2 * rows), hcol[0]], b3s))
    sent.append((chunks(nw2 - na), b4s))
    spread(0, (True,))

    def line_pieces(b, side, p, dev):
        if p == 0:
            parts = [wf.at[b, my_rows]]
        else:
            parts = [wf.at[b, slot(qy, pos_x(k)), hcol[0]] for k in range(1, nqx)]
            parts += [wf.at[b, slot(pos_y(k), qx), hcol[1]] for k in range(1, nqy)]
        return [describe(part, part, zfs.at[side, b], zfr.at[b, p], dev) for part in parts]

    def pass_on(b, side, p):
        to, there = (t + 1, t + 1 < nt) if side == 0 else (t - 1, t >= 1)

        @pl.when(there)
        def _():
            for copy in line_pieces(b, side, p, (dp, to)):
                copy.start()

    line_sent = [(0, t, t >= 0), (1, t, t >= 0)]

    def relay(d, p):
        for side, b, here in ((0, t - d, t - d >= 0), (1, t + d, t + d < nt)):
            @pl.when(here)
            def _(side=side, b=b):
                arrived(chunks(2 if p == 0 else na), zfr.at[b, p])
                pass_on(b, side, p)

            if p == 0:
                line_sent.append((side, b, here))

    for side, to, there in ((0, t + 1, t + 1 < nt), (1, t - 1, t >= 1)):
        @pl.when(there)
        def _(side=side, to=to):
            describe(wf.at[t, my_rows], wf.at[t, my_rows], zfs.at[side, t], zfr.at[t, 0], (dp, to)).start()

    def other_parts(b):
        parts = [wf.at[b, slot(pos_y(k), qx), hcol[0]] for k in range(1, nqy)]
        return parts + [wf.at[b, slot(qy, pos_x(k)), hcol[1]] for k in range(1, nqx)]

    half_line = nt // 2
    middle_low = t == half_line - 1
    middle_high = t == half_line

    def cross_over():
        for here, b, far in (
            (middle_low, 0, [half_line + n for n in range(half_line)]),
            (middle_high, nt - 1, [half_line - 1 - n for n in range(half_line)]),
        ):
            @pl.when(here)
            def _(b=b, far=far):
                for n, to in enumerate(far):
                    for part in other_parts(b):
                        remote(part, part, p2s.at[n], p2r, (dp, to))

    def crossed_over():
        @pl.when(jnp.logical_or(middle_low, middle_high))
        def _():
            for n in range(half_line):
                left(chunks(na), p2s.at[n])

    def gather_third(i):
        if i == nt - 1:
            arrived(chunks(na), p2r)
            arrived(chunks(nw2 - na), b3r.at[i])
        else:
            arrived(chunks(nw2), b3r.at[i])
        if i == nt - 3 and i > 1:
            cross_over()
        part = wf.at[block(i), pl.ds(mine, half)]
        remote(part, part, a3s, a3r.at[i], (mate, t))

    sent.append((wg.at[:, pl.ds(0, half)], a3s))

    cross[...] = jnp.zeros_like(cross)
    kg_in.wait()
    pos_in.wait()
    freq_in.wait()
    hh = HEAD // 2
    turn = jnp.broadcast_to(freq[...], (128, 128)).T[:hh, :tile]
    for k in range(ntile):
        lanes = pl.ds(k * tile, tile)
        angle = turn * pos[k : k + 1, :].astype(F32)
        cosine = jnp.cos(angle)
        sine = jnp.sin(angle)
        turned = kg[pl.ds(k * tile, tile), :].astype(F32).T
        for h in range(KV_HEADS):
            a = turned[h * HEAD : h * HEAD + hh]
            b = turned[h * HEAD + hh : (h + 1) * HEAD]
            for p, value in enumerate((a * cosine + b * sine, b * cosine - a * sine)):
                value = value.astype(BF16)
                for m in range(hh // rows):
                    n = (h * HEAD + p * hh) // rows + m
                    kbt[pl.ds((n % 2) * half + (n // 2) * rows, rows), lanes] = value[
                        m * rows : (m + 1) * rows
                    ]

    def sum_squares(k):
        x_in[k].wait()

        @pl.loop(0, tile // 16)
        def _(g):
            r = pl.ds(pl.multiple_of(k * tile + g * 16, 16), 16)
            total = None
            for b in range(width // 512):
                v = x[r, b * 512 : (b + 1) * 512].astype(F32)
                v = v * v
                v = (v[:, :128] + v[:, 128:256]) + (v[:, 256:384] + v[:, 384:])
                total = v if total is None else total + v
            ssq[r, :] = total

        lanes = pl.ds(k * tile, tile)
        mean = jnp.sum(ssq[lanes, :].T, axis=0, keepdims=True) / width
        sks[:, lanes] = (kbt[:, lanes].astype(F32) * lax.rsqrt(mean + eps_norm)).astype(BF16)

    for k in range(ntile):
        sum_squares(k)

    gain_copy.wait()
    for k in range(width // 128):
        gain[:, k * 128 : (k + 1) * 128] = gain_in[k : k + 1, :].astype(F32)

    sent.append((wg.at[:, pl.ds(0, half)], cs))

    def product(i, h, n, first=0, size=hc):
        j = dest(i)
        step = min(cc, size)

        @pl.loop(0, size // step)
        def _(m):
            off = pl.ds(pl.multiple_of(h * hc + first + m * step, step), step)
            col = pl.ds(pl.multiple_of(j * cols + h * hc + first + m * step, step), step)
            total = jnp.dot(sks[...], x[:, col], preferred_element_type=F32)
            wg[j, :, off] = (total * gain[:, col]).astype(BF16)

        part = pl.ds(h * hc + first, size)
        remote(wg.at[j, pl.ds(theirs, half), part], rcore.at[j, :, part], cs, cr.at[n], (mate, t))

    def pair_sum(i, h, n, first=0, size=hc):
        j = dest(i)
        part = pl.ds(h * hc + first, size)
        arrived(rcore.at[j, :, part], cr.at[n])

        @pl.loop(0, half // 16)
        def _(g):
            r = pl.ds(pl.multiple_of(mine + g * 16, 16), 16)
            l = pl.ds(pl.multiple_of(g * 16, 16), 16)
            a = wg[j, r, part].astype(F32) + rcore[j, l, part].astype(F32)
            wg[j, r, part] = a.astype(BF16)

    def reduce_first(i, h, first=0, size=hc):
        j = dest(i)
        if h == 0:
            for k in range(1, nqx):
                for yy in range(nqy):
                    n = (k - 1) * nqy + yy
                    src = wg.at[j, slot(yy, pos_x(k)), pl.ds(first, size)]
                    remote(src, r1a.at[i, n, :, pl.ds(first, size)], qs, qr.at[i, 0], dev_x(k))
        else:
            for k in range(1, nqy):
                src = wg.at[j, band(pos_y(k)), pl.ds(hc + first, size)]
                remote(src, r1b.at[i, k - 1, :, pl.ds(first, size)], qs, qr.at[i, 1], dev_y(k))

    sent.append((layers(nw2), qs))
    sent.append((layers(na), q2s))

    def middle(i, h):
        j = dest(i)
        arrived(chunks(ny1 if h else nx1), qr.at[i, h])
        if h == 0:
            @pl.loop(0, rows // 16)
            def _(g):
                l = pl.ds(pl.multiple_of(g * 16, 16), 16)
                for yy in range(nqy):
                    r = pl.ds(pl.multiple_of(mine + (yy * nqx + qx) * rows + g * 16, 16), 16)
                    a = wg[j, r, hcol[0]].astype(F32)
                    for k in range(nqx - 1):
                        a = a + r1a[i, k * nqy + yy, l, :].astype(F32)
                    wg[j, r, hcol[0]] = a.astype(BF16)

            for k in range(1, nqy):
                src = wg.at[j, slot(pos_y(k), qx), hcol[0]]
                remote(src, r2a.at[i, k - 1], q2s, q2r.at[i], dev_y(k))
        else:
            @pl.loop(0, nqx * rows // 16)
            def _(g):
                l = pl.ds(pl.multiple_of(g * 16, 16), 16)
                r = pl.ds(pl.multiple_of(mine + qy * nqx * rows + g * 16, 16), 16)
                a = wg[j, r, hcol[1]].astype(F32)
                for k in range(nqy - 1):
                    a = a + r1b[i, k, l, :].astype(F32)
                wg[j, r, hcol[1]] = a.astype(BF16)

            for k in range(1, nqx):
                src = wg.at[j, slot(qy, pos_x(k)), hcol[1]]
                remote(src, r2b.at[i, k - 1], q2s, q2r.at[i], dev_x(k))

    sent.append((zs, zsd))

    def final(i):
        j = dest(i)
        arrived(chunks(na), q2r.at[i])

        @pl.loop(0, rows // 16)
        def _(g):
            r = pl.ds(pl.multiple_of(g * 16, 16), 16)
            m = pl.ds(pl.multiple_of(mine + q * rows + g * 16, 16), 16)
            for part, other, count in ((hcol[0], r2a, nqy - 1), (hcol[1], r2b, nqx - 1)):
                a = wg[j, m, part].astype(F32)
                for k in range(count):
                    a = a + other[i, k, r, :].astype(F32)
                if i < nt - 1:
                    zs[i, r, part] = a.astype(BF16)
                else:
                    gsum[r, part] = a

        if i < nt - 1:
            remote(zs.at[i], rz.at[i], zsd, zr, (dp, j))

    uc = min(256, cols)

    def upstream(i):
        b = block(i)
        arrived(wf.at[b, pl.ds(mine, half)], a3r.at[i])

        @pl.loop(0, cols // uc)
        def _(h):
            off = pl.ds(pl.multiple_of(h * uc, uc), uc)
            col = pl.ds(pl.multiple_of(b * cols + h * uc, uc), uc)
            u = jnp.dot(kb[...], wf[b, :, off], preferred_element_type=F32) * gain[:, col]
            scale = ssq[...]
            u = jnp.concatenate([u[:, n * 128 : (n + 1) * 128] * scale for n in range(uc // 128)], axis=1)
            grad[:, col] = u.astype(BF16)
            p = u * x[:, col].astype(F32)
            total = p[:, :128]
            for n in range(1, uc // 128):
                total = total + p[:, n * 128 : (n + 1) * 128]
            cross[...] += total

    def turn_back():
        for k in range(ntile):
            lanes = pl.ds(k * tile, tile)
            kb[lanes, :] = kbt[:, lanes].astype(F32).T.astype(BF16)
            mean = jnp.sum(ssq[lanes, :], axis=1, keepdims=True) / width
            ssq[lanes, :] = jnp.broadcast_to(lax.rsqrt(mean + eps_norm), (tile, 128))

    hq = hc // 2
    units = [(0, 0, 0, 0, hq), (0, 1, 1, 0, hq), (0, 0, 2 * nt, hq, hq), (0, 1, 2 * nt + 1, hq, hq)]
    units += [(i, h, i * 2 + h) for i in range(1, nt) for h in range(2)]
    early = min(6, len(units))
    for n, unit in enumerate(units):
        product(*unit)
        if n == len(units) - 1:
            relay(1, 1)
        for m in {0: (), 1: (), 2: (), 3: (0, 1, 2, 3), 4: ()}.get(n, (n - 1,)):
            pair_sum(*units[m])
            if m < early:
                reduce_first(*units[m][:2], *units[m][3:])
        if n == 3:
            arrived(chunks(na), a1r)
            pass_on(t, 0, 1)
            pass_on(t, 1, 1)
        if n == early:
            relay(1, 0)
    pair_sum(*units[-1])
    turn_back()

    def both_middle(i):
        middle(i, 0)
        middle(i, 1)
        if i + 2 < nt:
            reduce_first(i + 2, 0)
            reduce_first(i + 2, 1)

    both_middle(0)
    both_middle(1)
    final(0)
    if nt > 3:
        relay(2, 0)
    for i in range(2, nt):
        both_middle(i)
        if i == nt - 1:
            spread(1)
            spread(0, (False,))
        final(i - 1)
        if 2 < i < nt - 1:
            relay(i - 1, 1)
            relay(i, 0)
    final(nt - 1)
    arrived(rz, zr)

    wide = min(512, cols)
    squares = jnp.zeros((16, 128), F32)
    for g in range(rows // 16):
        for part in range(cols // wide):
            r, col = slice(g * 16, (g + 1) * 16), slice(part * wide, (part + 1) * wide)
            a = gsum[r, col]
            for i in range(nt - 1):
                a = a + rz[i, r, col].astype(F32)
            gsum[r, col] = a
            a = a * a
            for k in range(wide // 128):
                squares = squares + a[:, k * 128 : (k + 1) * 128]
    nsend[...] = jnp.sum(squares, axis=0, keepdims=True)

    n = 0
    for b in reversed(range(nt)):
        for a in range(ndp):
            if a or b:
                remote(nsend, nrecv.at[n], nss, nsr, ((dp + a) % ndp, (t + b) % nt))
                n += 1
    sent.append((nrecv, nss))
    if nt > 3:
        relay(nt - 2, 1)
    gather_third(1)
    if nt - 3 == 1:
        cross_over()
    for i in range(2, nt - 1):
        spread(i)
    gather_third(0)
    upstream(1)
    arrived(nrecv, nsr)
    v = nsend[...] + jnp.sum(nrecv[...], axis=0)
    total_square = jnp.sum(v, axis=1, keepdims=True)
    limit = math.sqrt(kbt.shape[0] * width)
    clip = jnp.minimum(1.0, limit / (jnp.sqrt(total_square) + 1e-06))
    nat = pl.multiple_of(c * rows, rows)
    m1_in.wait()
    m2_in.wait()

    @pl.loop(0, rows // 16)
    def _(g):
        r = pl.ds(pl.multiple_of(g * 16, 16), 16)
        wr_ = pl.ds(pl.multiple_of(mine + q * rows + g * 16, 16), 16)
        to = pl.ds(pl.multiple_of(nat + g * 16, 16), 16)
        for part in range(cols // wide):
            col = slice(part * wide, (part + 1) * wide)
            clipped = gsum[r, col] * clip
            new_first = beta_one * m1[r, col] + (1.0 - beta_one) * clipped
            new_second = beta_two * m2[r, col] + (1.0 - beta_two) * clipped * clipped
            nf[r, col] = new_first
            ns[r, col] = new_second
            nwb[q, to, col] = (
                wf[t, wr_, col].astype(F32) * (1.0 - learn_rate * decay_rate)
                - learn_rate * new_first / (jnp.sqrt(new_second) + eps_adam)
            ).astype(BF16)

    def piece_of(yy, xx, part):
        return nwb.at[yy * nqx + xx, pl.ds(nat, rows), part]

    for k in range(1, nqx):
        part = piece_of(qy, qx, hcol[0])
        remote(part, part, ws, wr, dev_x(k))
    for k in range(1, nqy):
        part = piece_of(qy, qx, hcol[1])
        remote(part, part, ws, wr, dev_y(k))
    sent.append((chunks(na), ws))

    upstream(0)
    relay(nt - 1, 0)
    relay(nt - 1, 1)
    spread(nt - 1, (False,))
    for i in range(2, nt - 1):
        gather_third(i)
        if i < nt - 2:
            upstream(i)

    arrived(chunks(na), wr)
    for m in range(max(nqx, nqy)):
        for k in range(1, nqy if m < nqx else 1):
            part = piece_of(qy, pos_x(m), hcol[0])
            remote(part, part, vs, vr.at[min(m, 1)], dev_y(k))
        for k in range(1, nqx if m < nqy else 1):
            part = piece_of(pos_y(m), qx, hcol[1])
            remote(part, part, vs, vr.at[min(m, 1)], dev_x(k))
    sent.append((chunks(nw2), vs))
    early_parts = [(qy, pos_x(m), hcol[0]) for m in range(nqx)] + [(pos_y(m), qx, hcol[1]) for m in range(nqy)]
    for place in early_parts:
        part = piece_of(*place)
        remote(part, part, us, ur, (mate, t))
    upstream(nt - 2)
    gather_third(nt - 1)
    upstream(nt - 1)

    for k in range(ntile):
        lanes = pl.ds(k * tile, tile)
        down = ssq[lanes, :1] * (jnp.sum(cross[lanes, :], axis=1, keepdims=True) / width)
        cross[lanes, :] = jnp.broadcast_to(down, (tile, 128))

    for late, count in ((0, na), (1, nw2 - na)):
        arrived(chunks(count), vr.at[late])
        late_parts = [
            (pos_y(k), pos_x(m), hcol[0]) for k in range(1, nqy) for m in range(nqx) if min(m, 1) == late
        ]
        late_parts += [
            (pos_y(m), pos_x(k), hcol[1]) for k in range(1, nqx) for m in range(nqy) if min(m, 1) == late
        ]
        for place in late_parts:
            part = piece_of(*place)
            remote(part, part, us, ur, (mate, t))
    whole = nwb.at[:, pl.ds(nat, rows)]
    sent.append((whole, us))
    arrived(whole, ur)
    for like, sem in sent:
        left(like, sem)
    crossed_over()
    for side, b, here in line_sent:
        there = t + 1 < nt if side == 0 else t >= 1

        @pl.when(jnp.logical_and(here, there))
        def _(side=side, b=b):
            left(chunks(2 + na), zfs.at[side, b])


def write_out(grad, x, down, nwb, nf, ns, grad_out, nw_out, nf_out, ns_out, done, sem, gsem):
    tokens, width = x.shape
    tile = min(32, tokens)
    small = [
        pltpu.make_async_copy(src, dst, sem.at[n])
        for n, (src, dst) in enumerate(((nwb, nw_out), (nf, nf_out), (ns, ns_out)))
    ]
    for copy in small:
        copy.start()
    copies = list(small)
    for k in range(tokens // tile):
        @pl.loop(0, tile // 16)
        def _(g):
            r = pl.ds(pl.multiple_of(k * tile + g * 16, 16), 16)
            factor = down[r, :]
            for n in range(width // 128):
                col = slice(n * 128, (n + 1) * 128)
                done[r, col] = (grad[r, col].astype(F32) - factor * x[r, col].astype(F32)).astype(BF16)

        piece = pl.ds(k * tile, tile)
        copy = pltpu.make_async_copy(done.at[piece], grad_out.at[piece], gsem.at[k])
        copy.start()
        copies.append(copy)
    for copy in copies:
        copy.wait()


def body(ndp, nt, norm_input, key_grad, positions, norm_gain, key_weight, first_moment, second_moment):
    rows, cols = key_weight.shape
    tokens, width = norm_input.shape
    nq = ndp // 2
    features = ndp * rows
    tile = min(128, tokens)
    ntile = tokens // tile
    hh = HEAD // 2
    frequency = ROPE_BASE ** (-(2.0 * np.arange(hh)) / HEAD)
    frequency = np.resize(frequency.astype(np.float32), (1, 128))
    any_spec = pl.BlockSpec(memory_space=pl.ANY)
    vmem = pl.BlockSpec(memory_space=pltpu.VMEM)
    dma = pltpu.SemaphoreType.DMA
    nqx = math.isqrt(nq)
    while nq % nqx:
        nqx -= 1
    nqy = nq // nqx
    hc = cols // 2
    na = nqx + nqy - 2
    nx1 = (nqx - 1) * nqy
    nw2 = nx1 + (nqy - 1) * nqx
    nn = ndp * nt - 1
    scratch = [
        pltpu.VMEM((tokens, features), BF16),
        pltpu.VMEM((ntile, tile), jnp.int32),
        pltpu.VMEM((width // 128, 128), BF16),
        pltpu.VMEM((1, 128), F32),
        pltpu.VMEM((rows, cols), F32),
        pltpu.VMEM((rows, cols), F32),
        pltpu.VMEM((1, width), F32),
        pltpu.VMEM((tokens, features), BF16),
        pltpu.VMEM((features, tokens), BF16),
        pltpu.VMEM((features, tokens), BF16),
        pltpu.VMEM((tokens, 128), F32),
        pltpu.VMEM((nt, features, cols), BF16),
        pltpu.VMEM((nt, features, cols), BF16),
        pltpu.VMEM((nt, nq * rows, cols), BF16),
        pltpu.VMEM((nt, nx1, rows, hc), BF16),
        pltpu.VMEM((nt, nqy - 1, nqx * rows, hc), BF16),
        pltpu.VMEM((nt, nqy - 1, rows, hc), BF16),
        pltpu.VMEM((nt, nqx - 1, rows, hc), BF16),
        pltpu.VMEM((nt - 1, rows, cols), BF16),
        pltpu.VMEM((nt - 1, rows, cols), BF16),
        pltpu.VMEM((rows, cols), F32),
        pltpu.VMEM((1, 128), F32),
        pltpu.VMEM((nn, 1, 128), F32),
        dma((7,)), dma((ntile,)),
        dma, dma,
        dma((2, nt)), dma((nt, 2)),
        dma, dma((nt,)), dma,
        dma((nt // 2,)), dma,
        dma, dma((nt,)),
        dma, dma((2 * nt + 2,)),
        dma, dma((nt, 2)),
        dma, dma((nt,)),
        dma, dma,
        dma, dma,
        dma, dma,
        dma, dma((2,)),
        dma, dma,
    ]
    results = pl.pallas_call(
        functools.partial(kernel, ndp, nt, nqx),
        out_shape=(
            pltpu.VMEM((tokens, width), BF16),
            pltpu.VMEM((tokens, width), BF16),
            pltpu.VMEM((tokens, 128), F32),
            pltpu.VMEM((nq, 2 * rows, cols), BF16),
            pltpu.VMEM((rows, cols), F32),
            pltpu.VMEM((rows, cols), F32),
        ),
        in_specs=[any_spec] * 8,
        out_specs=(vmem,) * 6,
        scratch_shapes=scratch,
        compiler_params=pltpu.CompilerParams(
            collective_id=0, has_side_effects=True, vmem_limit_bytes=42 * 2**20
        ),
    )(
        norm_input, key_grad, positions.reshape(ntile, tile), norm_gain.reshape(width // 128, 128),
        jnp.asarray(frequency), key_weight, first_moment, second_moment,
    )
    results = [pltpu.with_memory_space_constraint(r, pltpu.VMEM) for r in results]
    input_grad, new_weight, new_first, new_second = pl.pallas_call(
        write_out,
        out_shape=[jax.ShapeDtypeStruct(results[n].shape, results[n].dtype) for n in (0, 3, 4, 5)],
        in_specs=[vmem] * 6,
        out_specs=[any_spec] * 4,
        scratch_shapes=[pltpu.VMEM((tokens, width), BF16), dma((3,)), dma((tokens // min(32, tokens),))],
        compiler_params=pltpu.CompilerParams(vmem_limit_bytes=10 * 2**20),
    )(*results)
    return (input_grad, new_weight.reshape(features, cols), new_first, new_second)


def solution(mesh):
    in_specs = (
        P(("dp", "tensor"), None),
        P(("dp", "tensor"), None),
        P(("dp", "tensor")),
        P(),
        P("dp", "tensor"),
        P("dp", "tensor"),
        P("dp", "tensor"),
    )
    out_specs = (P(("dp", "tensor"), None), P(None, "tensor"), P("dp", "tensor"), P("dp", "tensor"))
    return jax.shard_map(
        functools.partial(body, mesh.shape["dp"], mesh.shape["tensor"]),
        mesh=mesh, in_specs=in_specs, out_specs=out_specs, check_vma=False,
    )
```

```python
import functools
import math

import jax
import jax.numpy as jnp
import numpy as np
from jax import lax
from jax.experimental import pallas as pl
from jax.experimental.pallas import tpu as pltpu
from jax.sharding import PartitionSpec as P

KV_HEADS = 4
HEAD = 128
ROPE_BASE = 500000.0

eps_norm = 1e-05
beta_one = 0.9
beta_two = 0.95
learn_rate = 0.0003
decay_rate = 0.1
eps_adam = 1e-08

MESH = pl.DeviceIdType.MESH
F32 = jnp.float32
BF16 = jnp.bfloat16


def kernel(
    ndp, nt, nqx, x_hbm, kg_hbm, pos_hbm, gain_hbm, freq_hbm, w_hbm, m1_hbm, m2_hbm,
    grad, x, cross, nwb, nf, ns,
    kg, pos, gain_in, freq, m1, m2, gain, kb, kbt, sks, ssq,
    wf, wg, rcore, r1a, r1b, r2a, r2b, zs, rz, gsum, nsend, nrecv,
    isem, xsem, a1s, a1r, zfs, zfr, b3s, b3r, b4s, p2s, p2r, a3s, a3r, cs, cr, qs, qr, q2s, q2r,
    zsd, zr, nss, nsr, ws, wr, vs, vr, us, ur,
):
    nq = ndp // 2
    nqy = nq // nqx
    rows, cols = w_hbm.shape
    half = nq * rows
    tokens, width = x.shape
    tile = min(128, tokens)
    ntile = tokens // tile
    hc = cols // 2
    cc = min(512, hc)
    hcol = (pl.ds(0, hc), pl.ds(hc, hc))
    dp = lax.axis_index("dp")
    t = lax.axis_index("tensor")
    c = dp % 2
    q = dp // 2
    qy = q // nqx
    qx = q % nqx
    mate = q * 2 + (1 - c)
    mine = pl.multiple_of(c * half, half)
    theirs = pl.multiple_of((1 - c) * half, half)
    sent = []

    def describe(src, dst, ssem, rsem, dev):
        return pltpu.make_async_remote_copy(
            src_ref=src, dst_ref=dst, send_sem=ssem, recv_sem=rsem, device_id=dev, device_id_type=MESH
        )

    def remote(src, dst, ssem, rsem, dev):
        describe(src, dst, ssem, rsem, dev).start()

    def arrived(like, rsem):
        describe(like, like, a1s, rsem, (mate, t)).wait_recv()

    def left(like, ssem):
        describe(like, like, ssem, a1r, (mate, t)).wait_send()

    def chunks(n):
        return wg.at[0, pl.ds(0, n * rows), hcol[0]]

    def layers(n):
        return wg.at[:, pl.ds(0, n * rows), hcol[0]]

    def pos_x(k):
        return (qx + k) % nqx

    def pos_y(k):
        return (qy + k) % nqy

    def dev_x(k):
        return ((qy * nqx + pos_x(k)) * 2 + c, t)

    def dev_y(k):
        return ((pos_y(k) * nqx + qx) * 2 + c, t)

    def slot(yy, xx):
        return pl.ds(pl.multiple_of(mine + (yy * nqx + xx) * rows, rows), rows)

    def band(yy):
        return pl.ds(pl.multiple_of(mine + yy * nqx * rows, nqx * rows), nqx * rows)

    my_rows = slot(qy, qx)
    steps = sorted(range(1, nt), key=lambda o: (-min(o, nt - o), o)) + [0]

    def dest(i):
        return (t + steps[i]) % nt

    near = jnp.minimum(t, nt - 1 - t)
    low = t < nt - 1 - t

    def block(i):
        if i == 0:
            return t
        d = (i + 1) // 2
        both = t + (d if i % 2 else -d) * jnp.where(low, -1, 1)
        return jnp.where(i <= 2 * near, both, jnp.where(low, i, nt - 1 - i))

    def local(src, dst, sem):
        copy = pltpu.make_async_copy(src, dst, sem)
        copy.start()
        return copy

    own = local(w_hbm, wf.at[t, my_rows], isem.at[0])
    kg_in = local(kg_hbm, kg, isem.at[1])
    pos_in = local(pos_hbm, pos, isem.at[2])
    freq_in = local(freq_hbm, freq, isem.at[3])
    gain_copy = local(gain_hbm, gain_in, isem.at[4])
    x_in = []
    for k in range(ntile):
        piece = pl.ds(k * tile, tile)
        x_in.append(local(x_hbm.at[piece], x.at[piece], xsem.at[k]))
    m1_in = local(m1_hbm, m1, isem.at[5])
    m2_in = local(m2_hbm, m2, isem.at[6])

    barrier = pltpu.get_barrier_semaphore()

    def greet(dev):
        pl.semaphore_signal(barrier, inc=1, device_id=dev, device_id_type=MESH)

    greet((mate, t))
    for k in range(1, nqx):
        greet(dev_x(k))
    for k in range(1, nqy):
        greet(dev_y(k))
    met = 1 + (nqx - 1) + (nqy - 1)
    if nt > 4:
        for k in range(1, nt):
            greet((dp, (t + k) % nt))
        pl.semaphore_wait(barrier, met + nt - 1)
    else:
        pl.when(t >= 1)(lambda: greet((dp, t - 1)))
        pl.when(t + 1 < nt)(lambda: greet((dp, t + 1)))
        pl.semaphore_wait(barrier, met + jnp.where(t >= 1, 1, 0) + jnp.where(t + 1 < nt, 1, 0))


    na = nqx + nqy - 2
    nx1 = (nqx - 1) * nqy
    ny1 = (nqy - 1) * nqx
    nw2 = nx1 + ny1
    own.wait()
    for k in range(1, nqx):
        remote(wf.at[t, my_rows, hcol[0]], wf.at[t, my_rows, hcol[0]], a1s, a1r, dev_x(k))
    for k in range(1, nqy):
        remote(wf.at[t, my_rows, hcol[1]], wf.at[t, my_rows, hcol[1]], a1s, a1r, dev_y(k))
    sent.append((chunks(na), a1s))

    def spread(i, near=(False, True)):
        b = block(i)
        for h, count, other, dev in ((0, nqx, nqy, dev_y), (1, nqy, nqx, dev_x)):
            for k in range(1, other):
                for m in range(count):
                    place = slot(qy, pos_x(m)) if h == 0 else slot(pos_y(m), qx)
                    if (m == 0) in near:
                        part = wf.at[b, place, hcol[h]]
                        remote(part, part, b4s if i == nt - 1 else b3s, b3r.at[i], dev(k))

    sent.append((wg.at[pl.ds(0, nt - 1), pl.ds(0, nw2 * rows), hcol[0]], b3s))
    sent.append((chunks(nw2 - na), b4s))
    spread(0, (True,))

    def line_pieces(b, side, p, dev):
        if p == 0:
            parts = [wf.at[b, my_rows]]
        else:
            parts = [wf.at[b, slot(qy, pos_x(k)), hcol[0]] for k in range(1, nqx)]
            parts += [wf.at[b, slot(pos_y(k), qx), hcol[1]] for k in range(1, nqy)]
        return [describe(part, part, zfs.at[side, b], zfr.at[b, p], dev) for part in parts]

    def pass_on(b, side, p):
        to, there = (t + 1, t + 1 < nt) if side == 0 else (t - 1, t >= 1)

        @pl.when(there)
        def _():
            for copy in line_pieces(b, side, p, (dp, to)):
                copy.start()

    line_sent = [(0, t, t >= 0), (1, t, t >= 0)]

    def relay(d, p):
        for side, b, here in ((0, t - d, t - d >= 0), (1, t + d, t + d < nt)):
            @pl.when(here)
            def _(side=side, b=b):
                arrived(chunks(2 if p == 0 else na), zfr.at[b, p])
                pass_on(b, side, p)

            if p == 0:
                line_sent.append((side, b, here))

    for side, to, there in ((0, t + 1, t + 1 < nt), (1, t - 1, t >= 1)):
        @pl.when(there)
        def _(side=side, to=to):
            describe(wf.at[t, my_rows], wf.at[t, my_rows], zfs.at[side, t], zfr.at[t, 0], (dp, to)).start()

    def other_parts(b):
        parts = [wf.at[b, slot(pos_y(k), qx), hcol[0]] for k in range(1, nqy)]
        return parts + [wf.at[b, slot(qy, pos_x(k)), hcol[1]] for k in range(1, nqx)]

    half_line = nt // 2
    middle_low = t == half_line - 1
    middle_high = t == half_line

    def cross_over():
        for here, b, far in (
            (middle_low, 0, [half_line + n for n in range(half_line)]),
            (middle_high, nt - 1, [half_line - 1 - n for n in range(half_line)]),
        ):
            @pl.when(here)
            def _(b=b, far=far):
                for n, to in enumerate(far):
                    for part in other_parts(b):
                        remote(part, part, p2s.at[n], p2r, (dp, to))

    def crossed_over():
        @pl.when(jnp.logical_or(middle_low, middle_high))
        def _():
            for n in range(half_line):
                left(chunks(na), p2s.at[n])

    def gather_third(i):
        if i == nt - 1:
            arrived(chunks(na), p2r)
            arrived(chunks(nw2 - na), b3r.at[i])
        else:
            arrived(chunks(nw2), b3r.at[i])
        if i == nt - 3 and i > 1:
            cross_over()
        part = wf.at[block(i), pl.ds(mine, half)]
        remote(part, part, a3s, a3r.at[i], (mate, t))

    sent.append((wg.at[:, pl.ds(0, half)], a3s))

    gain_copy.wait()
    for k in range(width // 128):
        gain[:, k * 128 : (k + 1) * 128] = gain_in[k : k + 1, :].astype(F32)

    cross[...] = jnp.zeros_like(cross)
    kg_in.wait()
    pos_in.wait()
    freq_in.wait()
    hh = HEAD // 2
    turn = jnp.broadcast_to(freq[...], (128, 128)).T[:hh, :tile]
    for k in range(ntile):
        lanes = pl.ds(k * tile, tile)
        angle = turn * pos[k : k + 1, :].astype(F32)
        cosine = jnp.cos(angle)
        sine = jnp.sin(angle)
        turned = kg[pl.ds(k * tile, tile), :].astype(F32).T
        for h in range(KV_HEADS):
            a = turned[h * HEAD : h * HEAD + hh]
            b = turned[h * HEAD + hh : (h + 1) * HEAD]
            for p, value in enumerate((a * cosine + b * sine, b * cosine - a * sine)):
                value = value.astype(BF16)
                for m in range(hh // rows):
                    n = (h * HEAD + p * hh) // rows + m
                    kbt[pl.ds((n % 2) * half + (n // 2) * rows, rows), lanes] = value[
                        m * rows : (m + 1) * rows
                    ]

    def sum_squares(k):
        x_in[k].wait()

        @pl.loop(0, tile // 16)
        def _(g):
            r = pl.ds(pl.multiple_of(k * tile + g * 16, 16), 16)
            total = None
            for b in range(width // 512):
                v = x[r, b * 512 : (b + 1) * 512].astype(F32)
                v = v * v
                v = (v[:, :128] + v[:, 128:256]) + (v[:, 256:384] + v[:, 384:])
                total = v if total is None else total + v
            ssq[r, :] = total

        lanes = pl.ds(k * tile, tile)
        mean = jnp.sum(ssq[lanes, :].T, axis=0, keepdims=True) / width
        sks[:, lanes] = (kbt[:, lanes].astype(F32) * lax.rsqrt(mean + eps_norm)).astype(BF16)

    for k in range(ntile):
        sum_squares(k)

    sent.append((wg.at[:, pl.ds(0, half)], cs))

    def product(i, h, n, first=0, size=hc):
        j = dest(i)
        step = min(cc, size)

        @pl.loop(0, size // step)
        def _(m):
            off = pl.ds(pl.multiple_of(h * hc + first + m * step, step), step)
            col = pl.ds(pl.multiple_of(j * cols + h * hc + first + m * step, step), step)
            total = jnp.dot(sks[...], x[:, col], preferred_element_type=F32)
            wg[j, :, off] = (total * gain[:, col]).astype(BF16)

        part = pl.ds(h * hc + first, size)
        remote(wg.at[j, pl.ds(theirs, half), part], rcore.at[j, :, part], cs, cr.at[n], (mate, t))

    def pair_sum(i, h, n, first=0, size=hc):
        j = dest(i)
        part = pl.ds(h * hc + first, size)
        arrived(rcore.at[j, :, part], cr.at[n])

        @pl.loop(0, half // 16)
        def _(g):
            r = pl.ds(pl.multiple_of(mine + g * 16, 16), 16)
            l = pl.ds(pl.multiple_of(g * 16, 16), 16)
            a = wg[j, r, part].astype(F32) + rcore[j, l, part].astype(F32)
            wg[j, r, part] = a.astype(BF16)

    def reduce_first(i, h, first=0, size=hc):
        j = dest(i)
        if h == 0:
            for k in range(1, nqx):
                for yy in range(nqy):
                    n = (k - 1) * nqy + yy
                    src = wg.at[j, slot(yy, pos_x(k)), pl.ds(first, size)]
                    remote(src, r1a.at[i, n, :, pl.ds(first, size)], qs, qr.at[i, 0], dev_x(k))
        else:
            for k in range(1, nqy):
                src = wg.at[j, band(pos_y(k)), pl.ds(hc + first, size)]
                remote(src, r1b.at[i, k - 1, :, pl.ds(first, size)], qs, qr.at[i, 1], dev_y(k))

    sent.append((layers(nw2), qs))
    sent.append((layers(na), q2s))

    def middle(i, h):
        j = dest(i)
        arrived(chunks(ny1 if h else nx1), qr.at[i, h])
        if h == 0:
            @pl.loop(0, rows // 16)
            def _(g):
                l = pl.ds(pl.multiple_of(g * 16, 16), 16)
                for yy in range(nqy):
                    r = pl.ds(pl.multiple_of(mine + (yy * nqx + qx) * rows + g * 16, 16), 16)
                    a = wg[j, r, hcol[0]].astype(F32)
                    for k in range(nqx - 1):
                        a = a + r1a[i, k * nqy + yy, l, :].astype(F32)
                    wg[j, r, hcol[0]] = a.astype(BF16)

            for k in range(1, nqy):
                src = wg.at[j, slot(pos_y(k), qx), hcol[0]]
                remote(src, r2a.at[i, k - 1], q2s, q2r.at[i], dev_y(k))
        else:
            @pl.loop(0, nqx * rows // 16)
            def _(g):
                l = pl.ds(pl.multiple_of(g * 16, 16), 16)
                r = pl.ds(pl.multiple_of(mine + qy * nqx * rows + g * 16, 16), 16)
                a = wg[j, r, hcol[1]].astype(F32)
                for k in range(nqy - 1):
                    a = a + r1b[i, k, l, :].astype(F32)
                wg[j, r, hcol[1]] = a.astype(BF16)

            for k in range(1, nqx):
                src = wg.at[j, slot(qy, pos_x(k)), hcol[1]]
                remote(src, r2b.at[i, k - 1], q2s, q2r.at[i], dev_x(k))

    sent.append((zs, zsd))

    def final(i):
        j = dest(i)
        arrived(chunks(na), q2r.at[i])

        @pl.loop(0, rows // 16)
        def _(g):
            r = pl.ds(pl.multiple_of(g * 16, 16), 16)
            m = pl.ds(pl.multiple_of(mine + q * rows + g * 16, 16), 16)
            for part, other, count in ((hcol[0], r2a, nqy - 1), (hcol[1], r2b, nqx - 1)):
                a = wg[j, m, part].astype(F32)
                for k in range(count):
                    a = a + other[i, k, r, :].astype(F32)
                if i < nt - 1:
                    zs[i, r, part] = a.astype(BF16)
                else:
                    gsum[r, part] = a

        if i < nt - 1:
            remote(zs.at[i], rz.at[i], zsd, zr, (dp, j))

    uc = min(256, cols)

    def upstream(i):
        b = block(i)
        arrived(wf.at[b, pl.ds(mine, half)], a3r.at[i])

        @pl.loop(0, cols // uc)
        def _(h):
            off = pl.ds(pl.multiple_of(h * uc, uc), uc)
            col = pl.ds(pl.multiple_of(b * cols + h * uc, uc), uc)
            u = jnp.dot(kb[...], wf[b, :, off], preferred_element_type=F32) * gain[:, col]
            scale = ssq[...]
            u = jnp.concatenate([u[:, n * 128 : (n + 1) * 128] * scale for n in range(uc // 128)], axis=1)
            grad[:, col] = u.astype(BF16)
            p = u * x[:, col].astype(F32)
            total = p[:, :128]
            for n in range(1, uc // 128):
                total = total + p[:, n * 128 : (n + 1) * 128]
            cross[...] += total

    def turn_back():
        for k in range(ntile):
            lanes = pl.ds(k * tile, tile)
            kb[lanes, :] = kbt[:, lanes].astype(F32).T.astype(BF16)
            mean = jnp.sum(ssq[lanes, :], axis=1, keepdims=True) / width
            ssq[lanes, :] = jnp.broadcast_to(lax.rsqrt(mean + eps_norm), (tile, 128))

    hq = hc // 2
    units = [(0, 0, 0, 0, hq), (0, 1, 1, 0, hq), (0, 0, 2 * nt, hq, hq), (0, 1, 2 * nt + 1, hq, hq)]
    units += [(i, h, i * 2 + h) for i in range(1, nt) for h in range(2)]
    early = min(6, len(units))
    for n, unit in enumerate(units):
        product(*unit)
        if n == len(units) - 1:
            relay(1, 1)
        for m in {0: (), 1: (), 2: (), 3: (0, 1, 2, 3), 4: ()}.get(n, (n - 1,)):
            pair_sum(*units[m])
            if m < early:
                reduce_first(*units[m][:2], *units[m][3:])
        if n == 3:
            arrived(chunks(na), a1r)
            pass_on(t, 0, 1)
            pass_on(t, 1, 1)
        if n == early:
            relay(1, 0)
    pair_sum(*units[-1])
    turn_back()

    def both_middle(i):
        middle(i, 0)
        middle(i, 1)
        if i + 2 < nt:
            reduce_first(i + 2, 0)
            reduce_first(i + 2, 1)

    both_middle(0)
    both_middle(1)
    final(0)
    if nt > 3:
        relay(2, 0)
    for i in range(2, nt):
        both_middle(i)
        if i == nt - 1:
            spread(1)
            spread(0, (False,))
        final(i - 1)
        if 2 < i < nt - 1:
            relay(i - 1, 1)
            relay(i, 0)
    final(nt - 1)
    arrived(rz, zr)

    nsend[...] = jnp.zeros_like(nsend)

    @pl.loop(0, rows // 16)
    def _(g):
        r = pl.ds(pl.multiple_of(g * 16, 16), 16)
        a = gsum[r, :]
        for i in range(nt - 1):
            a = a + rz[i, r, :].astype(F32)
        gsum[r, :] = a
        a = a * a
        total = a[:, :128]
        for k in range(1, cols // 128):
            total = total + a[:, k * 128 : (k + 1) * 128]
        nsend[...] += jnp.sum(total, axis=0, keepdims=True)

    n = 0
    for b in reversed(range(nt)):
        for a in range(ndp):
            if a or b:
                remote(nsend, nrecv.at[n], nss, nsr, ((dp + a) % ndp, (t + b) % nt))
                n += 1
    sent.append((nrecv, nss))
    if nt > 3:
        relay(nt - 2, 1)
    gather_third(1)
    if nt - 3 == 1:
        cross_over()
    for i in range(2, nt - 1):
        spread(i)
    gather_third(0)
    upstream(1)
    arrived(nrecv, nsr)
    v = nsend[...] + jnp.sum(nrecv[...], axis=0)
    total_square = jnp.sum(v, axis=1, keepdims=True)
    limit = math.sqrt(kbt.shape[0] * width)
    clip = jnp.minimum(1.0, limit / (jnp.sqrt(total_square) + 1e-06))
    nat = pl.multiple_of(c * rows, rows)
    m1_in.wait()
    m2_in.wait()

    @pl.loop(0, rows // 16)
    def _(g):
        r = pl.ds(pl.multiple_of(g * 16, 16), 16)
        wr_ = pl.ds(pl.multiple_of(mine + q * rows + g * 16, 16), 16)
        clipped = gsum[r, :] * clip
        new_first = beta_one * m1[r, :] + (1.0 - beta_one) * clipped
        new_second = beta_two * m2[r, :] + (1.0 - beta_two) * clipped * clipped
        nf[r, :] = new_first
        ns[r, :] = new_second
        nwb[q, pl.ds(pl.multiple_of(nat + g * 16, 16), 16), :] = (
            wf[t, wr_, :].astype(F32) * (1.0 - learn_rate * decay_rate)
            - learn_rate * new_first / (jnp.sqrt(new_second) + eps_adam)
        ).astype(BF16)

    def piece_of(yy, xx, part):
        return nwb.at[yy * nqx + xx, pl.ds(nat, rows), part]

    for k in range(1, nqx):
        part = piece_of(qy, qx, hcol[0])
        remote(part, part, ws, wr, dev_x(k))
    for k in range(1, nqy):
        part = piece_of(qy, qx, hcol[1])
        remote(part, part, ws, wr, dev_y(k))
    sent.append((chunks(na), ws))

    upstream(0)
    relay(nt - 1, 0)
    relay(nt - 1, 1)
    spread(nt - 1, (False,))
    for i in range(2, nt - 1):
        gather_third(i)
        if i < nt - 2:
            upstream(i)

    arrived(chunks(na), wr)
    for m in range(max(nqx, nqy)):
        for k in range(1, nqy if m < nqx else 1):
            part = piece_of(qy, pos_x(m), hcol[0])
            remote(part, part, vs, vr.at[min(m, 1)], dev_y(k))
        for k in range(1, nqx if m < nqy else 1):
            part = piece_of(pos_y(m), qx, hcol[1])
            remote(part, part, vs, vr.at[min(m, 1)], dev_x(k))
    sent.append((chunks(nw2), vs))
    early_parts = [(qy, pos_x(m), hcol[0]) for m in range(nqx)] + [(pos_y(m), qx, hcol[1]) for m in range(nqy)]
    for place in early_parts:
        part = piece_of(*place)
        remote(part, part, us, ur, (mate, t))
    upstream(nt - 2)
    gather_third(nt - 1)
    upstream(nt - 1)

    for k in range(ntile):
        lanes = pl.ds(k * tile, tile)
        down = ssq[lanes, :1] * (jnp.sum(cross[lanes, :], axis=1, keepdims=True) / width)
        cross[lanes, :] = jnp.broadcast_to(down, (tile, 128))

    for late, count in ((0, na), (1, nw2 - na)):
        arrived(chunks(count), vr.at[late])
        late_parts = [
            (pos_y(k), pos_x(m), hcol[0]) for k in range(1, nqy) for m in range(nqx) if min(m, 1) == late
        ]
        late_parts += [
            (pos_y(m), pos_x(k), hcol[1]) for k in range(1, nqx) for m in range(nqy) if min(m, 1) == late
        ]
        for place in late_parts:
            part = piece_of(*place)
            remote(part, part, us, ur, (mate, t))
    whole = nwb.at[:, pl.ds(nat, rows)]
    sent.append((whole, us))
    arrived(whole, ur)
    for like, sem in sent:
        left(like, sem)
    crossed_over()
    for side, b, here in line_sent:
        there = t + 1 < nt if side == 0 else t >= 1

        @pl.when(jnp.logical_and(here, there))
        def _(side=side, b=b):
            left(chunks(2 + na), zfs.at[side, b])


def write_out(grad, x, down, nwb, nf, ns, grad_out, nw_out, nf_out, ns_out, done, sem, gsem):
    tokens, width = x.shape
    tile = min(32, tokens)
    small = [
        pltpu.make_async_copy(src, dst, sem.at[n])
        for n, (src, dst) in enumerate(((nwb, nw_out), (nf, nf_out), (ns, ns_out)))
    ]
    for copy in small:
        copy.start()
    copies = list(small)
    for k in range(tokens // tile):
        @pl.loop(0, tile // 16)
        def _(g):
            r = pl.ds(pl.multiple_of(k * tile + g * 16, 16), 16)
            factor = down[r, :]
            for n in range(width // 128):
                col = slice(n * 128, (n + 1) * 128)
                done[r, col] = (grad[r, col].astype(F32) - factor * x[r, col].astype(F32)).astype(BF16)

        piece = pl.ds(k * tile, tile)
        copy = pltpu.make_async_copy(done.at[piece], grad_out.at[piece], gsem.at[k])
        copy.start()
        copies.append(copy)
    for copy in copies:
        copy.wait()


def body(ndp, nt, norm_input, key_grad, positions, norm_gain, key_weight, first_moment, second_moment):
    rows, cols = key_weight.shape
    tokens, width = norm_input.shape
    nq = ndp // 2
    features = ndp * rows
    tile = min(128, tokens)
    ntile = tokens // tile
    hh = HEAD // 2
    frequency = ROPE_BASE ** (-(2.0 * np.arange(hh)) / HEAD)
    frequency = np.resize(frequency.astype(np.float32), (1, 128))
    any_spec = pl.BlockSpec(memory_space=pl.ANY)
    vmem = pl.BlockSpec(memory_space=pltpu.VMEM)
    dma = pltpu.SemaphoreType.DMA
    nqx = math.isqrt(nq)
    while nq % nqx:
        nqx -= 1
    nqy = nq // nqx
    hc = cols // 2
    na = nqx + nqy - 2
    nx1 = (nqx - 1) * nqy
    nw2 = nx1 + (nqy - 1) * nqx
    nn = ndp * nt - 1
    scratch = [
        pltpu.VMEM((tokens, features), BF16),
        pltpu.VMEM((ntile, tile), jnp.int32),
        pltpu.VMEM((width // 128, 128), BF16),
        pltpu.VMEM((1, 128), F32),
        pltpu.VMEM((rows, cols), F32),
        pltpu.VMEM((rows, cols), F32),
        pltpu.VMEM((1, width), F32),
        pltpu.VMEM((tokens, features), BF16),
        pltpu.VMEM((features, tokens), BF16),
        pltpu.VMEM((features, tokens), BF16),
        pltpu.VMEM((tokens, 128), F32),
        pltpu.VMEM((nt, features, cols), BF16),
        pltpu.VMEM((nt, features, cols), BF16),
        pltpu.VMEM((nt, nq * rows, cols), BF16),
        pltpu.VMEM((nt, nx1, rows, hc), BF16),
        pltpu.VMEM((nt, nqy - 1, nqx * rows, hc), BF16),
        pltpu.VMEM((nt, nqy - 1, rows, hc), BF16),
        pltpu.VMEM((nt, nqx - 1, rows, hc), BF16),
        pltpu.VMEM((nt - 1, rows, cols), BF16),
        pltpu.VMEM((nt - 1, rows, cols), BF16),
        pltpu.VMEM((rows, cols), F32),
        pltpu.VMEM((1, 128), F32),
        pltpu.VMEM((nn, 1, 128), F32),
        dma((7,)), dma((ntile,)),
        dma, dma,
        dma((2, nt)), dma((nt, 2)),
        dma, dma((nt,)), dma,
        dma((nt // 2,)), dma,
        dma, dma((nt,)),
        dma, dma((2 * nt + 2,)),
        dma, dma((nt, 2)),
        dma, dma((nt,)),
        dma, dma,
        dma, dma,
        dma, dma,
        dma, dma((2,)),
        dma, dma,
    ]
    results = pl.pallas_call(
        functools.partial(kernel, ndp, nt, nqx),
        out_shape=(
            pltpu.VMEM((tokens, width), BF16),
            pltpu.VMEM((tokens, width), BF16),
            pltpu.VMEM((tokens, 128), F32),
            pltpu.VMEM((nq, 2 * rows, cols), BF16),
            pltpu.VMEM((rows, cols), F32),
            pltpu.VMEM((rows, cols), F32),
        ),
        in_specs=[any_spec] * 8,
        out_specs=(vmem,) * 6,
        scratch_shapes=scratch,
        compiler_params=pltpu.CompilerParams(
            collective_id=0, has_side_effects=True, vmem_limit_bytes=42 * 2**20
        ),
    )(
        norm_input, key_grad, positions.reshape(ntile, tile), norm_gain.reshape(width // 128, 128),
        jnp.asarray(frequency), key_weight, first_moment, second_moment,
    )
    results = [pltpu.with_memory_space_constraint(r, pltpu.VMEM) for r in results]
    input_grad, new_weight, new_first, new_second = pl.pallas_call(
        write_out,
        out_shape=[jax.ShapeDtypeStruct(results[n].shape, results[n].dtype) for n in (0, 3, 4, 5)],
        in_specs=[vmem] * 6,
        out_specs=[any_spec] * 4,
        scratch_shapes=[pltpu.VMEM((tokens, width), BF16), dma((3,)), dma((tokens // min(32, tokens),))],
        compiler_params=pltpu.CompilerParams(vmem_limit_bytes=10 * 2**20),
    )(*results)
    return (input_grad, new_weight.reshape(features, cols), new_first, new_second)


def solution(mesh):
    in_specs = (
        P(("dp", "tensor"), None),
        P(("dp", "tensor"), None),
        P(("dp", "tensor")),
        P(),
        P("dp", "tensor"),
        P("dp", "tensor"),
        P("dp", "tensor"),
    )
    out_specs = (P(("dp", "tensor"), None), P(None, "tensor"), P("dp", "tensor"), P("dp", "tensor"))
    return jax.shard_map(
        functools.partial(body, mesh.shape["dp"], mesh.shape["tensor"]),
        mesh=mesh, in_specs=in_specs, out_specs=out_specs, check_vma=False,
    )
```
